512 devices in a mesh: cls: 32 (over z, x_hi), ptcl: 16 (over y, x_lo, core).
Axes of the slice: x: 4 (x_hi: 2, x_lo: 2; x = x_hi * 2 + x_lo), y: 4, z: 16, core: 2. Of those that a mesh axis runs over, the one named last changes fastest.
Arguments:
- images: bfloat16 [2048, 2048], P('cls', 'ptcl'), may hold values from -64 to 64
- references: bfloat16 [128, 2048], P('cls'), may hold values from -1 to 1
- log_prior: bfloat16 [128], P('cls'), may hold values from -1.5 to 0
- defocus: float32 [32], replicated, may hold values from 1.5 to 6
- groups: int32 [2048], P('cls'), may hold values from 0 to 31, as said below
Outputs:
- new_references: float32 [128, 2048], P('cls', 'ptcl')
- class_share: float32 [128], P('cls')
The draws below stay inside these ranges and needn't reach their ends.
Inputs may be any that keep to these rules, and one draw needn't show every extreme that they name: `groups`: every CTF group holds at least one particle.
All inputs are finite; a program needn't handle non-finite values.
Results may differ from the reference program's by a relative error of at most 0.0065.
Values may be sent and summed in bfloat16 or wider, within the bound.
A program may use at most 64 MiB of HBM per device.

```python
import math
import jax
import jax.numpy as jnp
from jax import lax

SIDE = 32
ROT = 36
CLS_DEV = 4
GROUPS = 32
PTCL_DEV = 64
CLASSES = 128
NTOT = 2048


def pixel_coords_drawn(pixels):
    center = SIDE // 2
    across = (pixels % SIDE - center).astype(jnp.float32)
    down = (pixels // SIDE - center).astype(jnp.float32)
    return (across, down)


def contrast_values_drawn(defocus, pixels):
    across, down = pixel_coords_drawn(pixels)
    radius_sq = (across * across + down * down) / float((SIDE // 2) ** 2)
    phase_shift = math.pi * defocus[:, None] * radius_sq[None, :]
    return -(0.99499 * jnp.sin(phase_shift) + 0.1 * jnp.cos(phase_shift))


def rotate_rows(fields, turns):
    pix_count = SIDE * SIDE
    center = SIDE // 2
    angle_rows = 2.0 * math.pi / ROT * turns.astype(jnp.float32)[:, None]
    across, down = pixel_coords_drawn(jnp.arange(pix_count, dtype=jnp.int32))
    source_across = jnp.cos(angle_rows) * across[None, :] + jnp.sin(angle_rows) * down[None, :]
    source_down = -jnp.sin(angle_rows) * across[None, :] + jnp.cos(angle_rows) * down[None, :]
    floor_across = jnp.floor(source_across)
    floor_down = jnp.floor(source_down)
    fraction_across = source_across - floor_across
    fraction_down = source_down - floor_down
    result = jnp.zeros(fields.shape, jnp.float32)
    for step_across in (0, 1):
        for step_down in (0, 1):
            col_pos = floor_across + step_across
            row_pos = floor_down + step_down
            weight_across = fraction_across if step_across else 1.0 - fraction_across
            weight_down = fraction_down if step_down else 1.0 - fraction_down
            inside = (col_pos >= -center) & (col_pos <= center - 1) & (row_pos >= -center) & (row_pos <= center - 1)
            flat_index = jnp.clip((row_pos + center) * SIDE + col_pos + center, 0, pix_count - 1).astype(jnp.int32)
            picked = jnp.take_along_axis(fields, flat_index[:, :, None], axis=1)
            result = result + jnp.where(inside, weight_across * weight_down, 0.0)[:, :, None] * picked
    return result


def draw_parts(key):
    pix_count = SIDE * SIDE
    keys_list = [jax.random.fold_in(key, 101 + offset) for offset in range(10)]
    base = jax.random.normal(keys_list[0], (CLASSES, pix_count, 2), jnp.float32) * 0.08
    defocus = jnp.exp(jax.random.uniform(keys_list[2], (GROUPS,), jnp.float32, math.log(1.5), math.log(6.0)))
    base = jnp.clip(base, -1.0, 1.0)
    groups = jax.random.randint(keys_list[3], (NTOT,), 0, GROUPS, jnp.int32)
    spots = jax.random.permutation(keys_list[4], NTOT)[:GROUPS]
    groups = groups.at[spots].set(jnp.arange(GROUPS, dtype=jnp.int32))
    positions = jnp.arange(NTOT, dtype=jnp.int32)
    block_index = positions // PTCL_DEV
    offsets = jax.random.randint(keys_list[5], (NTOT,), 0, max(CLASSES // 2, 1), jnp.int32)
    chosen = (block_index * CLS_DEV + offsets) % CLASSES
    turns = jax.random.randint(keys_list[6], (NTOT,), 0, ROT, jnp.int32)
    signal_first = rotate_rows(base[chosen], turns)
    contrast = contrast_values_drawn(defocus, jnp.arange(pix_count, dtype=jnp.int32))[groups]
    amplitude = jax.random.uniform(keys_list[7], (NTOT,), jnp.float32, 0.5, 2.5)
    noise = jax.random.normal(keys_list[8], (NTOT, pix_count, 2), jnp.float32)
    signal = signal_first
    images = jnp.clip(noise + amplitude[:, None, None] * contrast[:, :, None] * signal, -64.0, 64.0)
    return (images.reshape(NTOT, 2 * pix_count), base.reshape(CLASSES, 2 * pix_count), defocus, groups)


def draw_images(key, part):
    return draw_parts(key)[0].astype(jnp.bfloat16)


def draw_references(key, part):
    return draw_parts(key)[1].astype(jnp.bfloat16)


def draw_defocus(key, part):
    return draw_parts(key)[2]


def draw_groups(key, part):
    return draw_parts(key)[3]


def level_of(stream_key, shape, shards, least, top_value):
    factor_of = 1.0
    for axis_at, parts in shards:
        heights = jax.random.uniform(jax.random.fold_in(jax.random.fold_in(stream_key, 6), axis_at), (parts,), jnp.float32, least / len(shards), top_value / len(shards))
        factor_of = factor_of * jnp.repeat(jnp.exp(heights), shape[axis_at] // parts).reshape((-1,) + (1,) * (len(shape) - 1 - axis_at))
    return factor_of


def setup_inputs(seed: int = 0) -> dict:
    keys = jax.random.split(jax.random.key(seed), 6)
    images = draw_images(jax.random.fold_in(keys[5], 71), 0)
    references = draw_references(jax.random.fold_in(keys[5], 71), 0)
    log_prior = jnp.clip(-1.5 + 1.5 * jax.random.uniform(keys[2], (CLASSES,), jnp.float32) ** level_of(keys[2], (CLASSES,), ((0, 32),), -0.2, 0.2), -1.5, 0.0).astype(jnp.bfloat16)
    defocus = draw_defocus(jax.random.fold_in(keys[5], 71), 0)
    groups = draw_groups(jax.random.fold_in(keys[5], 71), 0)
    return dict(images=images, references=references, log_prior=log_prior, defocus=defocus, groups=groups)


def pixel_coords(pixels):
    center = SIDE // 2
    across = (pixels % SIDE - center).astype(jnp.float32)
    down = (pixels // SIDE - center).astype(jnp.float32)
    return across, down


def rotation_weights(out_pixels):
    angles = 2.0 * math.pi * jnp.arange(ROT, dtype=jnp.float32) / ROT
    cosine = jnp.cos(angles)[:, None, None]
    sine_val = jnp.sin(angles)[:, None, None]
    out_across, out_down = pixel_coords(out_pixels)
    in_across, in_down = pixel_coords(jnp.arange(SIDE * SIDE, dtype=jnp.int32))
    source_across = cosine * out_across[None, :, None] + sine_val * out_down[None, :, None]
    source_down = -sine_val * out_across[None, :, None] + cosine * out_down[None, :, None]
    first = jnp.maximum(0.0, 1.0 - jnp.abs(source_across - in_across[None, None, :]))
    second = jnp.maximum(0.0, 1.0 - jnp.abs(source_down - in_down[None, None, :]))
    return first * second


def contrast_values(defocus, pixels):
    across, down = pixel_coords(pixels)
    radius_sq = (across * across + down * down) / float((SIDE // 2) ** 2)
    phase_shift = math.pi * defocus[:, None] * radius_sq[None, :]
    return -(0.99499 * jnp.sin(phase_shift) + 0.1 * jnp.cos(phase_shift))


def reference(images, references, log_prior, defocus, groups):
    highest = lax.Precision.HIGHEST
    pix_count = SIDE * SIDE
    particles = images.shape[0]
    class_count = references.shape[0]
    all_pixels = jnp.arange(pix_count, dtype=jnp.int32)
    table_half = rotation_weights(all_pixels).astype(jnp.bfloat16)
    table_back = lax.optimization_barrier(table_half).astype(jnp.float32)
    contrast = contrast_values(defocus, all_pixels)
    selector = (groups[:, None] == jnp.arange(GROUPS, dtype=jnp.int32)[None, :]).astype(jnp.float32)
    particle_contrast = jnp.dot(selector, contrast, precision=highest)
    weighted = (images.reshape(particles, pix_count, 2).astype(jnp.float32) * particle_contrast[:, :, None]).astype(jnp.bfloat16)
    turned = jnp.einsum("rqp,kpt->krqt", table_back, references.reshape(class_count, pix_count, 2).astype(jnp.float32), precision=highest).astype(jnp.bfloat16)
    flat = turned.reshape(class_count * ROT, 2 * pix_count)
    matched = jnp.dot(weighted.reshape(particles, 2 * pix_count), flat.T, preferred_element_type=jnp.float32)
    turned_wide = turned.astype(jnp.float32)
    power = jnp.sum(turned_wide * turned_wide, axis=3).reshape(class_count * ROT, pix_count)
    group_penalty = jnp.dot(contrast * contrast, power.T, precision=highest)
    penalty = jnp.dot(selector, group_penalty, precision=highest)
    logits = matched - 0.5 * penalty + jnp.repeat(log_prior.astype(jnp.float32), ROT)[None, :]
    peak = jnp.max(logits, axis=1, keepdims=True)
    expo = jnp.exp(logits - peak)
    weights = (expo / jnp.sum(expo, axis=1, keepdims=True)).astype(jnp.bfloat16)
    contrast_sq = (particle_contrast * particle_contrast).astype(jnp.bfloat16)
    stacked = jnp.concatenate([weighted, contrast_sq[:, :, None]], axis=2).reshape(particles, 3 * pix_count)
    accumulated = jnp.dot(weights.T, stacked, preferred_element_type=jnp.float32)
    back = jnp.einsum("rqp,krqc->kpc", table_back, accumulated.reshape(class_count, ROT, pix_count, 3), precision=highest)
    new_references = (back[:, :, :2] / (back[:, :, 2:] + 1.0)).reshape(class_count, 2 * pix_count)
    occupancy = jnp.sum(weights.astype(jnp.float32).reshape(particles, class_count, ROT), axis=(0, 2))
    class_share = occupancy * (class_count / particles)
    return new_references, class_share
```

```python
import functools
import math

import jax
import jax.numpy as jnp
import numpy as np
from jax import lax
from jax.experimental import pallas as pl
from jax.experimental.pallas import tpu as pltpu
from jax.sharding import PartitionSpec as P

SIDE = 32
PIX = SIDE * SIDE
ROT = 36
BASE = ROT // 4
EXT = SIDE + 1
LANES = 1152
CHUNK = 384
CLS = 32
PTCL = 16
NK = 8
ROWS = BASE * NK
NB = 64
MESH = pl.DeviceIdType.MESH
F32 = jnp.float32
BF16 = jnp.bfloat16
VMEM = pltpu.VMEM


def grid_constants():
    table = np.zeros((16, LANES), np.float32)
    e = np.arange(EXT * EXT)
    across = e % EXT - SIDE // 2
    down = e // EXT - SIDE // 2
    table[0, : e.size] = across
    table[1, : e.size] = down
    table[2, : e.size] = (across * across + down * down) / float((SIDE // 2) ** 2)
    table[4:8] = -1.0
    a, d = across.copy(), down.copy()
    for s in range(4):
        inside = (a >= -16) & (a <= 15) & (d >= -16) & (d <= 15)
        table[4 + s, : e.size] = np.where(inside, (d + 16) * SIDE + a + 16, -1)
        table[8 + s, : e.size] = inside
        a, d = -d, a
    return table


def angle_constants():
    angles = (np.float32(2.0 * math.pi) * np.arange(BASE, dtype=np.float32) / np.float32(ROT)).astype(np.float32)
    return np.stack([np.cos(angles), np.sin(angles)]).astype(np.float32)


def split_constants():
    out = np.zeros((128, 128), np.float32)
    for l in range(64):
        out[2 * l, l] = 1
        out[2 * l + 1, 64 + l] = 1
    return out.astype(jnp.bfloat16)


def join_constants():
    out = np.zeros((2, 256, 128), np.float32)
    for h in range(2):
        for l in range(64):
            out[h, 64 * h + l, 2 * l] = 1
            out[h, 128 + 64 * h + l, 2 * l + 1] = 1
    return out


def sine_of(phase):
    return jnp.sin(phase)


def factors(grid_ref, cosine, sine, start):
    qa = grid_ref[0:1, pl.ds(start, CHUNK)]
    qd = grid_ref[1:2, pl.ds(start, CHUNK)]
    place = lax.broadcasted_iota(jnp.int32, (SIDE, CHUNK), 0).astype(F32) - float(SIDE // 2)
    hat_a = jnp.maximum(0.0, 1.0 - jnp.abs(cosine * qa + sine * qd - place))
    hat_d = jnp.maximum(0.0, 1.0 - jnp.abs(cosine * qd - sine * qa - place))
    return hat_a, hat_d


def table_rows(hat_a, hat_d, first):
    return jnp.concatenate(
        [hat_a * hat_d[first + i : first + i + 1, :] for i in range(8)], axis=0
    ).astype(BF16)


def pair_halves(first, second):
    low = lax.broadcasted_iota(jnp.int32, first.shape, 1) < 64
    real = jnp.where(low, first, pltpu.roll(second, 64, 1))
    imag = jnp.where(low, pltpu.roll(first, 64, 1), second)
    return real, imag


def score_kernel(
    angle_ref, grid_ref, split_ref, imgs_ref, refs_ref, focus_ref,
    logit_ref, stat_ref, vals_ref,
    flat, wide, refmat, turned, power_lo,
):
    flat[0 : NK * 32, :] = jnp.dot(
        refs_ref[...].reshape(NK * 32, 128), split_ref[...], preferred_element_type=F32
    )
    for u in range(8):
        real, imag = pair_halves(
            flat[pl.ds(2 * u, NK, stride=32), :], flat[pl.ds(2 * u + 1, NK, stride=32), :]
        )
        refmat[:, 128 * u : 128 * (u + 1)] = jnp.concatenate([real, imag], axis=0).astype(BF16)
    prior = flat[pl.ds(16, NK, stride=32), :]

    def rotate(step, _):
        r = step // (LANES // CHUNK)
        start = pl.multiple_of((step % (LANES // CHUNK)) * CHUNK, CHUNK)
        hat_a, hat_d = factors(grid_ref, angle_ref[0, r], angle_ref[1, r], start)
        acc = jnp.zeros((2 * NK, CHUNK), F32)
        for part in range(4):
            rows = table_rows(hat_a, hat_d, 8 * part)
            acc += jnp.dot(refmat[:, 256 * part : 256 * (part + 1)], rows, preferred_element_type=F32)
        acc = acc.astype(BF16).astype(F32)
        row = pl.multiple_of(r * NK, NK)
        turned[0, pl.ds(row, NK), pl.ds(start, CHUNK)] = acc[:NK]
        turned[1, pl.ds(row, NK), pl.ds(start, CHUNK)] = acc[NK:]
        return 0

    lax.fori_loop(0, BASE * (LANES // CHUNK), rotate, 0)

    for u in range(8):
        two = jnp.dot(
            imgs_ref[2 * u : 2 * u + 2].reshape(128, 128), split_ref[...], preferred_element_type=F32
        )
        real, imag = pair_halves(two[:NB], two[NB:])
        wide[:, 128 * u : 128 * (u + 1)] = jnp.concatenate([real, imag], axis=0).astype(BF16)

    phase = math.pi * focus_ref[...] * grid_ref[2:3, :]
    contrast = -(0.99499 * jnp.sin(phase) + 0.1 * jnp.cos(phase))
    square = contrast * contrast

    def turn(s, _):
        target = grid_ref[pl.ds(4 + s, 1), :]
        mask = grid_ref[pl.ds(8 + s, 1), :]
        acc = jnp.zeros((2 * NB, LANES), F32)
        for part in range(4):
            place = lax.broadcasted_iota(jnp.int32, (256, LANES), 0).astype(F32) + 256.0 * part
            pick = jnp.where(place == target, 1.0, 0.0).astype(BF16)
            acc += jnp.dot(wide[:, 256 * part : 256 * (part + 1)], pick, preferred_element_type=F32)
        row = pl.multiple_of(s * NB, NB)
        vals_ref[0, pl.ds(row, NB), :] = (acc[:NB] * contrast).astype(BF16)
        vals_ref[1, pl.ds(row, NB), :] = (acc[NB:] * contrast).astype(BF16)
        masked = square * mask
        high = masked.astype(BF16)
        vals_ref[2, pl.ds(row, NB), :] = high
        power_lo[pl.ds(row, NB), :] = (masked - high.astype(F32)).astype(BF16)
        return 0

    lax.fori_loop(0, 4, turn, 0)

    def over_pixels(a, b):
        return lax.dot_general(a, b, (((1,), (1,)), ((), ())), preferred_element_type=F32)

    real, imag = turned[0], turned[1]
    match = over_pixels(real.astype(BF16), vals_ref[0]) + over_pixels(imag.astype(BF16), vals_ref[1])
    power = real * real + imag * imag
    power_high = power.astype(BF16)
    power_low = (power - power_high.astype(F32)).astype(BF16)
    penalty = (
        over_pixels(power_high, vals_ref[2])
        + over_pixels(power_low, vals_ref[2])
        + over_pixels(power_high, power_lo[...])
    )
    both = jnp.concatenate([prior, prior], axis=1)
    logits = match - 0.5 * penalty + jnp.concatenate([both] * BASE, axis=0)
    logit_ref[...] = logits
    peak = jnp.max(logits, axis=0, keepdims=True)
    peak = jnp.maximum(peak[:, :128], peak[:, 128:])
    peak = jnp.maximum(peak, pltpu.roll(peak, 64, 1))
    total = jnp.sum(jnp.exp(logits - jnp.concatenate([peak, peak], axis=1)), axis=0, keepdims=True)
    total = total[:, :128] + total[:, 128:]
    total = total + pltpu.roll(total, 64, 1)
    stat_ref[...] = jnp.where(lax.broadcasted_iota(jnp.int32, (8, 128), 0) == 0, peak, total)


def score(imgs, refs, focus):
    vmem = pl.BlockSpec(memory_space=VMEM)
    return pl.pallas_call(
        score_kernel,
        out_shape=(
            jax.ShapeDtypeStruct((ROWS, 4 * NB), F32),
            jax.ShapeDtypeStruct((8, 128), F32),
            jax.ShapeDtypeStruct((3, 4 * NB, LANES), BF16),
        ),
        in_specs=[pl.BlockSpec(memory_space=pltpu.SMEM)] + [vmem] * 5,
        out_specs=(vmem, vmem, vmem),
        scratch_shapes=[
            VMEM((NK * 32, 128), F32),
            VMEM((2 * NB, PIX), BF16),
            VMEM((2 * NK, PIX), BF16),
            VMEM((2, ROWS, LANES), F32),
            VMEM((4 * NB, LANES), BF16),
        ],
        compiler_params=pltpu.CompilerParams(vmem_limit_bytes=48 << 20),
        name="score",
    )(jnp.asarray(angle_constants()), jnp.asarray(grid_constants()), jnp.asarray(split_constants()), imgs, refs, focus)


def sums_kernel(angle_ref, grid_ref, logit_ref, stats_ref, vals_ref, out_ref, spread, acc):
    peaks = stats_ref[:, 0:1, :]
    peak = jnp.max(peaks, axis=0)
    total = jnp.sum(stats_ref[:, 1:2, :] * jnp.exp(peaks - peak[None]), axis=0)
    peak2 = jnp.concatenate([peak, peak], axis=1)
    total2 = jnp.concatenate([total, total], axis=1)
    weights = (jnp.exp(logit_ref[...] - peak2) / total2).astype(BF16)
    counts = jnp.sum(weights.astype(F32), axis=1, keepdims=True)
    share = counts[0:NK]
    for r in range(1, BASE):
        share = share + counts[r * NK : (r + 1) * NK]
    for c in range(3):
        spread[c] = jnp.dot(weights, vals_ref[c], preferred_element_type=F32)
    acc[...] = jnp.zeros_like(acc)

    def project(step, _):
        r = step // (LANES // CHUNK)
        start = pl.multiple_of((step % (LANES // CHUNK)) * CHUNK, CHUNK)
        hat_a, hat_d = factors(grid_ref, angle_ref[0, r], angle_ref[1, r], start)
        row = pl.multiple_of(r * NK, NK)
        parts = jnp.concatenate([spread[c, pl.ds(row, NK), pl.ds(start, CHUNK)] for c in range(3)], axis=0)
        high = parts.astype(BF16)
        low = (parts - high.astype(F32)).astype(BF16)
        both = jnp.concatenate([high.astype(F32), low.astype(F32)], axis=0).astype(BF16)
        for part in range(4):
            rows = table_rows(hat_a, hat_d, 8 * part)
            acc[:, 256 * part : 256 * (part + 1)] += lax.dot_general(
                both, rows, (((1,), (1,)), ((), ())), preferred_element_type=F32
            )
        return 0

    lax.fori_loop(0, BASE * (LANES // CHUNK), project, 0)
    back = acc[0:24, :] + acc[24:48, :]
    for k in range(NK):
        for c in range(3):
            for u in range(8):
                out_ref[k, 8 * c + u : 8 * c + u + 1, :] = back[
                    NK * c + k : NK * c + k + 1, 128 * u : 128 * (u + 1)
                ]
        out_ref[k, 24:32, :] = jnp.broadcast_to(share[k : k + 1, :], (8, 128))


def sums(logits, stats, vals):
    vmem = pl.BlockSpec(memory_space=VMEM)
    return pl.pallas_call(
        sums_kernel,
        out_shape=jax.ShapeDtypeStruct((NK, 32, 128), F32),
        in_specs=[pl.BlockSpec(memory_space=pltpu.SMEM)] + [vmem] * 4,
        out_specs=vmem,
        scratch_shapes=[VMEM((3, ROWS, LANES), F32), VMEM((48, PIX), F32)],
        compiler_params=pltpu.CompilerParams(vmem_limit_bytes=48 << 20),
        name="sums",
    )(jnp.asarray(angle_constants()), jnp.asarray(grid_constants()), logits, stats, vals)


def gather_kernel(img_ref, msg_ref, imgs_ref, refs_ref, send, recv, rsend, rrecv):
    c = lax.axis_index("cls")
    j = lax.axis_index("ptcl")
    home = j // 4
    sender = lax.rem(c, 4) == home
    barrier = pltpu.get_barrier_semaphore()

    def greet_row(d, _):
        pl.semaphore_signal(barrier, inc=1, device_id={"ptcl": lax.rem(j + d, PTCL)}, device_id_type=MESH)
        return 0

    lax.fori_loop(1, PTCL, greet_row, 0)

    def greet_column(g, _):
        @pl.when(4 * g + home != c)
        def _():
            pl.semaphore_signal(barrier, inc=1, device_id={"cls": 4 * g + home}, device_id_type=MESH)

        return 0

    lax.fori_loop(0, NK, greet_column, 0)
    @pl.when(sender)
    def _():
        pl.semaphore_wait(barrier, PTCL - 1 + CLS - 1)

    @pl.when(jnp.logical_not(sender))
    def _():
        pl.semaphore_wait(barrier, PTCL - 1)

    def image(d):
        return pltpu.make_async_remote_copy(
            src_ref=img_ref, dst_ref=imgs_ref.at[j], send_sem=send.at[d], recv_sem=recv.at[d],
            device_id={"ptcl": lax.rem(j + d, PTCL)}, device_id_type=MESH,
        )

    def ref_row(d):
        return pltpu.make_async_remote_copy(
            src_ref=msg_ref.at[lax.rem(j, 4)], dst_ref=refs_ref.at[c // 4], send_sem=rsend.at[d],
            recv_sem=rrecv.at[c // 4], device_id={"cls": lax.rem(c + d, CLS)}, device_id_type=MESH,
        )

    def ref_arrival(g):
        return pltpu.make_async_remote_copy(
            src_ref=msg_ref.at[0], dst_ref=refs_ref.at[g], send_sem=rsend.at[0],
            recv_sem=rrecv.at[g], device_id={"cls": lax.rem(c + 1, CLS)}, device_id_type=MESH,
        )

    @pl.when(sender)
    def _():
        def start_ref(d, _):
            ref_row(d).start()
            return 0

        lax.fori_loop(1, CLS, start_ref, 0)

    def start_image(d, _):
        image(d).start()
        return 0

    lax.fori_loop(1, PTCL, start_image, 0)
    imgs_ref[j] = img_ref[...]

    @pl.when(sender)
    def _():
        refs_ref[c // 4] = msg_ref[lax.rem(j, 4)]

    def arrive_image(d, _):
        pltpu.make_async_remote_copy(
            src_ref=img_ref, dst_ref=imgs_ref.at[lax.rem(j + PTCL - d, PTCL)], send_sem=send.at[d],
            recv_sem=recv.at[d], device_id={"ptcl": lax.rem(j + d, PTCL)}, device_id_type=MESH,
        ).wait_recv()
        return 0

    lax.fori_loop(1, PTCL, arrive_image, 0)

    def arrive_ref(g, _):
        @pl.when(4 * g + home != c)
        def _():
            ref_arrival(g).wait_recv()

        return 0

    lax.fori_loop(0, NK, arrive_ref, 0)

    def leave_image(d, _):
        image(d).wait_send()
        return 0

    lax.fori_loop(1, PTCL, leave_image, 0)

    @pl.when(sender)
    def _():
        def leave_ref(d, _):
            ref_row(d).wait_send()
            return 0

        lax.fori_loop(1, CLS, leave_ref, 0)


def gather(image, message):
    vmem = pl.BlockSpec(memory_space=VMEM)
    return pl.pallas_call(
        gather_kernel,
        out_shape=(
            jax.ShapeDtypeStruct((PTCL, NB, 128), BF16),
            jax.ShapeDtypeStruct((NK, 32, 128), BF16),
        ),
        in_specs=[vmem, vmem],
        out_specs=(vmem, vmem),
        scratch_shapes=[
            pltpu.SemaphoreType.DMA((PTCL,)),
            pltpu.SemaphoreType.DMA((PTCL,)),
            pltpu.SemaphoreType.DMA((CLS,)),
            pltpu.SemaphoreType.DMA((NK,)),
        ],
        compiler_params=pltpu.CompilerParams(collective_id=0, has_side_effects=True),
        name="gather",
    )(image, message)


def stats_kernel(stat_ref, stats_ref, send, recv):
    j = lax.axis_index("ptcl")
    barrier = pltpu.get_barrier_semaphore()

    def greet(d, _):
        pl.semaphore_signal(barrier, inc=1, device_id={"ptcl": lax.rem(j + d, PTCL)}, device_id_type=MESH)
        return 0

    lax.fori_loop(1, PTCL, greet, 0)
    pl.semaphore_wait(barrier, PTCL - 1)

    def copy(d, slot):
        return pltpu.make_async_remote_copy(
            src_ref=stat_ref, dst_ref=stats_ref.at[slot], send_sem=send.at[d], recv_sem=recv.at[d],
            device_id={"ptcl": lax.rem(j + d, PTCL)}, device_id_type=MESH,
        )

    def start(d, _):
        copy(d, j).start()
        return 0

    lax.fori_loop(1, PTCL, start, 0)
    stats_ref[j] = stat_ref[...]

    def finish(d, _):
        copy(d, lax.rem(j + PTCL - d, PTCL)).wait_recv()
        copy(d, j).wait_send()
        return 0

    lax.fori_loop(1, PTCL, finish, 0)


def exchange(stat):
    vmem = pl.BlockSpec(memory_space=VMEM)
    return pl.pallas_call(
        stats_kernel,
        out_shape=jax.ShapeDtypeStruct((PTCL, 8, 128), F32),
        in_specs=[vmem],
        out_specs=vmem,
        scratch_shapes=[pltpu.SemaphoreType.DMA((PTCL,)), pltpu.SemaphoreType.DMA((PTCL,))],
        compiler_params=pltpu.CompilerParams(collective_id=1, has_side_effects=True),
        name="exchange",
    )(stat)


def finish_kernel(join_ref, part_ref, new_ref, share_ref, heap, outbox, inbox, s1, r1, s2, r2):
    c = lax.axis_index("cls")
    j = lax.axis_index("ptcl")
    home = j // 4
    mine = c // 4
    owner = lax.rem(c, 4) == home
    first = 4 * lax.rem(c, 4)
    barrier = pltpu.get_barrier_semaphore()

    @pl.when(owner)
    def _():
        def greet(d, _):
            pl.semaphore_signal(barrier, inc=1, device_id={"cls": lax.rem(c + d, CLS)}, device_id_type=MESH)
            return 0

        lax.fori_loop(1, CLS, greet, 0)

    def greet_owner(i, _):
        @pl.when(first + i != j)
        def _():
            pl.semaphore_signal(barrier, inc=1, device_id={"ptcl": first + i}, device_id_type=MESH)

        return 0

    lax.fori_loop(0, 4, greet_owner, 0)

    @pl.when(owner)
    def _():
        pl.semaphore_wait(barrier, NK - 1 + PTCL - 1)

    @pl.when(jnp.logical_not(owner))
    def _():
        pl.semaphore_wait(barrier, NK)

    def to_owner(g):
        return pltpu.make_async_remote_copy(
            src_ref=part_ref.at[g], dst_ref=heap.at[c], send_sem=s1.at[g], recv_sem=r1.at[c],
            device_id={"cls": 4 * g + home}, device_id_type=MESH,
        )

    def start_sum(g, _):
        @pl.when(4 * g + home != c)
        def _():
            to_owner(g).start()

        return 0

    lax.fori_loop(0, NK, start_sum, 0)

    def to_row(d):
        target = lax.rem(j + d, PTCL)
        return pltpu.make_async_remote_copy(
            src_ref=outbox.at[target], dst_ref=inbox.at[lax.rem(j, 4)], send_sem=s2.at[d],
            recv_sem=r2.at[lax.rem(j, 4)], device_id={"ptcl": target}, device_id_type=MESH,
        )

    @pl.when(owner)
    def _():
        heap[c] = part_ref[mine]

        def arrive(d, _):
            source = lax.rem(c + d, CLS)
            pltpu.make_async_remote_copy(
                src_ref=part_ref.at[0], dst_ref=heap.at[source], send_sem=s1.at[0], recv_sem=r1.at[source],
                device_id={"cls": source}, device_id_type=MESH,
            ).wait_recv()
            return 0

        lax.fori_loop(1, CLS, arrive, 0)
        total = lax.fori_loop(1, CLS, lambda i, t: t + heap[i], heap[0])
        scale = 1.0 / (total[16:24] + 1.0)
        planes = jnp.concatenate([total[0:8] * scale, total[8:16] * scale], axis=1)
        row = lax.broadcasted_iota(jnp.int32, (8, 128), 0)
        for h in range(2):
            joined = jnp.dot(planes, join_ref[h], precision=lax.Precision.HIGHEST, preferred_element_type=F32)
            for u in range(8):
                outbox[2 * u + h] = jnp.where(row == 0, joined[u : u + 1, :], total[24:25, :])

        def start_row(d, _):
            to_row(d).start()
            return 0

        lax.fori_loop(1, PTCL, start_row, 0)
        inbox[lax.rem(j, 4)] = outbox[j]

    def arrive_row(i, _):
        @pl.when(first + i != j)
        def _():
            pltpu.make_async_remote_copy(
                src_ref=outbox.at[0], dst_ref=inbox.at[i], send_sem=s2.at[0], recv_sem=r2.at[i],
                device_id={"ptcl": lax.rem(j + 1, PTCL)}, device_id_type=MESH,
            ).wait_recv()

        return 0

    lax.fori_loop(0, 4, arrive_row, 0)
    new_ref[...] = jnp.concatenate([inbox[i, 0:1, :] for i in range(4)], axis=0)
    share_ref[...] = jnp.concatenate([inbox[i, 1:2, :] for i in range(4)], axis=0)

    def leave_sum(g, _):
        @pl.when(4 * g + home != c)
        def _():
            to_owner(g).wait_send()

        return 0

    lax.fori_loop(0, NK, leave_sum, 0)

    @pl.when(owner)
    def _():
        def leave_row(d, _):
            to_row(d).wait_send()
            return 0

        lax.fori_loop(1, PTCL, leave_row, 0)


def finish(parts):
    vmem = pl.BlockSpec(memory_space=VMEM)
    return pl.pallas_call(
        finish_kernel,
        out_shape=(jax.ShapeDtypeStruct((4, 128), F32), jax.ShapeDtypeStruct((4, 128), F32)),
        in_specs=[vmem, vmem],
        out_specs=(vmem, vmem),
        scratch_shapes=[
            VMEM((CLS, 32, 128), F32),
            VMEM((PTCL, 8, 128), F32),
            VMEM((4, 8, 128), F32),
            pltpu.SemaphoreType.DMA((NK,)),
            pltpu.SemaphoreType.DMA((CLS,)),
            pltpu.SemaphoreType.DMA((PTCL,)),
            pltpu.SemaphoreType.DMA((4,)),
        ],
        compiler_params=pltpu.CompilerParams(collective_id=2, has_side_effects=True),
        name="finish",
    )(jnp.asarray(join_constants()), parts)


def on_device(images, references, log_prior, defocus, groups):
    prior = jnp.broadcast_to(log_prior[:, None, None], (4, 16, 128))
    message = jnp.concatenate([references.reshape(4, 16, 128), prior], axis=1)
    imgs, refs = gather(images, message)
    pick = groups[:, None] == jnp.arange(defocus.shape[0], dtype=jnp.int32)[None, :]
    focus = jnp.sum(jnp.where(pick, defocus[None, :], 0.0), axis=1, keepdims=True)
    logits, stat, vals = score(imgs, refs, focus)
    parts = sums(logits, exchange(stat), vals)
    new, share = finish(parts)
    return new, share[:, 0] * (128.0 / 2048.0)


def solution(mesh):
    return jax.shard_map(
        on_device,
        mesh=mesh,
        in_specs=(P("cls", "ptcl"), P("cls", None), P("cls"), P(), P("cls")),
        out_specs=(P("cls", "ptcl"), P("cls")),
        check_vma=False,
    )
```

```python
import functools
import math

import jax
import jax.numpy as jnp
import numpy as np
from jax import lax
from jax.experimental import pallas as pl
from jax.experimental.pallas import tpu as pltpu
from jax.sharding import PartitionSpec as P

SIDE = 32
PIX = SIDE * SIDE
ROT = 36
BASE = ROT // 4
EXT = SIDE + 1
LANES = 1152
CHUNK = 384
CLS = 32
PTCL = 16
NK = 8
ROWS = BASE * NK
NB = 64
MESH = pl.DeviceIdType.MESH
F32 = jnp.float32
BF16 = jnp.bfloat16
VMEM = pltpu.VMEM

ANGLES = (np.float32(2.0 * math.pi) * np.arange(BASE, dtype=np.float32) / np.float32(ROT)).astype(np.float32)
COSINES = [float(x) for x in np.cos(ANGLES).astype(np.float32)]
SINES = [float(x) for x in np.sin(ANGLES).astype(np.float32)]


def choose(values, r):
    out = jnp.float32(values[0])
    for i, value in enumerate(values[1:], 1):
        out = jnp.where(r == i, jnp.float32(value), out)
    return out


def iota(shape, axis):
    return lax.broadcasted_iota(jnp.int32, shape, axis)


def grid_rows(grid):
    e = iota((1, LANES), 1).astype(F32)
    down = jnp.floor((e + 0.5) * (1.0 / EXT))
    across = e - EXT * down - SIDE // 2
    down = down - SIDE // 2
    grid[0:1, :] = across
    grid[1:2, :] = down
    grid[2:3, :] = (across * across + down * down) * (1.0 / (SIDE // 2) ** 2)
    a, d = across, down
    for s in range(4):
        inside = (a >= -16.0) & (a <= 15.0) & (d >= -16.0) & (d <= 15.0)
        grid[4 + s : 5 + s, :] = jnp.where(inside, (d + 16.0) * SIDE + a + 16.0, -1.0)
        a, d = -d, a


def split_matrix():
    source, place = iota((128, 128), 0), iota((128, 128), 1)
    return jnp.where(source == 2 * (place % 64) + place // 64, 1.0, 0.0).astype(BF16)


def join_matrix():
    source, place = iota((256, 256), 0), iota((256, 256), 1)
    inner = place % 128
    return jnp.where(source == 128 * (inner % 2) + 64 * (place // 128) + inner // 2, 1.0, 0.0).astype(BF16)


def pair_halves(first, second):
    low = iota(first.shape, 1) < 64
    real = jnp.where(low, first, pltpu.roll(second, 64, 1))
    imag = jnp.where(low, pltpu.roll(first, 64, 1), second)
    return real, imag


def column_of(row, size):
    return jnp.sum(jnp.where(iota((size, size), 0) == iota((size, size), 1), row, 0.0), axis=1, keepdims=True)


def over_lanes(a, b):
    return lax.dot_general(a, b, (((1,), (1,)), ((), ())), preferred_element_type=F32)


def make_tables(grid, tables):
    def step(i, _):
        r = i // (LANES // CHUNK)
        start = pl.multiple_of((i % (LANES // CHUNK)) * CHUNK, CHUNK)
        cosine, sine = choose(COSINES, r), choose(SINES, r)
        qa = grid[0:1, pl.ds(start, CHUNK)]
        qd = grid[1:2, pl.ds(start, CHUNK)]
        place = iota((SIDE, CHUNK), 0).astype(F32) - float(SIDE // 2)
        hat_a = jnp.maximum(0.0, 1.0 - jnp.abs(cosine * qa + sine * qd - place))
        hat_d = jnp.maximum(0.0, 1.0 - jnp.abs(cosine * qd - sine * qa - place))
        row = pl.multiple_of(r * PIX, PIX)
        for p in range(SIDE):
            tables[pl.ds(row + p * SIDE, SIDE), pl.ds(start, CHUNK)] = (hat_a * hat_d[p : p + 1, :]).astype(BF16)
        return 0

    lax.fori_loop(0, BASE * (LANES // CHUNK), step, 0)


def make_picks(grid, picks):
    def step(i, _):
        target = grid[pl.ds(4 + i // 4, 1), :]
        place = (iota((256, LANES), 0) + 256 * (i % 4)).astype(F32)
        picks[pl.ds(pl.multiple_of(i * 256, 256), 256), :] = jnp.where(place == target, 1.0, 0.0).astype(BF16)
        return 0

    lax.fori_loop(0, 16, step, 0)


def em_kernel(
    img_ref, ref_ref, prior_ref, focus_ref, group_ref,
    new_ref, share_ref,
    grid, tables, picks, contrast, mrow, message, imgs, refs, flat, wide, refmat, turned, vals, square_lo,
    stat, stats, spread, acc, prow, parts, heap, outbox, inbox,
    img_send, img_recv, ref_send, ref_recv, stat_send, stat_recv, sum_send, sum_recv, out_send, out_recv,
):
    c = lax.axis_index("cls")
    j = lax.axis_index("ptcl")
    home = j // 4
    mine = c // 4
    lane = lax.rem(j, 4)
    owner = lax.rem(c, 4) == home
    first = 4 * lax.rem(c, 4)

    def loop(low, high, body):
        def step(i, _):
            body(i)
            return 0

        lax.fori_loop(low, high, step, 0)

    def owners(body):
        @functools.partial(loop, 0, NK)
        def _(g):
            @pl.when(4 * g + home != c)
            def _():
                body(g)

    def row_peer(d):
        return {"ptcl": lax.rem(j + d, PTCL)}

    def column_peer(d):
        return {"cls": lax.rem(c + d, CLS)}

    def remote(src, dst, send, recv, device):
        return pltpu.make_async_remote_copy(
            src_ref=src, dst_ref=dst, send_sem=send, recv_sem=recv, device_id=device, device_id_type=MESH
        )

    barrier = pltpu.get_barrier_semaphore()

    @pl.when(owner)
    def _():
        loop(1, CLS, lambda d: pl.semaphore_signal(barrier, inc=1, device_id=column_peer(d), device_id_type=MESH))

    @pl.when(jnp.logical_not(owner))
    def _():
        loop(0, NK, lambda g: pl.semaphore_signal(
            barrier, inc=1, device_id={"cls": 4 * g + home}, device_id_type=MESH))

    loop(1, PTCL, lambda d: pl.semaphore_signal(barrier, inc=1, device_id=row_peer(d), device_id_type=MESH))

    split = split_matrix()
    chosen = jnp.sum(
        jnp.where(iota((4, 2 * PIX), 0) == lane, ref_ref[...].astype(F32), 0.0), axis=0, keepdims=True
    )
    for m in range(16):
        mrow[m : m + 1, :] = chosen[:, 128 * m : 128 * (m + 1)]
    own_prior = jnp.sum(jnp.where(iota((1, 4), 1) == lane, prior_ref[...].astype(F32), 0.0), axis=1, keepdims=True)
    mrow[16:32, :] = jnp.broadcast_to(own_prior, (16, 128))
    message[...] = mrow[...].astype(BF16)
    grid_rows(grid)
    group = column_of(group_ref[...].astype(F32), NB)
    groups_count = focus_ref.shape[1]
    focus = jnp.sum(
        jnp.where(group == iota((NB, groups_count), 1).astype(F32), focus_ref[...], 0.0), axis=1, keepdims=True
    )
    phase = math.pi * focus * grid[2:3, :]
    contrast[...] = -(0.99499 * jnp.sin(phase) + 0.1 * jnp.cos(phase))
    make_tables(grid, tables)
    make_picks(grid, picks)

    @pl.when(owner)
    def _():
        pl.semaphore_wait(barrier, PTCL - 1 + CLS - 1)

    @pl.when(jnp.logical_not(owner))
    def _():
        pl.semaphore_wait(barrier, PTCL - 1 + NK)

    def ref_copy(d):
        return remote(message, refs.at[mine], ref_send.at[d], ref_recv.at[mine], column_peer(d))

    def image_copy(d, slot):
        return remote(img_ref, imgs.at[slot], img_send.at[d], img_recv.at[d], row_peer(d))

    @pl.when(owner)
    def _():
        loop(1, CLS, lambda d: ref_copy(d).start())
        refs[mine] = message[...]

    loop(1, PTCL, lambda d: image_copy(d, j).start())
    imgs[j] = img_ref[...]
    loop(1, PTCL, lambda d: image_copy(d, lax.rem(j + PTCL - d, PTCL)).wait_recv())

    for u in range(8):
        two = jnp.dot(imgs[2 * u : 2 * u + 2].reshape(128, 128), split, preferred_element_type=F32)
        real, imag = pair_halves(two[:NB], two[NB:])
        wide[:, 128 * u : 128 * (u + 1)] = jnp.concatenate([real, imag], axis=0).astype(BF16)

    @functools.partial(loop, 0, 4)
    def _(s):
        value = jnp.dot(
            wide[...], picks[pl.ds(pl.multiple_of(s * PIX, PIX), PIX), :], preferred_element_type=F32
        )
        here = contrast[...]
        row = pl.multiple_of(s * NB, NB)
        vals[0, pl.ds(row, NB), :] = (value[:NB] * here).astype(BF16)
        vals[1, pl.ds(row, NB), :] = (value[NB:] * here).astype(BF16)
        square = jnp.where(grid[pl.ds(4 + s, 1), :] >= 0.0, here * here, 0.0)
        high = square.astype(BF16)
        vals[2, pl.ds(row, NB), :] = high
        square_lo[pl.ds(row, NB), :] = (square - high.astype(F32)).astype(BF16)

    owners(lambda g: remote(message, refs.at[g], ref_send.at[0], ref_recv.at[g], column_peer(1)).wait_recv())

    flat[...] = jnp.dot(refs[...].reshape(NK * 32, 128), split, preferred_element_type=F32)
    for u in range(8):
        real, imag = pair_halves(
            flat[pl.ds(2 * u, NK, stride=32), :], flat[pl.ds(2 * u + 1, NK, stride=32), :]
        )
        refmat[:, 128 * u : 128 * (u + 1)] = jnp.concatenate([real, imag], axis=0).astype(BF16)
    prior = flat[pl.ds(16, NK, stride=32), :]

    @functools.partial(loop, 0, BASE)
    def _(r):
        both = jnp.dot(
            refmat[...], tables[pl.ds(pl.multiple_of(r * PIX, PIX), PIX), :], preferred_element_type=F32
        )
        both = both.astype(BF16).astype(F32)
        row = pl.multiple_of(r * NK, NK)
        turned[0, pl.ds(row, NK), :] = both[:NK]
        turned[1, pl.ds(row, NK), :] = both[NK:]

    real, imag = turned[0], turned[1]
    match = over_lanes(real.astype(BF16), vals[0]) + over_lanes(imag.astype(BF16), vals[1])
    power = real * real + imag * imag
    power_hi = power.astype(BF16)
    power_lo = (power - power_hi.astype(F32)).astype(BF16)
    penalty = (
        over_lanes(power_hi, vals[2]) + over_lanes(power_lo, vals[2]) + over_lanes(power_hi, square_lo[...])
    )
    prior = jnp.concatenate([prior, prior], axis=1)
    logits = match - 0.5 * penalty + jnp.concatenate([prior] * BASE, axis=0)
    peak = jnp.max(logits, axis=0, keepdims=True)
    peak = jnp.maximum(peak[:, :128], peak[:, 128:])
    peak = jnp.maximum(peak, pltpu.roll(peak, 64, 1))
    total = jnp.sum(jnp.exp(logits - jnp.concatenate([peak, peak], axis=1)), axis=0, keepdims=True)
    total = total[:, :128] + total[:, 128:]
    total = total + pltpu.roll(total, 64, 1)
    stat[...] = jnp.where(iota((8, 128), 0) == 0, peak, total)

    def stat_copy(d, slot):
        return remote(stat, stats.at[slot], stat_send.at[d], stat_recv.at[d], row_peer(d))

    loop(1, PTCL, lambda d: stat_copy(d, j).start())
    stats[j] = stat[...]
    loop(1, PTCL, lambda d: stat_copy(d, lax.rem(j + PTCL - d, PTCL)).wait_recv())
    peaks = stats[:, 0:1, :]
    peak = jnp.max(peaks, axis=0)
    total = jnp.sum(stats[:, 1:2, :] * jnp.exp(peaks - peak[None]), axis=0)
    weights = (
        jnp.exp(logits - jnp.concatenate([peak, peak], axis=1)) / jnp.concatenate([total, total], axis=1)
    ).astype(BF16)
    counts = jnp.sum(weights.astype(F32), axis=1, keepdims=True)
    share = counts[0:NK]
    for r in range(1, BASE):
        share = share + counts[r * NK : (r + 1) * NK]

    for part in range(3):
        spread[part] = jnp.dot(weights, vals[part], preferred_element_type=F32)
    acc[...] = jnp.zeros_like(acc)

    @functools.partial(loop, 0, BASE)
    def _(r):
        row = pl.multiple_of(r * NK, NK)
        value = jnp.concatenate([spread[part, pl.ds(row, NK), :] for part in range(3)], axis=0)
        high = value.astype(BF16).astype(F32)
        both = jnp.concatenate([high, value - high], axis=0).astype(BF16)
        acc[...] += over_lanes(both, tables[pl.ds(pl.multiple_of(r * PIX, PIX), PIX), :])

    back = acc[0:24, :] + acc[24:48, :]
    for k in range(NK):
        for part in range(3):
            for u in range(8):
                prow[8 * part + u : 8 * part + u + 1, :] = back[
                    NK * part + k : NK * part + k + 1, 128 * u : 128 * (u + 1)
                ]
        prow[24:32, :] = jnp.broadcast_to(share[k : k + 1, :], (8, 128))
        parts[k] = prow[...].astype(BF16)

    def sum_copy(g):
        return remote(parts.at[g], heap.at[c], sum_send.at[g], sum_recv.at[c], {"cls": 4 * g + home})

    def out_copy(d):
        target = lax.rem(j + d, PTCL)
        return remote(outbox.at[target], inbox.at[lane], out_send.at[d], out_recv.at[lane], row_peer(d))

    owners(lambda g: sum_copy(g).start())

    @pl.when(owner)
    def _():
        heap[c] = parts[mine]

        def arrive(d):
            source = lax.rem(c + d, CLS)
            remote(parts.at[0], heap.at[source], sum_send.at[0], sum_recv.at[source], {"cls": source}).wait_recv()

        loop(1, CLS, arrive)
        sums = lax.fori_loop(1, CLS, lambda i, t: t + heap[i].astype(F32), heap[0].astype(F32))
        below = sums[16:24] + 1.0
        planes = jnp.concatenate([sums[0:8] / below, sums[8:16] / below], axis=1)
        high = planes.astype(BF16).astype(F32)
        both = jnp.concatenate([high, planes - high], axis=0).astype(BF16)
        joined = jnp.dot(both, join_matrix(), preferred_element_type=F32)
        joined = joined[0:8] + joined[8:16]
        for b in range(PTCL):
            u, h = b // 2, b % 2
            outbox[b] = jnp.where(
                iota((8, 128), 0) == 0, joined[u : u + 1, 128 * h : 128 * (h + 1)], sums[24:25, :]
            )
        loop(1, PTCL, lambda d: out_copy(d).start())
        inbox[lane] = outbox[j]

    @functools.partial(loop, 0, 4)
    def _(i):
        @pl.when(first + i != j)
        def _():
            remote(outbox.at[0], inbox.at[i], out_send.at[0], out_recv.at[i], row_peer(1)).wait_recv()

    new_ref[...] = jnp.concatenate([inbox[i, 0:1, :] for i in range(4)], axis=0)
    share_row = inbox[0, 1:2, :]
    for i in range(1, 4):
        share_row = jnp.where(iota((1, 128), 1) == i, inbox[i, 1:2, :], share_row)
    share_ref[...] = share_row * (128.0 / 2048.0)

    loop(1, PTCL, lambda d: image_copy(d, j).wait_send())
    loop(1, PTCL, lambda d: stat_copy(d, j).wait_send())
    owners(lambda g: sum_copy(g).wait_send())

    @pl.when(owner)
    def _():
        loop(1, CLS, lambda d: ref_copy(d).wait_send())
        loop(1, PTCL, lambda d: out_copy(d).wait_send())


def on_device(images, references, log_prior, defocus, groups):
    vmem = pl.BlockSpec(memory_space=VMEM)
    dma = pltpu.SemaphoreType.DMA
    new, share = pl.pallas_call(
        em_kernel,
        out_shape=(jax.ShapeDtypeStruct((4, 128), F32), jax.ShapeDtypeStruct((1, 128), F32)),
        in_specs=[vmem] * 5,
        out_specs=(vmem, vmem),
        scratch_shapes=[
            VMEM((8, LANES), F32),
            VMEM((BASE * PIX, LANES), BF16),
            VMEM((4 * PIX, LANES), BF16),
            VMEM((NB, LANES), F32),
            VMEM((32, 128), F32),
            VMEM((32, 128), BF16),
            VMEM((PTCL, NB, 128), BF16),
            VMEM((NK, 32, 128), BF16),
            VMEM((NK * 32, 128), F32),
            VMEM((2 * NB, PIX), BF16),
            VMEM((2 * NK, PIX), BF16),
            VMEM((2, ROWS, LANES), F32),
            VMEM((3, 4 * NB, LANES), BF16),
            VMEM((4 * NB, LANES), BF16),
            VMEM((8, 128), F32),
            VMEM((PTCL, 8, 128), F32),
            VMEM((3, ROWS, LANES), F32),
            VMEM((48, PIX), F32),
            VMEM((32, 128), F32),
            VMEM((NK, 32, 128), BF16),
            VMEM((CLS, 32, 128), BF16),
            VMEM((PTCL, 8, 128), F32),
            VMEM((4, 8, 128), F32),
            dma((PTCL,)),
            dma((PTCL,)),
            dma((CLS,)),
            dma((NK,)),
            dma((PTCL,)),
            dma((PTCL,)),
            dma((NK,)),
            dma((CLS,)),
            dma((PTCL,)),
            dma((4,)),
        ],
        compiler_params=pltpu.CompilerParams(
            collective_id=0, has_side_effects=True, vmem_limit_bytes=60 << 20
        ),
        name="em",
    )(images, references, log_prior[None, :], defocus[None, :], groups[None, :])
    return new, share[0, :4]


def solution(mesh):
    return jax.shard_map(
        on_device,
        mesh=mesh,
        in_specs=(P("cls", "ptcl"), P("cls", None), P("cls"), P(), P("cls")),
        out_specs=(P("cls", "ptcl"), P("cls")),
        check_vma=False,
    )
```

```python
import functools
import math

import jax
import jax.numpy as jnp
import numpy as np
from jax import lax
from jax.experimental import pallas as pl
from jax.experimental.pallas import tpu as pltpu
from jax.sharding import PartitionSpec as P

SIDE = 32
PIX = SIDE * SIDE
ROT = 36
BASE = ROT // 4
EXT = SIDE + 1
PATCH = 11
PATCHES = 9
LANES = 128 * PATCHES
CLS = 32
PTCL = 16
NK = 8
ROWS = BASE * NK
NB = 64
MESH = pl.DeviceIdType.MESH
F32 = jnp.float32
BF16 = jnp.bfloat16
VMEM = pltpu.VMEM

ANGLES = (np.float32(2.0 * math.pi) * np.arange(BASE, dtype=np.float32) / np.float32(ROT)).astype(np.float32)
COSINES = [float(x) for x in np.cos(ANGLES).astype(np.float32)]
SINES = [float(x) for x in np.sin(ANGLES).astype(np.float32)]


def bands():
    out, offset = [], 0
    for r in range(BASE):
        for patch in range(PATCHES):
            down = np.arange(PATCH)[:, None] + PATCH * (patch // 3) - SIDE // 2
            across = np.arange(PATCH)[None, :] + PATCH * (patch % 3) - SIDE // 2
            source = COSINES[r] * down - SINES[r] * across
            low = max(int(np.floor(source.min() - 1e-3)) + SIDE // 2, 0)
            high = min(int(np.floor(source.max() + 1e-3)) + 1 + SIDE // 2, SIDE - 1)
            count = high // 4 - low // 4 + 1
            out.append((r, patch, low // 4, count, offset))
            offset += count
    return out, offset


BANDS, BLOCKS = bands()
TOUCH = [[(r, patch) for r, patch, g, n, _ in BANDS if g <= group < g + n] for group in range(8)]
STARTS = [sum(len(t) for t in TOUCH[:group]) for group in range(9)]


def iota(shape, axis):
    return lax.broadcasted_iota(jnp.int32, shape, axis)


def grid_rows(grid):
    column = iota((1, LANES), 1)
    patch = (column // 128).astype(F32)
    inner = (column % 128).astype(F32)
    patch_down = jnp.floor((patch + 0.5) * (1.0 / 3.0))
    inner_down = jnp.floor((inner + 0.5) * (1.0 / PATCH))
    down = PATCH * patch_down + inner_down - SIDE // 2
    across = PATCH * (patch - 3.0 * patch_down) + inner - PATCH * inner_down - SIDE // 2
    grid[0:1, :] = across
    grid[1:2, :] = down
    grid[2:3, :] = (across * across + down * down) * (1.0 / (SIDE // 2) ** 2)
    a, d = across, down
    for s in range(4):
        inside = (a >= -16.0) & (a <= 15.0) & (d >= -16.0) & (d <= 15.0) & (inner < PATCH * PATCH - 0.5)
        grid[4 + s : 5 + s, :] = jnp.where(inside, (d + 16.0) * SIDE + a + 16.0, -1.0)
        a, d = -d, a


def split_matrix():
    source, place = iota((128, 128), 0), iota((128, 128), 1)
    return jnp.where(source == 2 * (place % 64) + place // 64, 1.0, 0.0).astype(BF16)


def join_matrix():
    source, place = iota((256, 256), 0), iota((256, 256), 1)
    inner = place % 128
    return jnp.where(source == 128 * (inner % 2) + 64 * (place // 128) + inner // 2, 1.0, 0.0).astype(BF16)


def pair_halves(first, second):
    low = iota(first.shape, 1) < 64
    real = jnp.where(low, first, pltpu.roll(second, 64, 1))
    imag = jnp.where(low, pltpu.roll(first, 64, 1), second)
    return real, imag


def column_of(row, size):
    return jnp.sum(jnp.where(iota((size, size), 0) == iota((size, size), 1), row, 0.0), axis=1, keepdims=True)


def over_lanes(a, b):
    return lax.dot_general(a, b, (((1,), (1,)), ((), ())), preferred_element_type=F32)


def make_tables(grid, tables):
    place = iota((SIDE, 128), 0).astype(F32) - float(SIDE // 2)
    for r, patch, group, count, offset in BANDS:
        qa = grid[0:1, 128 * patch : 128 * (patch + 1)]
        qd = grid[1:2, 128 * patch : 128 * (patch + 1)]
        hat_a = jnp.maximum(0.0, 1.0 - jnp.abs(COSINES[r] * qa + SINES[r] * qd - place))
        line = iota((8 * ((count + 1) // 2), 128), 0).astype(F32) + float(4 * group - SIDE // 2)
        hat_d = jnp.maximum(0.0, 1.0 - jnp.abs(COSINES[r] * qd - SINES[r] * qa - line))
        for p in range(4 * count):
            row = 128 * offset + SIDE * p
            tables[row : row + SIDE, :] = (hat_a * hat_d[p : p + 1, :]).astype(BF16)


def turn_tables(tables, tables_t):
    for r, patch, group, count, offset in BANDS:
        for i in range(count):
            place = STARTS[group + i] + TOUCH[group + i].index((r, patch))
            tables_t[128 * place : 128 * (place + 1), :] = tables[128 * (offset + i) : 128 * (offset + i + 1), :].T


def make_picks(grid, picks):
    def step(i, _):
        target = grid[pl.ds(4 + i // 4, 1), :]
        place = (iota((256, LANES), 0) + 256 * (i % 4)).astype(F32)
        picks[pl.ds(pl.multiple_of(i * 256, 256), 256), :] = jnp.where(place == target, 1.0, 0.0).astype(BF16)
        return 0

    lax.fori_loop(0, 16, step, 0)


def em_kernel(
    img_ref, ref_ref, prior_ref, focus_ref, group_ref,
    new_ref, share_ref,
    grid, tables, tables_t, picks, contrast, mrow, message, imgs, refs, flat, wide, refmat, turned, vals, square_lo,
    stat, stats, spread, rows, parts, heap, outbox, inbox,
    img_send, img_recv, ref_send, ref_recv, stat_send, stat_recv, sum_send, sum_recv, out_send, out_recv,
):
    c = lax.axis_index("cls")
    j = lax.axis_index("ptcl")
    home = j // 4
    mine = c // 4
    lane = lax.rem(j, 4)
    owner = lax.rem(c, 4) == home
    first = 4 * lax.rem(c, 4)

    def loop(low, high, body):
        def step(i, _):
            body(i)
            return 0

        lax.fori_loop(low, high, step, 0)

    def farthest(count, body):
        loop(0, count - 1, lambda i: body(count // 2 + ((i + 1) // 2) * (2 * (i % 2) - 1)))

    def owners(body):
        @functools.partial(loop, 0, NK)
        def _(i):
            g = lax.rem(mine + NK // 2 + ((i + 1) // 2) * (2 * (i % 2) - 1) + NK, NK)

            @pl.when(4 * g + home != c)
            def _():
                body(g)

    def row_peer(d):
        return {"ptcl": lax.rem(j + d, PTCL)}

    def column_peer(d):
        return {"cls": lax.rem(c + d, CLS)}

    def remote(src, dst, send, recv, device):
        return pltpu.make_async_remote_copy(
            src_ref=src, dst_ref=dst, send_sem=send, recv_sem=recv, device_id=device, device_id_type=MESH
        )

    barrier = pltpu.get_barrier_semaphore()

    @pl.when(owner)
    def _():
        farthest(CLS, lambda d: pl.semaphore_signal(barrier, inc=1, device_id=column_peer(d), device_id_type=MESH))

    @pl.when(jnp.logical_not(owner))
    def _():
        owners(lambda g: pl.semaphore_signal(
            barrier, inc=1, device_id={"cls": 4 * g + home}, device_id_type=MESH))

    farthest(PTCL, lambda d: pl.semaphore_signal(barrier, inc=1, device_id=row_peer(d), device_id_type=MESH))

    split = split_matrix()
    chosen = jnp.sum(
        jnp.where(iota((4, 2 * PIX), 0) == lane, ref_ref[...].astype(F32), 0.0), axis=0, keepdims=True
    )
    for m in range(16):
        mrow[m : m + 1, :] = chosen[:, 128 * m : 128 * (m + 1)]
    own_prior = jnp.sum(jnp.where(iota((1, 4), 1) == lane, prior_ref[...].astype(F32), 0.0), axis=1, keepdims=True)
    mrow[16:32, :] = jnp.broadcast_to(own_prior, (16, 128))
    message[...] = mrow[...].astype(BF16)
    grid_rows(grid)
    group = column_of(group_ref[...].astype(F32), NB)
    groups_count = focus_ref.shape[1]
    focus = jnp.sum(
        jnp.where(group == iota((NB, groups_count), 1).astype(F32), focus_ref[...], 0.0), axis=1, keepdims=True
    )
    phase = math.pi * focus * grid[2:3, :]
    contrast[...] = -(0.99499 * jnp.sin(phase) + 0.1 * jnp.cos(phase))
    make_tables(grid, tables)
    make_picks(grid, picks)

    @pl.when(owner)
    def _():
        pl.semaphore_wait(barrier, PTCL - 1 + CLS - 1)

    @pl.when(jnp.logical_not(owner))
    def _():
        pl.semaphore_wait(barrier, PTCL - 1 + NK)

    def ref_copy(d):
        return remote(message, refs.at[mine], ref_send.at[d], ref_recv.at[mine], column_peer(d))

    def image_copy(d, slot):
        return remote(img_ref, imgs.at[slot], img_send.at[d], img_recv.at[d], row_peer(d))

    @pl.when(owner)
    def _():
        farthest(CLS, lambda d: ref_copy(d).start())
        refs[mine] = message[...]

    farthest(PTCL, lambda d: image_copy(d, j).start())
    imgs[j] = img_ref[...]
    turn_tables(tables, tables_t)
    loop(1, PTCL, lambda d: image_copy(d, lax.rem(j + PTCL - d, PTCL)).wait_recv())

    for u in range(8):
        two = jnp.dot(imgs[2 * u : 2 * u + 2].reshape(128, 128), split, preferred_element_type=F32)
        real, imag = pair_halves(two[:NB], two[NB:])
        wide[:, 128 * u : 128 * (u + 1)] = jnp.concatenate([real, imag], axis=0).astype(BF16)

    @functools.partial(loop, 0, 4)
    def _(s):
        value = jnp.dot(
            wide[...], picks[pl.ds(pl.multiple_of(s * PIX, PIX), PIX), :], preferred_element_type=F32
        )
        here = contrast[...]
        row = pl.multiple_of(s * NB, NB)
        vals[0, pl.ds(row, NB), :] = (value[:NB] * here).astype(BF16)
        vals[1, pl.ds(row, NB), :] = (value[NB:] * here).astype(BF16)
        square = jnp.where(grid[pl.ds(4 + s, 1), :] >= 0.0, here * here, 0.0)
        high = square.astype(BF16)
        vals[2, pl.ds(row, NB), :] = high
        square_lo[pl.ds(row, NB), :] = (square - high.astype(F32)).astype(BF16)

    owners(lambda g: remote(message, refs.at[g], ref_send.at[0], ref_recv.at[g], column_peer(1)).wait_recv())

    flat[...] = jnp.dot(refs[...].reshape(NK * 32, 128), split, preferred_element_type=F32)
    for u in range(8):
        real, imag = pair_halves(
            flat[pl.ds(2 * u, NK, stride=32), :], flat[pl.ds(2 * u + 1, NK, stride=32), :]
        )
        refmat[:, 128 * u : 128 * (u + 1)] = jnp.concatenate([real, imag], axis=0).astype(BF16)
    prior = flat[pl.ds(16, NK, stride=32), :]

    for r, patch, group, count, offset in BANDS:
        both = jnp.dot(
            refmat[:, 128 * group : 128 * (group + count)],
            tables[128 * offset : 128 * (offset + count), :],
            preferred_element_type=F32,
        )
        both = both.astype(BF16).astype(F32)
        turned[0, NK * r : NK * (r + 1), 128 * patch : 128 * (patch + 1)] = both[:NK]
        turned[1, NK * r : NK * (r + 1), 128 * patch : 128 * (patch + 1)] = both[NK:]

    real, imag = turned[0], turned[1]
    match = over_lanes(real.astype(BF16), vals[0]) + over_lanes(imag.astype(BF16), vals[1])
    power = real * real + imag * imag
    power_hi = power.astype(BF16)
    power_lo = (power - power_hi.astype(F32)).astype(BF16)
    penalty = (
        over_lanes(power_hi, vals[2]) + over_lanes(power_lo, vals[2]) + over_lanes(power_hi, square_lo[...])
    )
    prior = jnp.concatenate([prior, prior], axis=1)
    logits = match - 0.5 * penalty + jnp.concatenate([prior] * BASE, axis=0)
    peak = jnp.max(logits, axis=0, keepdims=True)
    peak = jnp.maximum(peak[:, :128], peak[:, 128:])
    peak = jnp.maximum(peak, pltpu.roll(peak, 64, 1))
    total = jnp.sum(jnp.exp(logits - jnp.concatenate([peak, peak], axis=1)), axis=0, keepdims=True)
    total = total[:, :128] + total[:, 128:]
    total = total + pltpu.roll(total, 64, 1)
    stat[...] = jnp.where(iota((8, 128), 0) == 0, peak, total)

    def stat_copy(d, slot):
        return remote(stat, stats.at[slot], stat_send.at[d], stat_recv.at[d], row_peer(d))

    farthest(PTCL, lambda d: stat_copy(d, j).start())
    stats[j] = stat[...]
    loop(1, PTCL, lambda d: stat_copy(d, lax.rem(j + PTCL - d, PTCL)).wait_recv())
    peaks = stats[:, 0:1, :]
    peak = jnp.max(peaks, axis=0)
    total = jnp.sum(stats[:, 1:2, :] * jnp.exp(peaks - peak[None]), axis=0)
    weights = (
        jnp.exp(logits - jnp.concatenate([peak, peak], axis=1)) / jnp.concatenate([total, total], axis=1)
    ).astype(BF16)
    counts = jnp.sum(weights.astype(F32), axis=1, keepdims=True)
    share = counts[0:NK]
    for r in range(1, BASE):
        share = share + counts[r * NK : (r + 1) * NK]

    for part in range(3):
        spread[part] = jnp.dot(weights, vals[part], preferred_element_type=F32)
    split_sums = []
    for r in range(BASE):
        value = jnp.concatenate([spread[part, NK * r : NK * (r + 1), :] for part in range(3)], axis=0)
        high = value.astype(BF16).astype(F32)
        split_sums.append(jnp.concatenate([high, value - high], axis=0).astype(BF16))
    for group in range(8):
        points = jnp.concatenate(
            [split_sums[r][:, 128 * patch : 128 * (patch + 1)] for r, patch in TOUCH[group]], axis=1
        )
        back = jnp.dot(
            points, tables_t[128 * STARTS[group] : 128 * STARTS[group + 1], :], preferred_element_type=F32
        )
        back = back[0:24] + back[24:48]
        for part in range(3):
            rows[pl.ds(8 * part + group, NK, stride=32), :] = back[NK * part : NK * (part + 1), :]
    for i in range(24, 32):
        rows[pl.ds(i, NK, stride=32), :] = jnp.broadcast_to(share, (NK, 128))
    for k in range(NK):
        parts[k] = rows[32 * k : 32 * (k + 1), :].astype(BF16)

    def sum_copy(g):
        return remote(parts.at[g], heap.at[c], sum_send.at[g], sum_recv.at[c], {"cls": 4 * g + home})

    def out_copy(d):
        target = lax.rem(j + d, PTCL)
        return remote(outbox.at[target], inbox.at[lane], out_send.at[d], out_recv.at[lane], row_peer(d))

    owners(lambda g: sum_copy(g).start())

    @pl.when(owner)
    def _():
        heap[c] = parts[mine]

        def arrive(d):
            source = lax.rem(c + d, CLS)
            remote(parts.at[0], heap.at[source], sum_send.at[0], sum_recv.at[source], {"cls": source}).wait_recv()

        loop(1, CLS, arrive)
        sums = lax.fori_loop(1, CLS, lambda i, t: t + heap[i].astype(F32), heap[0].astype(F32))
        below = sums[16:24] + 1.0
        planes = jnp.concatenate([sums[0:8] / below, sums[8:16] / below], axis=1)
        high = planes.astype(BF16).astype(F32)
        both = jnp.concatenate([high, planes - high], axis=0).astype(BF16)
        joined = jnp.dot(both, join_matrix(), preferred_element_type=F32)
        joined = joined[0:8] + joined[8:16]
        for b in range(PTCL):
            u, h = b // 2, b % 2
            outbox[b] = jnp.where(
                iota((8, 128), 0) == 0, joined[u : u + 1, 128 * h : 128 * (h + 1)], sums[24:25, :]
            )
        farthest(PTCL, lambda d: out_copy(d).start())
        inbox[lane] = outbox[j]

    @functools.partial(loop, 0, 4)
    def _(i):
        @pl.when(first + i != j)
        def _():
            remote(outbox.at[0], inbox.at[i], out_send.at[0], out_recv.at[i], row_peer(1)).wait_recv()

    new_ref[...] = jnp.concatenate([inbox[i, 0:1, :] for i in range(4)], axis=0)
    share_row = inbox[0, 1:2, :]
    for i in range(1, 4):
        share_row = jnp.where(iota((1, 128), 1) == i, inbox[i, 1:2, :], share_row)
    share_ref[...] = share_row * (128.0 / 2048.0)

    loop(1, PTCL, lambda d: image_copy(d, j).wait_send())
    loop(1, PTCL, lambda d: stat_copy(d, j).wait_send())
    owners(lambda g: sum_copy(g).wait_send())

    @pl.when(owner)
    def _():
        loop(1, CLS, lambda d: ref_copy(d).wait_send())
        loop(1, PTCL, lambda d: out_copy(d).wait_send())


def on_device(images, references, log_prior, defocus, groups):
    vmem = pl.BlockSpec(memory_space=VMEM)
    dma = pltpu.SemaphoreType.DMA
    new, share = pl.pallas_call(
        em_kernel,
        out_shape=(jax.ShapeDtypeStruct((4, 128), F32), jax.ShapeDtypeStruct((1, 128), F32)),
        in_specs=[vmem] * 5,
        out_specs=(vmem, vmem),
        scratch_shapes=[
            VMEM((8, LANES), F32),
            VMEM((BLOCKS * 128, 128), BF16),
            VMEM((BLOCKS * 128, 128), BF16),
            VMEM((4 * PIX, LANES), BF16),
            VMEM((NB, LANES), F32),
            VMEM((32, 128), F32),
            VMEM((32, 128), BF16),
            VMEM((PTCL, NB, 128), BF16),
            VMEM((NK, 32, 128), BF16),
            VMEM((NK * 32, 128), F32),
            VMEM((2 * NB, PIX), BF16),
            VMEM((2 * NK, PIX), BF16),
            VMEM((2, ROWS, LANES), F32),
            VMEM((3, 4 * NB, LANES), BF16),
            VMEM((4 * NB, LANES), BF16),
            VMEM((8, 128), F32),
            VMEM((PTCL, 8, 128), F32),
            VMEM((3, ROWS, LANES), F32),
            VMEM((NK * 32, 128), F32),
            VMEM((NK, 32, 128), BF16),
            VMEM((CLS, 32, 128), BF16),
            VMEM((PTCL, 8, 128), F32),
            VMEM((4, 8, 128), F32),
            dma((PTCL,)),
            dma((PTCL,)),
            dma((CLS,)),
            dma((NK,)),
            dma((PTCL,)),
            dma((PTCL,)),
            dma((NK,)),
            dma((CLS,)),
            dma((PTCL,)),
            dma((4,)),
        ],
        compiler_params=pltpu.CompilerParams(
            collective_id=0, has_side_effects=True, vmem_limit_bytes=60 << 20
        ),
        name="em",
    )(images, references, log_prior[None, :], defocus[None, :], groups[None, :])
    return new, share[0, :4]


def solution(mesh):
    return jax.shard_map(
        on_device,
        mesh=mesh,
        in_specs=(P("cls", "ptcl"), P("cls", None), P("cls"), P(), P("cls")),
        out_specs=(P("cls", "ptcl"), P("cls")),
        check_vma=False,
    )
```

```python
import functools
import math

import jax
import jax.numpy as jnp
import numpy as np
from jax import lax
from jax.experimental import pallas as pl
from jax.experimental.pallas import tpu as pltpu
from jax.sharding import PartitionSpec as P

SIDE = 32
PIX = SIDE * SIDE
ROT = 36
BASE = ROT // 4
EXT = SIDE + 1
PATCH = 11
PATCHES = 9
LANES = 128 * PATCHES
CLS = 32
PTCL = 16
NK = 8
NEAR = 17
ROWS = BASE * NK
NB = 64
MESH = pl.DeviceIdType.MESH
F32 = jnp.float32
BF16 = jnp.bfloat16
VMEM = pltpu.VMEM

ANGLES = (np.float32(2.0 * math.pi) * np.arange(BASE, dtype=np.float32) / np.float32(ROT)).astype(np.float32)
COSINES = [float(x) for x in np.cos(ANGLES).astype(np.float32)]
SINES = [float(x) for x in np.sin(ANGLES).astype(np.float32)]


def bands():
    out, offset = [], 0
    for r in range(BASE):
        for patch in range(PATCHES):
            down = np.arange(PATCH)[:, None] + PATCH * (patch // 3) - SIDE // 2
            across = np.arange(PATCH)[None, :] + PATCH * (patch % 3) - SIDE // 2
            source = COSINES[r] * down - SINES[r] * across
            low = max(int(np.floor(source.min() - 1e-3)) + SIDE // 2, 0)
            high = min(int(np.floor(source.max() + 1e-3)) + 1 + SIDE // 2, SIDE - 1)
            count = high // 4 - low // 4 + 1
            out.append((r, patch, low // 4, count, offset))
            offset += count
    return out, offset


BANDS, BLOCKS = bands()
TOUCH = [[(r, patch) for r, patch, g, n, _ in BANDS if g <= group < g + n] for group in range(8)]
STARTS = [sum(len(t) for t in TOUCH[:group]) for group in range(9)]


def iota(shape, axis):
    return lax.broadcasted_iota(jnp.int32, shape, axis)


def grid_rows(grid):
    column = iota((1, LANES), 1)
    patch = (column // 128).astype(F32)
    inner = (column % 128).astype(F32)
    patch_down = jnp.floor((patch + 0.5) * (1.0 / 3.0))
    inner_down = jnp.floor((inner + 0.5) * (1.0 / PATCH))
    down = PATCH * patch_down + inner_down - SIDE // 2
    across = PATCH * (patch - 3.0 * patch_down) + inner - PATCH * inner_down - SIDE // 2
    grid[0:1, :] = across
    grid[1:2, :] = down
    grid[2:3, :] = (across * across + down * down) * (1.0 / (SIDE // 2) ** 2)
    a, d = across, down
    for s in range(4):
        inside = (a >= -16.0) & (a <= 15.0) & (d >= -16.0) & (d <= 15.0) & (inner < PATCH * PATCH - 0.5)
        grid[4 + s : 5 + s, :] = jnp.where(inside, (d + 16.0) * SIDE + a + 16.0, -1.0)
        a, d = -d, a


def split_matrix():
    source, place = iota((128, 128), 0), iota((128, 128), 1)
    return jnp.where(source == 2 * (place % 64) + place // 64, 1.0, 0.0).astype(BF16)


def join_matrix():
    source, place = iota((256, 256), 0), iota((256, 256), 1)
    inner = place % 128
    return jnp.where(source == 128 * (inner % 2) + 64 * (place // 128) + inner // 2, 1.0, 0.0).astype(BF16)


def pair_halves(first, second):
    low = iota(first.shape, 1) < 64
    real = jnp.where(low, first, pltpu.roll(second, 64, 1))
    imag = jnp.where(low, pltpu.roll(first, 64, 1), second)
    return real, imag


def column_of(row, size):
    return jnp.sum(jnp.where(iota((size, size), 0) == iota((size, size), 1), row, 0.0), axis=1, keepdims=True)


def over_lanes(a, b):
    return lax.dot_general(a, b, (((1,), (1,)), ((), ())), preferred_element_type=F32)


def make_tables(grid, tables):
    place = iota((SIDE, 128), 0).astype(F32) - float(SIDE // 2)
    for r, patch, group, count, offset in BANDS:
        qa = grid[0:1, 128 * patch : 128 * (patch + 1)]
        qd = grid[1:2, 128 * patch : 128 * (patch + 1)]
        hat_a = jnp.maximum(0.0, 1.0 - jnp.abs(COSINES[r] * qa + SINES[r] * qd - place))
        line = iota((8 * ((count + 1) // 2), 128), 0).astype(F32) + float(4 * group - SIDE // 2)
        hat_d = jnp.maximum(0.0, 1.0 - jnp.abs(COSINES[r] * qd - SINES[r] * qa - line))
        for p in range(4 * count):
            row = 128 * offset + SIDE * p
            tables[row : row + SIDE, :] = (hat_a * hat_d[p : p + 1, :]).astype(BF16)


def turn_tables(tables, tables_t):
    for r, patch, group, count, offset in BANDS:
        for i in range(count):
            place = STARTS[group + i] + TOUCH[group + i].index((r, patch))
            tables_t[128 * place : 128 * (place + 1), :] = tables[128 * (offset + i) : 128 * (offset + i + 1), :].T


def make_picks(grid, picks):
    def step(i, _):
        target = grid[pl.ds(4 + i // 4, 1), :]
        place = (iota((256, LANES), 0) + 256 * (i % 4)).astype(F32)
        picks[pl.ds(pl.multiple_of(i * 256, 256), 256), :] = jnp.where(place == target, 1.0, 0.0).astype(BF16)
        return 0

    lax.fori_loop(0, 16, step, 0)


def em_kernel(
    img_in, ref_in, prior_in, focus_in, group_in,
    new_ref, share_ref,
    grid, tables, tables_t, picks, contrast, mrow, message, imgs, refs, flat, wide, refmat, turned, vals, square_lo,
    stat, stats, spread, rows, parts, heap, outbox, inbox,
    img_ref, ref_ref, prior_ref, focus_ref, group_ref, fetched,
    img_send, img_recv, ref_send, ref_recv, stat_send, stat_recv, sum_send, sum_recv, out_send, out_recv,
):
    c = lax.axis_index("cls")
    j = lax.axis_index("ptcl")
    home = j // 4
    mine = c // 4
    lane = lax.rem(j, 4)
    owner = lax.rem(c, 4) == home
    first = 4 * lax.rem(c, 4)

    def loop(low, high, body):
        def step(i, _):
            body(i)
            return 0

        lax.fori_loop(low, high, step, 0)

    def farthest(count, body):
        loop(0, count - 1, lambda i: body(count // 2 + ((i + 1) // 2) * (2 * (i % 2) - 1)))

    def owners(body):
        @functools.partial(loop, 0, NK)
        def _(i):
            g = lax.rem(mine + NK // 2 + ((i + 1) // 2) * (2 * (i % 2) - 1) + NK, NK)

            @pl.when(4 * g + home != c)
            def _():
                body(g)

    def row_peer(d):
        return {"ptcl": lax.rem(j + d, PTCL)}

    def column_peer(d):
        return {"cls": lax.rem(c + d, CLS)}

    def remote(src, dst, send, recv, device):
        return pltpu.make_async_remote_copy(
            src_ref=src, dst_ref=dst, send_sem=send, recv_sem=recv, device_id=device, device_id_type=MESH
        )

    fetches = [
        pltpu.make_async_copy(source, place, fetched.at[i])
        for i, (source, place) in enumerate(
            [(ref_in, ref_ref), (prior_in, prior_ref), (img_in, img_ref), (focus_in, focus_ref), (group_in, group_ref)]
        )
    ]
    for fetch in fetches:
        fetch.start()

    barrier = pltpu.get_barrier_semaphore()
    z, x = c // 2, lax.rem(c, 2)

    @functools.partial(owners)
    def _(g):
        @pl.when(lax.rem(2 * g + home // 2 - z + 20, 16) <= 8)
        def _():
            pl.semaphore_signal(barrier, inc=1, device_id={"cls": 4 * g + home}, device_id_type=MESH)

    farthest(PTCL, lambda d: pl.semaphore_signal(barrier, inc=1, device_id=row_peer(d), device_id_type=MESH))
    for fetch in fetches:
        fetch.wait()

    split = split_matrix()
    chosen = jnp.sum(
        jnp.where(iota((4, 2 * PIX), 0) == lane, ref_ref[...].astype(F32), 0.0), axis=0, keepdims=True
    )
    for m in range(16):
        mrow[m : m + 1, :] = chosen[:, 128 * m : 128 * (m + 1)]
    own_prior = jnp.sum(jnp.where(iota((1, 4), 1) == lane, prior_ref[...].astype(F32), 0.0), axis=1, keepdims=True)
    mrow[16:32, :] = jnp.broadcast_to(own_prior, (16, 128))
    message[...] = mrow[...].astype(BF16)
    grid_rows(grid)
    @pl.when(owner)
    def _():
        pl.semaphore_wait(barrier, PTCL - 1 + NEAR)

    @pl.when(jnp.logical_not(owner))
    def _():
        pl.semaphore_wait(barrier, PTCL - 1)

    def near(dz, flip):
        return {"cls": 2 * lax.rem(z + dz + 16, 16) + lax.rem(x + flip, 2)}

    def ref_copy(i):
        target = near((4 - i // 4) * (1 - 2 * ((i // 2) % 2)), lax.rem(i + 1, 2))
        return remote(message, refs.at[mine], ref_send.at[i], ref_recv.at[mine], target)

    behind, ahead = lax.rem(mine + NK - 2, NK), lax.rem(mine + 2, NK)

    def pass_on(i):
        source = jnp.where(i < 8, behind, ahead)
        target = near(jnp.where(i < 8, 4 - i // 2, i // 2 - 7), lax.rem(i, 2))
        return remote(refs.at[source], refs.at[source], ref_send.at[NEAR + i], ref_recv.at[source], target)

    def ref_arrives(g):
        remote(message, refs.at[g], ref_send.at[0], ref_recv.at[g], column_peer(1)).wait_recv()

    def image_copy(d, slot):
        return remote(img_ref, imgs.at[slot], img_send.at[d], img_recv.at[d], row_peer(d))

    @pl.when(owner)
    def _():
        loop(0, NEAR, lambda i: ref_copy(i).start())
        refs[mine] = message[...]

    farthest(PTCL, lambda d: image_copy(d, j).start())
    imgs[j] = img_ref[...]

    make_tables(grid, tables)
    group = column_of(group_ref[...].astype(F32), NB)
    groups_count = focus_ref.shape[1]
    focus = jnp.sum(
        jnp.where(group == iota((NB, groups_count), 1).astype(F32), focus_ref[...], 0.0), axis=1, keepdims=True
    )
    phase = math.pi * focus * grid[2:3, :]
    contrast[...] = -(0.99499 * jnp.sin(phase) + 0.1 * jnp.cos(phase))
    make_picks(grid, picks)

    @pl.when(owner)
    def _():
        ref_arrives(behind)
        loop(0, 8, lambda i: pass_on(i).start())
        ref_arrives(ahead)
        loop(8, 14, lambda i: pass_on(i).start())

    loop(1, PTCL, lambda d: image_copy(d, lax.rem(j + PTCL - d, PTCL)).wait_recv())

    for u in range(8):
        two = jnp.dot(imgs[2 * u : 2 * u + 2].reshape(128, 128), split, preferred_element_type=F32)
        real, imag = pair_halves(two[:NB], two[NB:])
        wide[:, 128 * u : 128 * (u + 1)] = jnp.concatenate([real, imag], axis=0).astype(BF16)

    @functools.partial(loop, 0, 4)
    def _(s):
        value = jnp.dot(
            wide[...], picks[pl.ds(pl.multiple_of(s * PIX, PIX), PIX), :], preferred_element_type=F32
        )
        here = contrast[...]
        row = pl.multiple_of(s * NB, NB)
        vals[0, pl.ds(row, NB), :] = (value[:NB] * here).astype(BF16)
        vals[1, pl.ds(row, NB), :] = (value[NB:] * here).astype(BF16)
        square = jnp.where(grid[pl.ds(4 + s, 1), :] >= 0.0, here * here, 0.0)
        high = square.astype(BF16)
        vals[2, pl.ds(row, NB), :] = high
        square_lo[pl.ds(row, NB), :] = (square - high.astype(F32)).astype(BF16)

    @functools.partial(owners)
    def _(g):
        @pl.when(jnp.logical_not(owner) | ((g != behind) & (g != ahead)))
        def _():
            ref_arrives(g)


    flat[...] = jnp.dot(refs[...].reshape(NK * 32, 128), split, preferred_element_type=F32)
    for u in range(8):
        real, imag = pair_halves(
            flat[pl.ds(2 * u, NK, stride=32), :], flat[pl.ds(2 * u + 1, NK, stride=32), :]
        )
        refmat[:, 128 * u : 128 * (u + 1)] = jnp.concatenate([real, imag], axis=0).astype(BF16)
    prior = flat[pl.ds(16, NK, stride=32), :]

    for r, patch, group, count, offset in BANDS:
        both = jnp.dot(
            refmat[:, 128 * group : 128 * (group + count)],
            tables[128 * offset : 128 * (offset + count), :],
            preferred_element_type=F32,
        )
        both = both.astype(BF16).astype(F32)
        turned[0, NK * r : NK * (r + 1), 128 * patch : 128 * (patch + 1)] = both[:NK]
        turned[1, NK * r : NK * (r + 1), 128 * patch : 128 * (patch + 1)] = both[NK:]

    real, imag = turned[0], turned[1]
    match = over_lanes(real.astype(BF16), vals[0]) + over_lanes(imag.astype(BF16), vals[1])
    power = real * real + imag * imag
    power_hi = power.astype(BF16)
    power_lo = (power - power_hi.astype(F32)).astype(BF16)
    penalty = (
        over_lanes(power_hi, vals[2]) + over_lanes(power_lo, vals[2]) + over_lanes(power_hi, square_lo[...])
    )
    prior = jnp.concatenate([prior, prior], axis=1)
    logits = match - 0.5 * penalty + jnp.concatenate([prior] * BASE, axis=0)
    peak = jnp.max(logits, axis=0, keepdims=True)
    peak = jnp.maximum(peak[:, :128], peak[:, 128:])
    peak = jnp.maximum(peak, pltpu.roll(peak, 64, 1))
    total = jnp.sum(jnp.exp(logits - jnp.concatenate([peak, peak], axis=1)), axis=0, keepdims=True)
    total = total[:, :128] + total[:, 128:]
    total = total + pltpu.roll(total, 64, 1)
    stat[...] = jnp.where(iota((8, 128), 0) == 0, peak, total)

    def stat_copy(d, slot):
        return remote(stat, stats.at[slot], stat_send.at[d], stat_recv.at[d], row_peer(d))

    farthest(PTCL, lambda d: stat_copy(d, j).start())
    stats[j] = stat[...]
    turn_tables(tables, tables_t)
    loop(1, PTCL, lambda d: stat_copy(d, lax.rem(j + PTCL - d, PTCL)).wait_recv())
    peaks = stats[:, 0:1, :]
    peak = jnp.max(peaks, axis=0)
    total = jnp.sum(stats[:, 1:2, :] * jnp.exp(peaks - peak[None]), axis=0)
    weights = (
        jnp.exp(logits - jnp.concatenate([peak, peak], axis=1)) / jnp.concatenate([total, total], axis=1)
    ).astype(BF16)
    counts = jnp.sum(weights.astype(F32), axis=1, keepdims=True)
    share = counts[0:NK]
    for r in range(1, BASE):
        share = share + counts[r * NK : (r + 1) * NK]

    for part in range(3):
        spread[part] = jnp.dot(weights, vals[part], preferred_element_type=F32)
    split_sums = []
    for r in range(BASE):
        value = jnp.concatenate([spread[part, NK * r : NK * (r + 1), :] for part in range(3)], axis=0)
        high = value.astype(BF16).astype(F32)
        split_sums.append(jnp.concatenate([high, value - high], axis=0).astype(BF16))
    for group in range(8):
        points = jnp.concatenate(
            [split_sums[r][:, 128 * patch : 128 * (patch + 1)] for r, patch in TOUCH[group]], axis=1
        )
        back = jnp.dot(
            points, tables_t[128 * STARTS[group] : 128 * STARTS[group + 1], :], preferred_element_type=F32
        )
        back = back[0:24] + back[24:48]
        for part in range(3):
            rows[pl.ds(8 * part + group, NK, stride=32), :] = back[NK * part : NK * (part + 1), :]
    for i in range(24, 32):
        rows[pl.ds(i, NK, stride=32), :] = jnp.broadcast_to(share, (NK, 128))
    for k in range(NK):
        parts[k] = rows[32 * k : 32 * (k + 1), :].astype(BF16)

    def sum_copy(g):
        return remote(parts.at[g], heap.at[c], sum_send.at[g], sum_recv.at[c], {"cls": 4 * g + home})

    def out_copy(d):
        target = lax.rem(j + d, PTCL)
        return remote(outbox.at[target], inbox.at[lane], out_send.at[d], out_recv.at[lane], row_peer(d))

    owners(lambda g: sum_copy(g).start())

    @pl.when(owner)
    def _():
        heap[c] = parts[mine]

        def arrive(d):
            source = lax.rem(c + d, CLS)
            remote(parts.at[0], heap.at[source], sum_send.at[0], sum_recv.at[source], {"cls": source}).wait_recv()

        loop(1, CLS, arrive)
        sums = lax.fori_loop(1, CLS, lambda i, t: t + heap[i].astype(F32), heap[0].astype(F32))
        below = sums[16:24] + 1.0
        planes = jnp.concatenate([sums[0:8] / below, sums[8:16] / below], axis=1)
        high = planes.astype(BF16).astype(F32)
        both = jnp.concatenate([high, planes - high], axis=0).astype(BF16)
        joined = jnp.dot(both, join_matrix(), preferred_element_type=F32)
        joined = joined[0:8] + joined[8:16]
        for b in range(PTCL):
            u, h = b // 2, b % 2
            outbox[b] = jnp.where(
                iota((8, 128), 0) == 0, joined[u : u + 1, 128 * h : 128 * (h + 1)], sums[24:25, :]
            )
        farthest(PTCL, lambda d: out_copy(d).start())
        inbox[lane] = outbox[j]

    @functools.partial(loop, 0, 4)
    def _(i):
        @pl.when(first + i != j)
        def _():
            remote(outbox.at[0], inbox.at[i], out_send.at[0], out_recv.at[i], row_peer(1)).wait_recv()

    new_ref[...] = jnp.concatenate([inbox[i, 0:1, :] for i in range(4)], axis=0)
    share_row = inbox[0, 1:2, :]
    for i in range(1, 4):
        share_row = jnp.where(iota((1, 128), 1) == i, inbox[i, 1:2, :], share_row)
    share_ref[...] = share_row * (128.0 / 2048.0)

    loop(1, PTCL, lambda d: image_copy(d, j).wait_send())
    loop(1, PTCL, lambda d: stat_copy(d, j).wait_send())
    owners(lambda g: sum_copy(g).wait_send())

    @pl.when(owner)
    def _():
        loop(0, NEAR, lambda i: ref_copy(i).wait_send())
        loop(0, 14, lambda i: pass_on(i).wait_send())
        loop(1, PTCL, lambda d: out_copy(d).wait_send())


def on_device(images, references, log_prior, defocus, groups):
    vmem = pl.BlockSpec(memory_space=VMEM)
    dma = pltpu.SemaphoreType.DMA
    new, share = pl.pallas_call(
        em_kernel,
        out_shape=(VMEM((4, 128), F32), VMEM((1, 128), F32)),
        in_specs=[pl.BlockSpec(memory_space=pl.ANY)] * 5,
        out_specs=(vmem, vmem),
        scratch_shapes=[
            VMEM((8, LANES), F32),
            VMEM((BLOCKS * 128, 128), BF16),
            VMEM((BLOCKS * 128, 128), BF16),
            VMEM((4 * PIX, LANES), BF16),
            VMEM((NB, LANES), F32),
            VMEM((32, 128), F32),
            VMEM((32, 128), BF16),
            VMEM((PTCL, NB, 128), BF16),
            VMEM((NK, 32, 128), BF16),
            VMEM((NK * 32, 128), F32),
            VMEM((2 * NB, PIX), BF16),
            VMEM((2 * NK, PIX), BF16),
            VMEM((2, ROWS, LANES), F32),
            VMEM((3, 4 * NB, LANES), BF16),
            VMEM((4 * NB, LANES), BF16),
            VMEM((8, 128), F32),
            VMEM((PTCL, 8, 128), F32),
            VMEM((3, ROWS, LANES), F32),
            VMEM((NK * 32, 128), F32),
            VMEM((NK, 32, 128), BF16),
            VMEM((CLS, 32, 128), BF16),
            VMEM((PTCL, 8, 128), F32),
            VMEM((4, 8, 128), F32),
            VMEM((NB, 128), BF16),
            VMEM((4, 2 * PIX), BF16),
            VMEM((1, 4), BF16),
            VMEM((1, defocus.shape[0]), F32),
            VMEM((1, NB), jnp.int32),
            dma((5,)),
            dma((PTCL,)),
            dma((PTCL,)),
            dma((CLS,)),
            dma((NK,)),
            dma((PTCL,)),
            dma((PTCL,)),
            dma((NK,)),
            dma((CLS,)),
            dma((PTCL,)),
            dma((4,)),
        ],
        compiler_params=pltpu.CompilerParams(
            collective_id=0, has_side_effects=True, vmem_limit_bytes=60 << 20
        ),
        name="em",
    )(images, references, log_prior[None, :], defocus[None, :], groups[None, :])
    return new, share[0, :4]


def solution(mesh):
    return jax.shard_map(
        on_device,
        mesh=mesh,
        in_specs=(P("cls", "ptcl"), P("cls", None), P("cls"), P(), P("cls")),
        out_specs=(P("cls", "ptcl"), P("cls")),
        check_vma=False,
    )
```

```python
import functools
import math

import jax
import jax.numpy as jnp
import numpy as np
from jax import lax
from jax.experimental import pallas as pl
from jax.experimental.pallas import tpu as pltpu
from jax.sharding import PartitionSpec as P

SIDE = 32
PIX = SIDE * SIDE
ROT = 36
BASE = ROT // 4
EXT = SIDE + 1
PATCH = 11
PATCHES = 9
LANES = 128 * PATCHES
CLS = 32
PTCL = 16
NK = 8
NEAR = 17
ROWS = BASE * NK
NB = 64
MESH = pl.DeviceIdType.MESH
F32 = jnp.float32
BF16 = jnp.bfloat16
VMEM = pltpu.VMEM

ANGLES = (np.float32(2.0 * math.pi) * np.arange(BASE, dtype=np.float32) / np.float32(ROT)).astype(np.float32)
COSINES = [float(x) for x in np.cos(ANGLES).astype(np.float32)]
SINES = [float(x) for x in np.sin(ANGLES).astype(np.float32)]


def bands():
    out, offset = [], 0
    for r in range(BASE):
        for patch in range(PATCHES):
            down = np.arange(PATCH)[:, None] + PATCH * (patch // 3) - SIDE // 2
            across = np.arange(PATCH)[None, :] + PATCH * (patch % 3) - SIDE // 2
            source = COSINES[r] * down - SINES[r] * across
            low = max(int(np.floor(source.min() - 1e-3)) + SIDE // 2, 0)
            high = min(int(np.floor(source.max() + 1e-3)) + 1 + SIDE // 2, SIDE - 1)
            count = high // 4 - low // 4 + 1
            out.append((r, patch, low // 4, count, offset))
            offset += count
    return out, offset


BANDS, BLOCKS = bands()
TOUCH = [[(r, patch) for r, patch, g, n, _ in BANDS if g <= group < g + n] for group in range(8)]
STARTS = [sum(len(t) for t in TOUCH[:group]) for group in range(9)]


def iota(shape, axis):
    return lax.broadcasted_iota(jnp.int32, shape, axis)


def grid_rows(grid):
    column = iota((1, LANES), 1)
    patch = (column // 128).astype(F32)
    inner = (column % 128).astype(F32)
    patch_down = jnp.floor((patch + 0.5) * (1.0 / 3.0))
    inner_down = jnp.floor((inner + 0.5) * (1.0 / PATCH))
    down = PATCH * patch_down + inner_down - SIDE // 2
    across = PATCH * (patch - 3.0 * patch_down) + inner - PATCH * inner_down - SIDE // 2
    grid[0:1, :] = across
    grid[1:2, :] = down
    grid[2:3, :] = (across * across + down * down) * (1.0 / (SIDE // 2) ** 2)
    a, d = across, down
    for s in range(4):
        inside = (a >= -16.0) & (a <= 15.0) & (d >= -16.0) & (d <= 15.0) & (inner < PATCH * PATCH - 0.5)
        grid[4 + s : 5 + s, :] = jnp.where(inside, (d + 16.0) * SIDE + a + 16.0, -1.0)
        a, d = -d, a


def split_matrix():
    source, place = iota((128, 128), 0), iota((128, 128), 1)
    return jnp.where(source == 2 * (place % 64) + place // 64, 1.0, 0.0).astype(BF16)


def join_matrix():
    source, place = iota((256, 256), 0), iota((256, 256), 1)
    inner = place % 128
    return jnp.where(source == 128 * (inner % 2) + 64 * (place // 128) + inner // 2, 1.0, 0.0).astype(BF16)


def pair_halves(first, second):
    low = iota(first.shape, 1) < 64
    real = jnp.where(low, first, pltpu.roll(second, 64, 1))
    imag = jnp.where(low, pltpu.roll(first, 64, 1), second)
    return real, imag


def column_of(row, size):
    return jnp.sum(jnp.where(iota((size, size), 0) == iota((size, size), 1), row, 0.0), axis=1, keepdims=True)


def over_lanes(a, b):
    return lax.dot_general(a, b, (((1,), (1,)), ((), ())), preferred_element_type=F32)


def make_tables(grid, tables):
    place = iota((SIDE, 128), 0).astype(F32) - float(SIDE // 2)
    for r, patch, group, count, offset in BANDS:
        qa = grid[0:1, 128 * patch : 128 * (patch + 1)]
        qd = grid[1:2, 128 * patch : 128 * (patch + 1)]
        hat_a = jnp.maximum(0.0, 1.0 - jnp.abs(COSINES[r] * qa + SINES[r] * qd - place))
        line = iota((8 * ((count + 1) // 2), 128), 0).astype(F32) + float(4 * group - SIDE // 2)
        hat_d = jnp.maximum(0.0, 1.0 - jnp.abs(COSINES[r] * qd - SINES[r] * qa - line))
        for p in range(4 * count):
            row = 128 * offset + SIDE * p
            tables[row : row + SIDE, :] = (hat_a * hat_d[p : p + 1, :]).astype(BF16)


def turn_tables(tables, tables_t):
    for r, patch, group, count, offset in BANDS:
        for i in range(count):
            place = STARTS[group + i] + TOUCH[group + i].index((r, patch))
            tables_t[128 * place : 128 * (place + 1), :] = tables[128 * (offset + i) : 128 * (offset + i + 1), :].T


def make_picks(grid, picks):
    def step(i, _):
        target = grid[pl.ds(4 + i // 4, 1), :]
        place = (iota((256, LANES), 0) + 256 * (i % 4)).astype(F32)
        picks[pl.ds(pl.multiple_of(i * 256, 256), 256), :] = jnp.where(place == target, 1.0, 0.0).astype(BF16)
        return 0

    lax.fori_loop(0, 16, step, 0)


def em_kernel(
    img_in, ref_in, prior_in, focus_in, group_in,
    new_ref, share_ref,
    grid, tables, tables_t, picks, contrast, mrow, message, imgs, refs, flat, wide, refmat, turned, vals, square_lo,
    stat, stats, spread, rows, parts, heap, outbox, inbox,
    img_ref, ref_ref, prior_ref, focus_ref, group_ref, fetched,
    img_send, img_recv, ref_send, ref_recv, stat_send, stat_recv, sum_send, sum_recv, out_send, out_recv,
):
    c = lax.axis_index("cls")
    j = lax.axis_index("ptcl")
    home = j // 4
    mine = c // 4
    lane = lax.rem(j, 4)
    owner = lax.rem(c, 4) == home
    first = 4 * lax.rem(c, 4)

    def loop(low, high, body):
        def step(i, _):
            body(i)
            return 0

        lax.fori_loop(low, high, step, 0)

    def farthest(count, body):
        loop(0, count - 1, lambda i: body(count // 2 + ((i + 1) // 2) * (2 * (i % 2) - 1)))

    def owners(body):
        @functools.partial(loop, 0, NK)
        def _(i):
            g = lax.rem(mine + NK // 2 + ((i + 1) // 2) * (2 * (i % 2) - 1) + NK, NK)

            @pl.when(4 * g + home != c)
            def _():
                body(g)

    def row_peer(d):
        return {"ptcl": lax.rem(j + d, PTCL)}

    def column_peer(d):
        return {"cls": lax.rem(c + d, CLS)}

    def remote(src, dst, send, recv, device):
        return pltpu.make_async_remote_copy(
            src_ref=src, dst_ref=dst, send_sem=send, recv_sem=recv, device_id=device, device_id_type=MESH
        )

    fetches = [
        pltpu.make_async_copy(source, place, fetched.at[i])
        for i, (source, place) in enumerate(
            [(ref_in, ref_ref), (prior_in, prior_ref), (img_in, img_ref), (focus_in, focus_ref), (group_in, group_ref)]
        )
    ]
    for fetch in fetches:
        fetch.start()

    barrier = pltpu.get_barrier_semaphore()
    z, x = c // 2, lax.rem(c, 2)

    @functools.partial(owners)
    def _(g):
        other = 2 * g + home // 2

        @pl.when((lax.rem(other - z + 20, 16) <= 8) | (other > z))
        def _():
            pl.semaphore_signal(barrier, inc=1, device_id={"cls": 4 * g + home}, device_id_type=MESH)

    farthest(PTCL, lambda d: pl.semaphore_signal(barrier, inc=1, device_id=row_peer(d), device_id_type=MESH))
    for fetch in fetches:
        fetch.wait()

    split = split_matrix()
    chosen = jnp.sum(
        jnp.where(iota((4, 2 * PIX), 0) == lane, ref_ref[...].astype(F32), 0.0), axis=0, keepdims=True
    )
    for m in range(16):
        mrow[m : m + 1, :] = chosen[:, 128 * m : 128 * (m + 1)]
    own_prior = jnp.sum(jnp.where(iota((1, 4), 1) == lane, prior_ref[...].astype(F32), 0.0), axis=1, keepdims=True)
    mrow[16:32, :] = jnp.broadcast_to(own_prior, (16, 128))
    message[...] = mrow[...].astype(BF16)
    grid_rows(grid)
    def near(dz, flip):
        return {"cls": 2 * lax.rem(z + dz + 16, 16) + lax.rem(x + flip, 2)}

    def ref_copy(i):
        target = near((4 - i // 4) * (1 - 2 * ((i // 2) % 2)), lax.rem(i + 1, 2))
        return remote(message, refs.at[mine], ref_send.at[i], ref_recv.at[mine], target)

    behind, ahead = lax.rem(mine + NK - 2, NK), lax.rem(mine + 2, NK)

    def pass_on(i):
        source = jnp.where(i < 8, behind, ahead)
        target = near(jnp.where(i < 8, 4 - i // 2, i // 2 - 7), lax.rem(i, 2))
        return remote(refs.at[source], refs.at[source], ref_send.at[NEAR + i], ref_recv.at[source], target)

    def passed(low, high, body):
        @functools.partial(loop, low, high)
        def _(i):
            start = jnp.where(i < 8, lax.rem(z + 12, 16), lax.rem(z + 4, 16))

            @pl.when(start + jnp.where(i < 8, 8 - i // 2, 5 + i // 2) < 16)
            def _():
                body(pass_on(i))

    def far_copies(body):
        @functools.partial(loop, 0, 14)
        def _(i):
            k = 5 + i // 2

            @pl.when(z + k >= 16)
            def _():
                body(remote(
                    message, refs.at[mine], ref_send.at[NEAR + 14 + i], ref_recv.at[mine], near(k, lax.rem(i, 2))
                ))

    def ref_arrives(g):
        remote(message, refs.at[g], ref_send.at[0], ref_recv.at[g], column_peer(1)).wait_recv()

    def image_copy(d, slot):
        return remote(img_ref, imgs.at[slot], img_send.at[d], img_recv.at[d], row_peer(d))

    def prepare():
        make_tables(grid, tables)
        group = column_of(group_ref[...].astype(F32), NB)
        groups_count = focus_ref.shape[1]
        focus = jnp.sum(
            jnp.where(group == iota((NB, groups_count), 1).astype(F32), focus_ref[...], 0.0), axis=1, keepdims=True
        )
        phase = math.pi * focus * grid[2:3, :]
        contrast[...] = -(0.99499 * jnp.sin(phase) + 0.1 * jnp.cos(phase))
        make_picks(grid, picks)

    def send_out():
        @pl.when(owner)
        def _():
            pl.semaphore_wait(barrier, PTCL - 1 + NEAR + 2 * jnp.clip(z - 4, 0, 7))
            far_copies(lambda copy: copy.start())
            loop(0, NEAR, lambda i: ref_copy(i).start())

        @pl.when(jnp.logical_not(owner))
        def _():
            pl.semaphore_wait(barrier, PTCL - 1)

        farthest(PTCL, lambda d: image_copy(d, j).start())

        @pl.when(owner)
        def _():
            refs[mine] = message[...]

        imgs[j] = img_ref[...]

        @pl.when(owner)
        def _():
            ref_arrives(behind)
            passed(0, 8, lambda copy: copy.start())
            ref_arrives(ahead)
            passed(8, 14, lambda copy: copy.start())

    last = ((z >= 7) & (z <= 11)).astype(jnp.int32)

    @functools.partial(loop, 0, 2)
    def _(turn):
        @pl.when(turn == last)
        def _():
            prepare()

        @pl.when(turn == 0)
        def _():
            send_out()

    loop(1, PTCL, lambda d: image_copy(d, lax.rem(j + PTCL - d, PTCL)).wait_recv())

    for u in range(8):
        two = jnp.dot(imgs[2 * u : 2 * u + 2].reshape(128, 128), split, preferred_element_type=F32)
        real, imag = pair_halves(two[:NB], two[NB:])
        wide[:, 128 * u : 128 * (u + 1)] = jnp.concatenate([real, imag], axis=0).astype(BF16)

    @functools.partial(loop, 0, 4)
    def _(s):
        value = jnp.dot(
            wide[...], picks[pl.ds(pl.multiple_of(s * PIX, PIX), PIX), :], preferred_element_type=F32
        )
        here = contrast[...]
        row = pl.multiple_of(s * NB, NB)
        vals[0, pl.ds(row, NB), :] = (value[:NB] * here).astype(BF16)
        vals[1, pl.ds(row, NB), :] = (value[NB:] * here).astype(BF16)
        square = jnp.where(grid[pl.ds(4 + s, 1), :] >= 0.0, here * here, 0.0)
        high = square.astype(BF16)
        vals[2, pl.ds(row, NB), :] = high
        square_lo[pl.ds(row, NB), :] = (square - high.astype(F32)).astype(BF16)

    @functools.partial(owners)
    def _(g):
        @pl.when(jnp.logical_not(owner) | ((g != behind) & (g != ahead)))
        def _():
            ref_arrives(g)


    flat[...] = jnp.dot(refs[...].reshape(NK * 32, 128), split, preferred_element_type=F32)
    for u in range(8):
        real, imag = pair_halves(
            flat[pl.ds(2 * u, NK, stride=32), :], flat[pl.ds(2 * u + 1, NK, stride=32), :]
        )
        refmat[:, 128 * u : 128 * (u + 1)] = jnp.concatenate([real, imag], axis=0).astype(BF16)
    prior = flat[pl.ds(16, NK, stride=32), :]

    for r, patch, group, count, offset in BANDS:
        both = jnp.dot(
            refmat[:, 128 * group : 128 * (group + count)],
            tables[128 * offset : 128 * (offset + count), :],
            preferred_element_type=F32,
        )
        both = both.astype(BF16).astype(F32)
        turned[0, NK * r : NK * (r + 1), 128 * patch : 128 * (patch + 1)] = both[:NK]
        turned[1, NK * r : NK * (r + 1), 128 * patch : 128 * (patch + 1)] = both[NK:]

    real, imag = turned[0], turned[1]
    match = over_lanes(real.astype(BF16), vals[0]) + over_lanes(imag.astype(BF16), vals[1])
    power = real * real + imag * imag
    power_hi = power.astype(BF16)
    power_lo = (power - power_hi.astype(F32)).astype(BF16)
    penalty = (
        over_lanes(power_hi, vals[2]) + over_lanes(power_lo, vals[2]) + over_lanes(power_hi, square_lo[...])
    )
    prior = jnp.concatenate([prior, prior], axis=1)
    logits = match - 0.5 * penalty + jnp.concatenate([prior] * BASE, axis=0)
    peak = jnp.max(logits, axis=0, keepdims=True)
    peak = jnp.maximum(peak[:, :128], peak[:, 128:])
    peak = jnp.maximum(peak, pltpu.roll(peak, 64, 1))
    total = jnp.sum(jnp.exp(logits - jnp.concatenate([peak, peak], axis=1)), axis=0, keepdims=True)
    total = total[:, :128] + total[:, 128:]
    total = total + pltpu.roll(total, 64, 1)
    stat[...] = jnp.where(iota((8, 128), 0) == 0, peak, total)

    def stat_copy(d, slot):
        return remote(stat, stats.at[slot], stat_send.at[d], stat_recv.at[d], row_peer(d))

    farthest(PTCL, lambda d: stat_copy(d, j).start())
    stats[j] = stat[...]
    turn_tables(tables, tables_t)
    loop(1, PTCL, lambda d: image_copy(d, j).wait_send())

    @pl.when(owner)
    def _():
        loop(0, NEAR, lambda i: ref_copy(i).wait_send())
        passed(0, 14, lambda copy: copy.wait_send())
        far_copies(lambda copy: copy.wait_send())

    loop(1, PTCL, lambda d: stat_copy(d, lax.rem(j + PTCL - d, PTCL)).wait_recv())
    peaks = stats[:, 0:1, :]
    peak = jnp.max(peaks, axis=0)
    total = jnp.sum(stats[:, 1:2, :] * jnp.exp(peaks - peak[None]), axis=0)
    weights = (
        jnp.exp(logits - jnp.concatenate([peak, peak], axis=1)) / jnp.concatenate([total, total], axis=1)
    ).astype(BF16)
    counts = jnp.sum(weights.astype(F32), axis=1, keepdims=True)
    share = counts[0:NK]
    for r in range(1, BASE):
        share = share + counts[r * NK : (r + 1) * NK]

    for part in range(3):
        spread[part] = jnp.dot(weights, vals[part], preferred_element_type=F32)
    split_sums = []
    for r in range(BASE):
        value = jnp.concatenate([spread[part, NK * r : NK * (r + 1), :] for part in range(3)], axis=0)
        high = value.astype(BF16).astype(F32)
        split_sums.append(jnp.concatenate([high, value - high], axis=0).astype(BF16))
    for group in range(8):
        points = jnp.concatenate(
            [split_sums[r][:, 128 * patch : 128 * (patch + 1)] for r, patch in TOUCH[group]], axis=1
        )
        back = jnp.dot(
            points, tables_t[128 * STARTS[group] : 128 * STARTS[group + 1], :], preferred_element_type=F32
        )
        back = back[0:24] + back[24:48]
        for part in range(3):
            rows[pl.ds(8 * part + group, NK, stride=32), :] = back[NK * part : NK * (part + 1), :]
    for i in range(24, 32):
        rows[pl.ds(i, NK, stride=32), :] = jnp.broadcast_to(share, (NK, 128))
    for k in range(NK):
        parts[k] = rows[32 * k : 32 * (k + 1), :].astype(BF16)

    def sum_copy(g):
        return remote(parts.at[g], heap.at[c], sum_send.at[g], sum_recv.at[c], {"cls": 4 * g + home})

    def out_copy(d):
        target = lax.rem(j + d, PTCL)
        return remote(outbox.at[target], inbox.at[lane], out_send.at[d], out_recv.at[lane], row_peer(d))

    owners(lambda g: sum_copy(g).start())
    loop(1, PTCL, lambda d: stat_copy(d, j).wait_send())

    @pl.when(owner)
    def _():
        def arrive(i, total):
            source = lax.rem(c + CLS + ((i + 2) // 2) * (1 - 2 * lax.rem(i, 2)), CLS)
            remote(parts.at[0], heap.at[source], sum_send.at[0], sum_recv.at[source], {"cls": source}).wait_recv()
            return total + heap[source].astype(F32)

        sums = lax.fori_loop(0, CLS - 1, arrive, parts[mine].astype(F32))
        below = sums[16:24] + 1.0
        planes = jnp.concatenate([sums[0:8] / below, sums[8:16] / below], axis=1)
        high = planes.astype(BF16).astype(F32)
        both = jnp.concatenate([high, planes - high], axis=0).astype(BF16)
        joined = jnp.dot(both, join_matrix(), preferred_element_type=F32)
        joined = joined[0:8] + joined[8:16]
        for b in range(PTCL):
            u, h = b // 2, b % 2
            outbox[b] = jnp.where(
                iota((8, 128), 0) == 0, joined[u : u + 1, 128 * h : 128 * (h + 1)], sums[24:25, :]
            )
        farthest(PTCL, lambda d: out_copy(d).start())
        inbox[lane] = outbox[j]

    owners(lambda g: sum_copy(g).wait_send())

    @functools.partial(loop, 0, 4)
    def _(i):
        @pl.when(first + i != j)
        def _():
            remote(outbox.at[0], inbox.at[i], out_send.at[0], out_recv.at[i], row_peer(1)).wait_recv()

    new_ref[...] = jnp.concatenate([inbox[i, 0:1, :] for i in range(4)], axis=0)
    share_row = inbox[0, 1:2, :]
    for i in range(1, 4):
        share_row = jnp.where(iota((1, 128), 1) == i, inbox[i, 1:2, :], share_row)
    share_ref[...] = share_row * (128.0 / 2048.0)


    @pl.when(owner)
    def _():
        loop(1, PTCL, lambda d: out_copy(d).wait_send())


def on_device(images, references, log_prior, defocus, groups):
    vmem = pl.BlockSpec(memory_space=VMEM)
    dma = pltpu.SemaphoreType.DMA
    new, share = pl.pallas_call(
        em_kernel,
        out_shape=(VMEM((4, 128), F32), VMEM((1, 128), F32)),
        in_specs=[pl.BlockSpec(memory_space=pl.ANY)] * 5,
        out_specs=(vmem, vmem),
        scratch_shapes=[
            VMEM((8, LANES), F32),
            VMEM((BLOCKS * 128, 128), BF16),
            VMEM((BLOCKS * 128, 128), BF16),
            VMEM((4 * PIX, LANES), BF16),
            VMEM((NB, LANES), F32),
            VMEM((32, 128), F32),
            VMEM((32, 128), BF16),
            VMEM((PTCL, NB, 128), BF16),
            VMEM((NK, 32, 128), BF16),
            VMEM((NK * 32, 128), F32),
            VMEM((2 * NB, PIX), BF16),
            VMEM((2 * NK, PIX), BF16),
            VMEM((2, ROWS, LANES), F32),
            VMEM((3, 4 * NB, LANES), BF16),
            VMEM((4 * NB, LANES), BF16),
            VMEM((8, 128), F32),
            VMEM((PTCL, 8, 128), F32),
            VMEM((3, ROWS, LANES), F32),
            VMEM((NK * 32, 128), F32),
            VMEM((NK, 32, 128), BF16),
            VMEM((CLS, 32, 128), BF16),
            VMEM((PTCL, 8, 128), F32),
            VMEM((4, 8, 128), F32),
            VMEM((NB, 128), BF16),
            VMEM((4, 2 * PIX), BF16),
            VMEM((1, 4), BF16),
            VMEM((1, defocus.shape[0]), F32),
            VMEM((1, NB), jnp.int32),
            dma((5,)),
            dma((PTCL,)),
            dma((PTCL,)),
            dma((NEAR + 28,)),
            dma((NK,)),
            dma((PTCL,)),
            dma((PTCL,)),
            dma((NK,)),
            dma((CLS,)),
            dma((PTCL,)),
            dma((4,)),
        ],
        compiler_params=pltpu.CompilerParams(
            collective_id=0, has_side_effects=True, vmem_limit_bytes=60 << 20
        ),
        name="em",
    )(images, references, log_prior[None, :], defocus[None, :], groups[None, :])
    return new, share[0, :4]


def solution(mesh):
    return jax.shard_map(
        on_device,
        mesh=mesh,
        in_specs=(P("cls", "ptcl"), P("cls", None), P("cls"), P(), P("cls")),
        out_specs=(P("cls", "ptcl"), P("cls")),
        check_vma=False,
    )
```

```python
import functools
import math

import jax
import jax.numpy as jnp
import numpy as np
from jax import lax
from jax.experimental import pallas as pl
from jax.experimental.pallas import tpu as pltpu
from jax.sharding import PartitionSpec as P

SIDE = 32
PIX = SIDE * SIDE
ROT = 36
BASE = ROT // 4
EXT = SIDE + 1
PATCH = 11
PATCHES = 9
LANES = 128 * PATCHES
CLS = 32
PTCL = 16
NK = 8
NEAR = 17
ROWS = BASE * NK
NB = 64
MESH = pl.DeviceIdType.MESH
F32 = jnp.float32
BF16 = jnp.bfloat16
VMEM = pltpu.VMEM

ANGLES = (np.float32(2.0 * math.pi) * np.arange(BASE, dtype=np.float32) / np.float32(ROT)).astype(np.float32)
COSINES = [float(x) for x in np.cos(ANGLES).astype(np.float32)]
SINES = [float(x) for x in np.sin(ANGLES).astype(np.float32)]


def bands():
    out, offset = [], 0
    for r in range(BASE):
        for patch in range(PATCHES):
            down = np.arange(PATCH)[:, None] + PATCH * (patch // 3) - SIDE // 2
            across = np.arange(PATCH)[None, :] + PATCH * (patch % 3) - SIDE // 2
            source = COSINES[r] * down - SINES[r] * across
            low = max(int(np.floor(source.min() - 1e-3)) + SIDE // 2, 0)
            high = min(int(np.floor(source.max() + 1e-3)) + 1 + SIDE // 2, SIDE - 1)
            count = high // 4 - low // 4 + 1
            out.append((r, patch, low // 4, count, offset))
            offset += count
    return out, offset


BANDS, BLOCKS = bands()
TOUCH = [[(r, patch) for r, patch, g, n, _ in BANDS if g <= group < g + n] for group in range(8)]
STARTS = [sum(len(t) for t in TOUCH[:group]) for group in range(9)]


def iota(shape, axis):
    return lax.broadcasted_iota(jnp.int32, shape, axis)


def grid_rows(grid):
    column = iota((1, LANES), 1)
    patch = (column // 128).astype(F32)
    inner = (column % 128).astype(F32)
    patch_down = jnp.floor((patch + 0.5) * (1.0 / 3.0))
    inner_down = jnp.floor((inner + 0.5) * (1.0 / PATCH))
    down = PATCH * patch_down + inner_down - SIDE // 2
    across = PATCH * (patch - 3.0 * patch_down) + inner - PATCH * inner_down - SIDE // 2
    grid[0:1, :] = across
    grid[1:2, :] = down
    grid[2:3, :] = (across * across + down * down) * (1.0 / (SIDE // 2) ** 2)
    a, d = across, down
    for s in range(4):
        inside = (a >= -16.0) & (a <= 15.0) & (d >= -16.0) & (d <= 15.0) & (inner < PATCH * PATCH - 0.5)
        grid[4 + s : 5 + s, :] = jnp.where(inside, (d + 16.0) * SIDE + a + 16.0, -1.0)
        a, d = -d, a


def split_matrix():
    source, place = iota((128, 128), 0), iota((128, 128), 1)
    return jnp.where(source == 2 * (place % 64) + place // 64, 1.0, 0.0).astype(BF16)


def join_matrix():
    source, place = iota((256, 256), 0), iota((256, 256), 1)
    inner = place % 128
    return jnp.where(source == 128 * (inner % 2) + 64 * (place // 128) + inner // 2, 1.0, 0.0).astype(BF16)


def pair_halves(first, second):
    low = iota(first.shape, 1) < 64
    real = jnp.where(low, first, pltpu.roll(second, 64, 1))
    imag = jnp.where(low, pltpu.roll(first, 64, 1), second)
    return real, imag


def column_of(row, size):
    return jnp.sum(jnp.where(iota((size, size), 0) == iota((size, size), 1), row, 0.0), axis=1, keepdims=True)


def over_lanes(a, b):
    return lax.dot_general(a, b, (((1,), (1,)), ((), ())), preferred_element_type=F32)


def make_tables(grid, tables):
    place = iota((SIDE, 128), 0).astype(F32) - float(SIDE // 2)
    for r, patch, group, count, offset in BANDS:
        qa = grid[0:1, 128 * patch : 128 * (patch + 1)]
        qd = grid[1:2, 128 * patch : 128 * (patch + 1)]
        hat_a = jnp.maximum(0.0, 1.0 - jnp.abs(COSINES[r] * qa + SINES[r] * qd - place))
        line = iota((8 * ((count + 1) // 2), 128), 0).astype(F32) + float(4 * group - SIDE // 2)
        hat_d = jnp.maximum(0.0, 1.0 - jnp.abs(COSINES[r] * qd - SINES[r] * qa - line))
        for p in range(4 * count):
            row = 128 * offset + SIDE * p
            tables[row : row + SIDE, :] = (hat_a * hat_d[p : p + 1, :]).astype(BF16)


def turn_tables(tables, tables_t):
    for r, patch, group, count, offset in BANDS:
        for i in range(count):
            place = STARTS[group + i] + TOUCH[group + i].index((r, patch))
            tables_t[128 * place : 128 * (place + 1), :] = tables[128 * (offset + i) : 128 * (offset + i + 1), :].T


def make_picks(grid, picks):
    def step(i, _):
        target = grid[pl.ds(4 + i // 4, 1), :]
        place = (iota((256, LANES), 0) + 256 * (i % 4)).astype(F32)
        picks[pl.ds(pl.multiple_of(i * 256, 256), 256), :] = jnp.where(place == target, 1.0, 0.0).astype(BF16)
        return 0

    lax.fori_loop(0, 16, step, 0)


def em_kernel(
    img_in, ref_in, prior_in, focus_in, group_in,
    new_ref, share_ref,
    grid, tables, tables_t, picks, contrast, mrow, message, imgs, refs, flat, wide, refmat, turned, vals, square_lo,
    stat, stats, spread, rows, parts, heap, outbox, inbox,
    img_ref, ref_ref, prior_ref, focus_ref, group_ref, fetched,
    img_send, img_recv, ref_send, ref_recv, stat_send, stat_recv, sum_send, sum_recv, out_send, out_recv,
):
    c = lax.axis_index("cls")
    j = lax.axis_index("ptcl")
    home = j // 4
    mine = c // 4
    lane = lax.rem(j, 4)
    owner = lax.rem(c, 4) == home
    first = 4 * lax.rem(c, 4)

    def loop(low, high, body):
        def step(i, _):
            body(i)
            return 0

        lax.fori_loop(low, high, step, 0)

    def farthest(count, body):
        loop(0, count - 1, lambda i: body(count // 2 + ((i + 1) // 2) * (2 * (i % 2) - 1)))

    def owners(body):
        @functools.partial(loop, 0, NK)
        def _(i):
            g = lax.rem(mine + NK // 2 + ((i + 1) // 2) * (2 * (i % 2) - 1) + NK, NK)

            @pl.when(4 * g + home != c)
            def _():
                body(g)

    def row_peer(d):
        return {"ptcl": lax.rem(j + d, PTCL)}

    def column_peer(d):
        return {"cls": lax.rem(c + d, CLS)}

    def remote(src, dst, send, recv, device):
        return pltpu.make_async_remote_copy(
            src_ref=src, dst_ref=dst, send_sem=send, recv_sem=recv, device_id=device, device_id_type=MESH
        )

    fetches = [
        pltpu.make_async_copy(source, place, fetched.at[i])
        for i, (source, place) in enumerate(
            [(ref_in, ref_ref), (prior_in, prior_ref), (img_in, img_ref), (focus_in, focus_ref), (group_in, group_ref)]
        )
    ]
    for fetch in fetches:
        fetch.start()

    barrier = pltpu.get_barrier_semaphore()
    z, x = c // 2, lax.rem(c, 2)

    @functools.partial(owners)
    def _(g):
        other = 2 * g + home // 2

        @pl.when((lax.rem(other - z + 20, 16) <= 8) | (other > z))
        def _():
            pl.semaphore_signal(barrier, inc=1, device_id={"cls": 4 * g + home}, device_id_type=MESH)

    farthest(PTCL, lambda d: pl.semaphore_signal(barrier, inc=1, device_id=row_peer(d), device_id_type=MESH))
    for fetch in fetches:
        fetch.wait()

    split = split_matrix()
    chosen = jnp.sum(
        jnp.where(iota((4, 2 * PIX), 0) == lane, ref_ref[...].astype(F32), 0.0), axis=0, keepdims=True
    )
    for m in range(16):
        mrow[m : m + 1, :] = chosen[:, 128 * m : 128 * (m + 1)]
    own_prior = jnp.sum(jnp.where(iota((1, 4), 1) == lane, prior_ref[...].astype(F32), 0.0), axis=1, keepdims=True)
    mrow[16:32, :] = jnp.broadcast_to(own_prior, (16, 128))
    message[...] = mrow[...].astype(BF16)
    grid_rows(grid)
    def near(dz, flip):
        return {"cls": 2 * lax.rem(z + dz + 16, 16) + lax.rem(x + flip, 2)}

    def ref_copy(i):
        target = near((4 - i // 4) * (1 - 2 * ((i // 2) % 2)), lax.rem(i + 1, 2))
        return remote(message, refs.at[mine], ref_send.at[i], ref_recv.at[mine], target)

    behind, ahead = lax.rem(mine + NK - 2, NK), lax.rem(mine + 2, NK)

    def pass_on(i):
        source = jnp.where(i < 8, behind, ahead)
        target = near(jnp.where(i < 8, 4 - i // 2, i // 2 - 7), lax.rem(i, 2))
        return remote(refs.at[source], refs.at[source], ref_send.at[NEAR + i], ref_recv.at[source], target)

    def passed(low, high, body):
        @functools.partial(loop, low, high)
        def _(i):
            start = jnp.where(i < 8, lax.rem(z + 12, 16), lax.rem(z + 4, 16))

            @pl.when(start + jnp.where(i < 8, 8 - i // 2, 5 + i // 2) < 16)
            def _():
                body(pass_on(i))

    def far_copies(body):
        @functools.partial(loop, 0, 14)
        def _(i):
            k = 5 + i // 2

            @pl.when(z + k >= 16)
            def _():
                body(remote(
                    message, refs.at[mine], ref_send.at[NEAR + 14 + i], ref_recv.at[mine], near(k, lax.rem(i, 2))
                ))

    def ref_arrives(g):
        remote(message, refs.at[g], ref_send.at[0], ref_recv.at[g], column_peer(1)).wait_recv()

    def image_copy(d, slot):
        return remote(img_ref, imgs.at[slot], img_send.at[d], img_recv.at[d], row_peer(d))

    def prepare():
        make_tables(grid, tables)
        group = column_of(group_ref[...].astype(F32), NB)
        groups_count = focus_ref.shape[1]
        focus = jnp.sum(
            jnp.where(group == iota((NB, groups_count), 1).astype(F32), focus_ref[...], 0.0), axis=1, keepdims=True
        )
        phase = math.pi * focus * grid[2:3, :]
        contrast[...] = -(0.99499 * jnp.sin(phase) + 0.1 * jnp.cos(phase))
        make_picks(grid, picks)

    def send_out():
        @pl.when(owner)
        def _():
            pl.semaphore_wait(barrier, PTCL - 1 + NEAR + 2 * jnp.clip(z - 4, 0, 7))
            far_copies(lambda copy: copy.start())
            loop(0, NEAR, lambda i: ref_copy(i).start())

        @pl.when(jnp.logical_not(owner))
        def _():
            pl.semaphore_wait(barrier, PTCL - 1)

        farthest(PTCL, lambda d: image_copy(d, j).start())

        @pl.when(owner)
        def _():
            refs[mine] = message[...]

        imgs[j] = img_ref[...]

    last = ((z >= 7) & (z <= 11)).astype(jnp.int32)

    @functools.partial(loop, 0, 2)
    def _(turn):
        @pl.when(turn == last)
        def _():
            prepare()

        @pl.when(turn == 0)
        def _():
            send_out()

    @pl.when(owner)
    def _():
        ref_arrives(behind)
        passed(0, 8, lambda copy: copy.start())
        ref_arrives(ahead)
        passed(8, 14, lambda copy: copy.start())

    loop(1, PTCL, lambda d: image_copy(d, lax.rem(j + PTCL - d, PTCL)).wait_recv())

    for u in range(8):
        two = jnp.dot(imgs[2 * u : 2 * u + 2].reshape(128, 128), split, preferred_element_type=F32)
        real, imag = pair_halves(two[:NB], two[NB:])
        wide[:, 128 * u : 128 * (u + 1)] = jnp.concatenate([real, imag], axis=0).astype(BF16)

    @functools.partial(loop, 0, 4)
    def _(s):
        value = jnp.dot(
            wide[...], picks[pl.ds(pl.multiple_of(s * PIX, PIX), PIX), :], preferred_element_type=F32
        )
        here = contrast[...]
        row = pl.multiple_of(s * NB, NB)
        vals[0, pl.ds(row, NB), :] = (value[:NB] * here).astype(BF16)
        vals[1, pl.ds(row, NB), :] = (value[NB:] * here).astype(BF16)
        square = jnp.where(grid[pl.ds(4 + s, 1), :] >= 0.0, here * here, 0.0)
        high = square.astype(BF16)
        vals[2, pl.ds(row, NB), :] = high
        square_lo[pl.ds(row, NB), :] = (square - high.astype(F32)).astype(BF16)

    @functools.partial(owners)
    def _(g):
        @pl.when(jnp.logical_not(owner) | ((g != behind) & (g != ahead)))
        def _():
            ref_arrives(g)


    flat[...] = jnp.dot(refs[...].reshape(NK * 32, 128), split, preferred_element_type=F32)
    for u in range(8):
        real, imag = pair_halves(
            flat[pl.ds(2 * u, NK, stride=32), :], flat[pl.ds(2 * u + 1, NK, stride=32), :]
        )
        refmat[:, 128 * u : 128 * (u + 1)] = jnp.concatenate([real, imag], axis=0).astype(BF16)
    prior = flat[pl.ds(16, NK, stride=32), :]

    for r, patch, group, count, offset in BANDS:
        both = jnp.dot(
            refmat[:, 128 * group : 128 * (group + count)],
            tables[128 * offset : 128 * (offset + count), :],
            preferred_element_type=F32,
        )
        both = both.astype(BF16).astype(F32)
        turned[0, NK * r : NK * (r + 1), 128 * patch : 128 * (patch + 1)] = both[:NK]
        turned[1, NK * r : NK * (r + 1), 128 * patch : 128 * (patch + 1)] = both[NK:]

    real, imag = turned[0], turned[1]
    match = over_lanes(real.astype(BF16), vals[0]) + over_lanes(imag.astype(BF16), vals[1])
    power = real * real + imag * imag
    power_hi = power.astype(BF16)
    power_lo = (power - power_hi.astype(F32)).astype(BF16)
    penalty = (
        over_lanes(power_hi, vals[2]) + over_lanes(power_lo, vals[2]) + over_lanes(power_hi, square_lo[...])
    )
    prior = jnp.concatenate([prior, prior], axis=1)
    logits = match - 0.5 * penalty + jnp.concatenate([prior] * BASE, axis=0)
    peak = jnp.max(logits, axis=0, keepdims=True)
    peak = jnp.maximum(peak[:, :128], peak[:, 128:])
    peak = jnp.maximum(peak, pltpu.roll(peak, 64, 1))
    total = jnp.sum(jnp.exp(logits - jnp.concatenate([peak, peak], axis=1)), axis=0, keepdims=True)
    total = total[:, :128] + total[:, 128:]
    total = total + pltpu.roll(total, 64, 1)
    stat[...] = jnp.where(iota((8, 128), 0) == 0, peak, total)

    def stat_copy(d, slot):
        return remote(stat, stats.at[slot], stat_send.at[d], stat_recv.at[d], row_peer(d))

    farthest(PTCL, lambda d: stat_copy(d, j).start())
    stats[j] = stat[...]
    turn_tables(tables, tables_t)
    loop(1, PTCL, lambda d: image_copy(d, j).wait_send())

    @pl.when(owner)
    def _():
        loop(0, NEAR, lambda i: ref_copy(i).wait_send())
        passed(0, 14, lambda copy: copy.wait_send())
        far_copies(lambda copy: copy.wait_send())

    loop(1, PTCL, lambda d: stat_copy(d, lax.rem(j + PTCL - d, PTCL)).wait_recv())
    peaks = stats[:, 0:1, :]
    peak = jnp.max(peaks, axis=0)
    total = jnp.sum(stats[:, 1:2, :] * jnp.exp(peaks - peak[None]), axis=0)
    weights = (
        jnp.exp(logits - jnp.concatenate([peak, peak], axis=1)) / jnp.concatenate([total, total], axis=1)
    ).astype(BF16)
    counts = jnp.sum(weights.astype(F32), axis=1, keepdims=True)
    share = counts[0:NK]
    for r in range(1, BASE):
        share = share + counts[r * NK : (r + 1) * NK]

    for part in range(3):
        spread[part] = jnp.dot(weights, vals[part], preferred_element_type=F32)
    split_sums = []
    for r in range(BASE):
        value = jnp.concatenate([spread[part, NK * r : NK * (r + 1), :] for part in range(3)], axis=0)
        high = value.astype(BF16).astype(F32)
        split_sums.append(jnp.concatenate([high, value - high], axis=0).astype(BF16))
    for group in range(8):
        points = jnp.concatenate(
            [split_sums[r][:, 128 * patch : 128 * (patch + 1)] for r, patch in TOUCH[group]], axis=1
        )
        back = jnp.dot(
            points, tables_t[128 * STARTS[group] : 128 * STARTS[group + 1], :], preferred_element_type=F32
        )
        back = back[0:24] + back[24:48]
        for part in range(3):
            rows[pl.ds(8 * part + group, NK, stride=32), :] = back[NK * part : NK * (part + 1), :]
    for i in range(24, 32):
        rows[pl.ds(i, NK, stride=32), :] = jnp.broadcast_to(share, (NK, 128))
    for k in range(NK):
        parts[k] = rows[32 * k : 32 * (k + 1), :].astype(BF16)

    def sum_copy(g):
        return remote(parts.at[g], heap.at[c], sum_send.at[g], sum_recv.at[c], {"cls": 4 * g + home})

    def out_copy(d):
        target = lax.rem(j + d, PTCL)
        return remote(outbox.at[target], inbox.at[lane], out_send.at[d], out_recv.at[lane], row_peer(d))

    owners(lambda g: sum_copy(g).start())
    loop(1, PTCL, lambda d: stat_copy(d, j).wait_send())

    @pl.when(owner)
    def _():
        def arrive(i, total):
            source = lax.rem(c + CLS + ((i + 2) // 2) * (1 - 2 * lax.rem(i, 2)), CLS)
            remote(parts.at[0], heap.at[source], sum_send.at[0], sum_recv.at[source], {"cls": source}).wait_recv()
            return total + heap[source].astype(F32)

        sums = lax.fori_loop(0, CLS - 1, arrive, parts[mine].astype(F32))
        below = sums[16:24] + 1.0
        planes = jnp.concatenate([sums[0:8] / below, sums[8:16] / below], axis=1)
        high = planes.astype(BF16).astype(F32)
        both = jnp.concatenate([high, planes - high], axis=0).astype(BF16)
        joined = jnp.dot(both, join_matrix(), preferred_element_type=F32)
        joined = joined[0:8] + joined[8:16]
        for b in range(PTCL):
            u, h = b // 2, b % 2
            outbox[b] = jnp.where(
                iota((8, 128), 0) == 0, joined[u : u + 1, 128 * h : 128 * (h + 1)], sums[24:25, :]
            )
        farthest(PTCL, lambda d: out_copy(d).start())
        inbox[lane] = outbox[j]

    owners(lambda g: sum_copy(g).wait_send())

    @functools.partial(loop, 0, 4)
    def _(i):
        @pl.when(first + i != j)
        def _():
            remote(outbox.at[0], inbox.at[i], out_send.at[0], out_recv.at[i], row_peer(1)).wait_recv()

    new_ref[...] = jnp.concatenate([inbox[i, 0:1, :] for i in range(4)], axis=0)
    share_row = inbox[0, 1:2, :]
    for i in range(1, 4):
        share_row = jnp.where(iota((1, 128), 1) == i, inbox[i, 1:2, :], share_row)
    share_ref[...] = share_row * (128.0 / 2048.0)


    @pl.when(owner)
    def _():
        loop(1, PTCL, lambda d: out_copy(d).wait_send())


def on_device(images, references, log_prior, defocus, groups):
    vmem = pl.BlockSpec(memory_space=VMEM)
    dma = pltpu.SemaphoreType.DMA
    new, share = pl.pallas_call(
        em_kernel,
        out_shape=(VMEM((4, 128), F32), VMEM((1, 128), F32)),
        in_specs=[pl.BlockSpec(memory_space=pl.ANY)] * 5,
        out_specs=(vmem, vmem),
        scratch_shapes=[
            VMEM((8, LANES), F32),
            VMEM((BLOCKS * 128, 128), BF16),
            VMEM((BLOCKS * 128, 128), BF16),
            VMEM((4 * PIX, LANES), BF16),
            VMEM((NB, LANES), F32),
            VMEM((32, 128), F32),
            VMEM((32, 128), BF16),
            VMEM((PTCL, NB, 128), BF16),
            VMEM((NK, 32, 128), BF16),
            VMEM((NK * 32, 128), F32),
            VMEM((2 * NB, PIX), BF16),
            VMEM((2 * NK, PIX), BF16),
            VMEM((2, ROWS, LANES), F32),
            VMEM((3, 4 * NB, LANES), BF16),
            VMEM((4 * NB, LANES), BF16),
            VMEM((8, 128), F32),
            VMEM((PTCL, 8, 128), F32),
            VMEM((3, ROWS, LANES), F32),
            VMEM((NK * 32, 128), F32),
            VMEM((NK, 32, 128), BF16),
            VMEM((CLS, 32, 128), BF16),
            VMEM((PTCL, 8, 128), F32),
            VMEM((4, 8, 128), F32),
            VMEM((NB, 128), BF16),
            VMEM((4, 2 * PIX), BF16),
            VMEM((1, 4), BF16),
            VMEM((1, defocus.shape[0]), F32),
            VMEM((1, NB), jnp.int32),
            dma((5,)),
            dma((PTCL,)),
            dma((PTCL,)),
            dma((NEAR + 28,)),
            dma((NK,)),
            dma((PTCL,)),
            dma((PTCL,)),
            dma((NK,)),
            dma((CLS,)),
            dma((PTCL,)),
            dma((4,)),
        ],
        compiler_params=pltpu.CompilerParams(
            collective_id=0, has_side_effects=True, vmem_limit_bytes=60 << 20
        ),
        name="em",
    )(images, references, log_prior[None, :], defocus[None, :], groups[None, :])
    return new, share[0, :4]


def solution(mesh):
    return jax.shard_map(
        on_device,
        mesh=mesh,
        in_specs=(P("cls", "ptcl"), P("cls", None), P("cls"), P(), P("cls")),
        out_specs=(P("cls", "ptcl"), P("cls")),
        check_vma=False,
    )
```

```python
import functools
import math

import jax
import jax.numpy as jnp
import numpy as np
from jax import lax
from jax.experimental import pallas as pl
from jax.experimental.pallas import tpu as pltpu
from jax.sharding import PartitionSpec as P

SIDE = 32
PIX = SIDE * SIDE
ROT = 36
BASE = ROT // 4
EXT = SIDE + 1
PATCH = 11
PATCHES = 9
LANES = 128 * PATCHES
CLS = 32
PTCL = 16
NK = 8
NEAR = 17
ROWS = BASE * NK
NB = 64
MESH = pl.DeviceIdType.MESH
F32 = jnp.float32
BF16 = jnp.bfloat16
VMEM = pltpu.VMEM

ANGLES = (np.float32(2.0 * math.pi) * np.arange(BASE, dtype=np.float32) / np.float32(ROT)).astype(np.float32)
COSINES = [float(x) for x in np.cos(ANGLES).astype(np.float32)]
SINES = [float(x) for x in np.sin(ANGLES).astype(np.float32)]


def bands():
    out, offset = [], 0
    for r in range(BASE):
        for patch in range(PATCHES):
            down = np.arange(PATCH)[:, None] + PATCH * (patch // 3) - SIDE // 2
            across = np.arange(PATCH)[None, :] + PATCH * (patch % 3) - SIDE // 2
            source = COSINES[r] * down - SINES[r] * across
            low = max(int(np.floor(source.min() - 1e-3)) + SIDE // 2, 0)
            high = min(int(np.floor(source.max() + 1e-3)) + 1 + SIDE // 2, SIDE - 1)
            count = high // 4 - low // 4 + 1
            out.append((r, patch, low // 4, count, offset))
            offset += count
    return out, offset


BANDS, BLOCKS = bands()
TOUCH = [[(r, patch) for r, patch, g, n, _ in BANDS if g <= group < g + n] for group in range(8)]
STARTS = [sum(len(t) for t in TOUCH[:group]) for group in range(9)]


def iota(shape, axis):
    return lax.broadcasted_iota(jnp.int32, shape, axis)


def grid_rows(grid):
    column = iota((1, LANES), 1)
    patch = (column // 128).astype(F32)
    inner = (column % 128).astype(F32)
    patch_down = jnp.floor((patch + 0.5) * (1.0 / 3.0))
    inner_down = jnp.floor((inner + 0.5) * (1.0 / PATCH))
    down = PATCH * patch_down + inner_down - SIDE // 2
    across = PATCH * (patch - 3.0 * patch_down) + inner - PATCH * inner_down - SIDE // 2
    grid[0:1, :] = across
    grid[1:2, :] = down
    grid[2:3, :] = (across * across + down * down) * (1.0 / (SIDE // 2) ** 2)
    a, d = across, down
    for s in range(4):
        inside = (a >= -16.0) & (a <= 15.0) & (d >= -16.0) & (d <= 15.0) & (inner < PATCH * PATCH - 0.5)
        grid[4 + s : 5 + s, :] = jnp.where(inside, (d + 16.0) * SIDE + a + 16.0, -1.0)
        a, d = -d, a


def split_matrix():
    source, place = iota((128, 128), 0), iota((128, 128), 1)
    return jnp.where(source == 2 * (place % 64) + place // 64, 1.0, 0.0).astype(BF16)


def join_matrix():
    source, place = iota((128, 128), 0), iota((128, 128), 1)
    return jnp.where(source == 64 * (place % 2) + place // 2, 1.0, 0.0).astype(BF16)


def pair_halves(first, second):
    low = iota(first.shape, 1) < 64
    real = jnp.where(low, first, pltpu.roll(second, 64, 1))
    imag = jnp.where(low, pltpu.roll(first, 64, 1), second)
    return real, imag


def column_of(row, size):
    return jnp.sum(jnp.where(iota((size, size), 0) == iota((size, size), 1), row, 0.0), axis=1, keepdims=True)


def over_lanes(a, b):
    return lax.dot_general(a, b, (((1,), (1,)), ((), ())), preferred_element_type=F32)


def make_tables(grid, tables):
    place = iota((SIDE, 128), 0).astype(F32) - float(SIDE // 2)
    for r, patch, group, count, offset in BANDS:
        qa = grid[0:1, 128 * patch : 128 * (patch + 1)]
        qd = grid[1:2, 128 * patch : 128 * (patch + 1)]
        hat_a = jnp.maximum(0.0, 1.0 - jnp.abs(COSINES[r] * qa + SINES[r] * qd - place))
        line = iota((8 * ((count + 1) // 2), 128), 0).astype(F32) + float(4 * group - SIDE // 2)
        hat_d = jnp.maximum(0.0, 1.0 - jnp.abs(COSINES[r] * qd - SINES[r] * qa - line))
        for p in range(4 * count):
            row = 128 * offset + SIDE * p
            tables[row : row + SIDE, :] = (hat_a * hat_d[p : p + 1, :]).astype(BF16)


def turn_tables(tables, tables_t):
    for r, patch, group, count, offset in BANDS:
        for i in range(count):
            place = STARTS[group + i] + TOUCH[group + i].index((r, patch))
            tables_t[128 * place : 128 * (place + 1), :] = tables[128 * (offset + i) : 128 * (offset + i + 1), :].T


def make_picks(grid, picks):
    def step(i, _):
        target = grid[pl.ds(4 + i // 4, 1), :]
        place = (iota((256, LANES), 0) + 256 * (i % 4)).astype(F32)
        picks[pl.ds(pl.multiple_of(i * 256, 256), 256), :] = jnp.where(place == target, 1.0, 0.0).astype(BF16)
        return 0

    lax.fori_loop(0, 16, step, 0)


def em_kernel(
    img_in, ref_in, prior_in, focus_in, group_in,
    new_ref, share_ref,
    grid, tables, tables_t, picks, contrast, mrow, message, imgs, refs, flat, wide, refmat, turned, vals, square_lo,
    stat, stats, spread, rows, parts, heap,
    img_ref, ref_ref, prior_ref, focus_ref, group_ref, fetched,
    img_send, img_recv, ref_send, ref_recv, stat_send, stat_recv, sum_send, sum_recv,
):
    c = lax.axis_index("cls")
    j = lax.axis_index("ptcl")
    home = j // 4
    mine = c // 4
    lane = lax.rem(j, 4)
    owner = lax.rem(c, 4) == home
    first = 4 * lax.rem(c, 4)

    def loop(low, high, body):
        def step(i, _):
            body(i)
            return 0

        lax.fori_loop(low, high, step, 0)

    def farthest(count, body):
        loop(0, count - 1, lambda i: body(count // 2 + ((i + 1) // 2) * (2 * (i % 2) - 1)))

    def owners(body):
        @functools.partial(loop, 0, NK)
        def _(i):
            g = lax.rem(mine + NK // 2 + ((i + 1) // 2) * (2 * (i % 2) - 1) + NK, NK)

            @pl.when(4 * g + home != c)
            def _():
                body(g)

    def row_peer(d):
        return {"ptcl": lax.rem(j + d, PTCL)}

    def column_peer(d):
        return {"cls": lax.rem(c + d, CLS)}

    def remote(src, dst, send, recv, device):
        return pltpu.make_async_remote_copy(
            src_ref=src, dst_ref=dst, send_sem=send, recv_sem=recv, device_id=device, device_id_type=MESH
        )

    fetches = [
        pltpu.make_async_copy(source, place, fetched.at[i])
        for i, (source, place) in enumerate(
            [(ref_in, ref_ref), (prior_in, prior_ref), (img_in, img_ref), (focus_in, focus_ref), (group_in, group_ref)]
        )
    ]
    for fetch in fetches:
        fetch.start()

    barrier = pltpu.get_barrier_semaphore()
    z, x = c // 2, lax.rem(c, 2)

    @functools.partial(owners)
    def _(g):
        @pl.when(lax.rem(2 * g + home // 2 - z + 20, 16) <= 8)
        def _():
            pl.semaphore_signal(barrier, inc=1, device_id={"cls": 4 * g + home}, device_id_type=MESH)

    farthest(PTCL, lambda d: pl.semaphore_signal(barrier, inc=1, device_id=row_peer(d), device_id_type=MESH))
    for fetch in fetches:
        fetch.wait()

    split = split_matrix()
    chosen = jnp.sum(
        jnp.where(iota((4, 2 * PIX), 0) == lane, ref_ref[...].astype(F32), 0.0), axis=0, keepdims=True
    )
    for m in range(16):
        mrow[m : m + 1, :] = chosen[:, 128 * m : 128 * (m + 1)]
    own_prior = jnp.sum(jnp.where(iota((1, 4), 1) == lane, prior_ref[...].astype(F32), 0.0), axis=1, keepdims=True)
    mrow[16:32, :] = jnp.broadcast_to(own_prior, (16, 128))
    message[...] = mrow[...].astype(BF16)
    grid_rows(grid)
    @pl.when(owner)
    def _():
        pl.semaphore_wait(barrier, PTCL - 1 + NEAR)

    @pl.when(jnp.logical_not(owner))
    def _():
        pl.semaphore_wait(barrier, PTCL - 1)

    def near(dz, flip):
        return {"cls": 2 * lax.rem(z + dz + 16, 16) + lax.rem(x + flip, 2)}

    def ref_copy(i):
        target = near((4 - i // 4) * (1 - 2 * ((i // 2) % 2)), lax.rem(i + 1, 2))
        return remote(message, refs.at[mine], ref_send.at[i], ref_recv.at[mine], target)

    behind, ahead = lax.rem(mine + NK - 2, NK), lax.rem(mine + 2, NK)

    def pass_on(i):
        source = jnp.where(i < 8, behind, ahead)
        target = near(jnp.where(i < 8, 4 - i // 2, i // 2 - 7), lax.rem(i, 2))
        return remote(refs.at[source], refs.at[source], ref_send.at[NEAR + i], ref_recv.at[source], target)

    def ref_arrives(g):
        remote(message, refs.at[g], ref_send.at[0], ref_recv.at[g], column_peer(1)).wait_recv()

    def image_copy(d, slot):
        return remote(img_ref, imgs.at[slot], img_send.at[d], img_recv.at[d], row_peer(d))

    @pl.when(owner)
    def _():
        loop(0, NEAR, lambda i: ref_copy(i).start())
        refs[mine] = message[...]

    farthest(PTCL, lambda d: image_copy(d, j).start())
    imgs[j] = img_ref[...]

    make_tables(grid, tables)
    group = column_of(group_ref[...].astype(F32), NB)
    groups_count = focus_ref.shape[1]
    focus = jnp.sum(
        jnp.where(group == iota((NB, groups_count), 1).astype(F32), focus_ref[...], 0.0), axis=1, keepdims=True
    )
    phase = math.pi * focus * grid[2:3, :]
    contrast[...] = -(0.99499 * jnp.sin(phase) + 0.1 * jnp.cos(phase))
    make_picks(grid, picks)

    @pl.when(owner)
    def _():
        ref_arrives(behind)
        loop(0, 8, lambda i: pass_on(i).start())
        ref_arrives(ahead)
        loop(8, 14, lambda i: pass_on(i).start())

    loop(1, PTCL, lambda d: image_copy(d, lax.rem(j + PTCL - d, PTCL)).wait_recv())

    for u in range(8):
        two = jnp.dot(imgs[2 * u : 2 * u + 2].reshape(128, 128), split, preferred_element_type=F32)
        real, imag = pair_halves(two[:NB], two[NB:])
        wide[:, 128 * u : 128 * (u + 1)] = jnp.concatenate([real, imag], axis=0).astype(BF16)

    @functools.partial(loop, 0, 4)
    def _(s):
        value = jnp.dot(
            wide[...], picks[pl.ds(pl.multiple_of(s * PIX, PIX), PIX), :], preferred_element_type=F32
        )
        here = contrast[...]
        row = pl.multiple_of(s * NB, NB)
        vals[0, pl.ds(row, NB), :] = (value[:NB] * here).astype(BF16)
        vals[1, pl.ds(row, NB), :] = (value[NB:] * here).astype(BF16)
        square = jnp.where(grid[pl.ds(4 + s, 1), :] >= 0.0, here * here, 0.0)
        high = square.astype(BF16)
        vals[2, pl.ds(row, NB), :] = high
        square_lo[pl.ds(row, NB), :] = (square - high.astype(F32)).astype(BF16)

    @functools.partial(owners)
    def _(g):
        @pl.when(jnp.logical_not(owner) | ((g != behind) & (g != ahead)))
        def _():
            ref_arrives(g)


    flat[...] = jnp.dot(refs[...].reshape(NK * 32, 128), split, preferred_element_type=F32)
    for u in range(8):
        real, imag = pair_halves(
            flat[pl.ds(2 * u, NK, stride=32), :], flat[pl.ds(2 * u + 1, NK, stride=32), :]
        )
        refmat[:, 128 * u : 128 * (u + 1)] = jnp.concatenate([real, imag], axis=0).astype(BF16)
    prior = flat[pl.ds(16, NK, stride=32), :]

    for r, patch, group, count, offset in BANDS:
        both = jnp.dot(
            refmat[:, 128 * group : 128 * (group + count)],
            tables[128 * offset : 128 * (offset + count), :],
            preferred_element_type=F32,
        )
        both = both.astype(BF16).astype(F32)
        turned[0, NK * r : NK * (r + 1), 128 * patch : 128 * (patch + 1)] = both[:NK]
        turned[1, NK * r : NK * (r + 1), 128 * patch : 128 * (patch + 1)] = both[NK:]

    real, imag = turned[0], turned[1]
    match = over_lanes(real.astype(BF16), vals[0]) + over_lanes(imag.astype(BF16), vals[1])
    power = real * real + imag * imag
    power_hi = power.astype(BF16)
    power_lo = (power - power_hi.astype(F32)).astype(BF16)
    penalty = (
        over_lanes(power_hi, vals[2]) + over_lanes(power_lo, vals[2]) + over_lanes(power_hi, square_lo[...])
    )
    prior = jnp.concatenate([prior, prior], axis=1)
    logits = match - 0.5 * penalty + jnp.concatenate([prior] * BASE, axis=0)
    peak = jnp.max(logits, axis=0, keepdims=True)
    peak = jnp.maximum(peak[:, :128], peak[:, 128:])
    peak = jnp.maximum(peak, pltpu.roll(peak, 64, 1))
    total = jnp.sum(jnp.exp(logits - jnp.concatenate([peak, peak], axis=1)), axis=0, keepdims=True)
    total = total[:, :128] + total[:, 128:]
    total = total + pltpu.roll(total, 64, 1)
    stat[...] = jnp.where(iota((8, 128), 0) == 0, peak, total)

    def stat_copy(d, slot):
        return remote(stat, stats.at[slot], stat_send.at[d], stat_recv.at[d], row_peer(d))

    farthest(PTCL, lambda d: stat_copy(d, j).start())
    stats[j] = stat[...]
    turn_tables(tables, tables_t)
    loop(1, PTCL, lambda d: stat_copy(d, lax.rem(j + PTCL - d, PTCL)).wait_recv())
    peaks = stats[:, 0:1, :]
    peak = jnp.max(peaks, axis=0)
    total = jnp.sum(stats[:, 1:2, :] * jnp.exp(peaks - peak[None]), axis=0)
    weights = (
        jnp.exp(logits - jnp.concatenate([peak, peak], axis=1)) / jnp.concatenate([total, total], axis=1)
    ).astype(BF16)
    counts = jnp.sum(weights.astype(F32), axis=1, keepdims=True)
    share = counts[0:NK]
    for r in range(1, BASE):
        share = share + counts[r * NK : (r + 1) * NK]

    for part in range(3):
        spread[part] = jnp.dot(weights, vals[part], preferred_element_type=F32)
    split_sums = []
    for r in range(BASE):
        value = jnp.concatenate([spread[part, NK * r : NK * (r + 1), :] for part in range(3)], axis=0)
        high = value.astype(BF16).astype(F32)
        split_sums.append(jnp.concatenate([high, value - high], axis=0).astype(BF16))
    for group in range(8):
        points = jnp.concatenate(
            [split_sums[r][:, 128 * patch : 128 * (patch + 1)] for r, patch in TOUCH[group]], axis=1
        )
        back = jnp.dot(
            points, tables_t[128 * STARTS[group] : 128 * STARTS[group + 1], :], preferred_element_type=F32
        )
        back = back[0:24] + back[24:48]
        real, imag, square = back[0:8], back[8:16], back[16:24]
        low = iota((NK, 128), 1) < 64
        rows[pl.ds(4 * group, NK, stride=32), :] = jnp.where(low, real, pltpu.roll(imag, 64, 1))
        rows[pl.ds(4 * group + 1, NK, stride=32), :] = jnp.where(low, square, share)
        rows[pl.ds(4 * group + 2, NK, stride=32), :] = jnp.where(low, pltpu.roll(real, 64, 1), imag)
        rows[pl.ds(4 * group + 3, NK, stride=32), :] = jnp.where(low, pltpu.roll(square, 64, 1), share)
    for i in range(NK * PTCL):
        parts[i] = rows[2 * i : 2 * i + 2, :].astype(BF16)

    def blocks(body):
        @functools.partial(loop, 0, NK * PTCL)
        def _(i):
            step, b = i // PTCL, lax.rem(i, PTCL)
            g = lax.rem(mine + NK // 2 + ((step + 1) // 2) * (2 * (step % 2) - 1) + NK, NK)

            @pl.when((4 * g + home != c) | (b != j))
            def _():
                body(remote(
                    parts.at[PTCL * g + b], heap.at[c, lane], sum_send.at[PTCL * g + b], sum_recv.at[c, lane],
                    {"cls": 4 * g + home, "ptcl": b},
                ))

    blocks(lambda copy: copy.start())

    @pl.when(owner)
    def _():
        heap[c, lane] = parts[PTCL * mine + j]

    loop(1, PTCL, lambda d: image_copy(d, j).wait_send())
    loop(1, PTCL, lambda d: stat_copy(d, j).wait_send())

    @pl.when(owner)
    def _():
        loop(0, NEAR, lambda i: ref_copy(i).wait_send())
        loop(0, 14, lambda i: pass_on(i).wait_send())

    blocks(lambda copy: copy.wait_send())

    def arrive(i, total):
        source = lax.rem(c + CLS + ((i + 1) // 2) * (1 - 2 * lax.rem(i, 2)), CLS)

        @functools.partial(loop, 0, 4)
        def _(t):
            @pl.when((source != c) | (first + t != j))
            def _():
                remote(
                    parts.at[0], heap.at[source, t], sum_send.at[0], sum_recv.at[source, t], row_peer(1)
                ).wait_recv()

        return total + heap[source].astype(F32)

    sums = lax.fori_loop(0, CLS, arrive, jnp.zeros((4, 2, 128), F32))
    top = jnp.concatenate([sums[i, 0:1, :] for i in range(4)], axis=0)
    bottom = jnp.concatenate([sums[i, 1:2, :] for i in range(4)], axis=0)
    turned_bottom = pltpu.roll(bottom, 64, 1)
    value = top / (jnp.where(iota((4, 128), 1) < 64, bottom, turned_bottom) + 1.0)
    high = value.astype(BF16).astype(F32)
    both = jnp.concatenate([high, value - high], axis=0).astype(BF16)
    joined = jnp.dot(both, join_matrix(), preferred_element_type=F32)
    new_ref[...] = joined[0:4] + joined[4:8]
    diagonal = iota((4, 128), 0) == iota((4, 128), 1)
    share_ref[...] = jnp.sum(jnp.where(diagonal, turned_bottom, 0.0), axis=0, keepdims=True) * (128.0 / 2048.0)


def on_device(images, references, log_prior, defocus, groups):
    vmem = pl.BlockSpec(memory_space=VMEM)
    dma = pltpu.SemaphoreType.DMA
    new, share = pl.pallas_call(
        em_kernel,
        out_shape=(VMEM((4, 128), F32), VMEM((1, 128), F32)),
        in_specs=[pl.BlockSpec(memory_space=pl.ANY)] * 5,
        out_specs=(vmem, vmem),
        scratch_shapes=[
            VMEM((8, LANES), F32),
            VMEM((BLOCKS * 128, 128), BF16),
            VMEM((BLOCKS * 128, 128), BF16),
            VMEM((4 * PIX, LANES), BF16),
            VMEM((NB, LANES), F32),
            VMEM((32, 128), F32),
            VMEM((32, 128), BF16),
            VMEM((PTCL, NB, 128), BF16),
            VMEM((NK, 32, 128), BF16),
            VMEM((NK * 32, 128), F32),
            VMEM((2 * NB, PIX), BF16),
            VMEM((2 * NK, PIX), BF16),
            VMEM((2, ROWS, LANES), F32),
            VMEM((3, 4 * NB, LANES), BF16),
            VMEM((4 * NB, LANES), BF16),
            VMEM((8, 128), F32),
            VMEM((PTCL, 8, 128), F32),
            VMEM((3, ROWS, LANES), F32),
            VMEM((NK * 32, 128), F32),
            VMEM((NK * PTCL, 2, 128), BF16),
            VMEM((CLS, 4, 2, 128), BF16),
            VMEM((NB, 128), BF16),
            VMEM((4, 2 * PIX), BF16),
            VMEM((1, 4), BF16),
            VMEM((1, defocus.shape[0]), F32),
            VMEM((1, NB), jnp.int32),
            dma((5,)),
            dma((PTCL,)),
            dma((PTCL,)),
            dma((CLS,)),
            dma((NK,)),
            dma((PTCL,)),
            dma((PTCL,)),
            dma((NK * PTCL,)),
            dma((CLS, 4)),
        ],
        compiler_params=pltpu.CompilerParams(
            collective_id=0, has_side_effects=True, vmem_limit_bytes=60 << 20
        ),
        name="em",
    )(images, references, log_prior[None, :], defocus[None, :], groups[None, :])
    return new, share[0, :4]


def solution(mesh):
    return jax.shard_map(
        on_device,
        mesh=mesh,
        in_specs=(P("cls", "ptcl"), P("cls", None), P("cls"), P(), P("cls")),
        out_specs=(P("cls", "ptcl"), P("cls")),
        check_vma=False,
    )
```

```python
import functools
import math

import jax
import jax.numpy as jnp
import numpy as np
from jax import lax
from jax.experimental import pallas as pl
from jax.experimental.pallas import tpu as pltpu
from jax.sharding import PartitionSpec as P

SIDE = 32
PIX = SIDE * SIDE
ROT = 36
BASE = ROT // 4
EXT = SIDE + 1
PATCH = 11
PATCHES = 9
LANES = 128 * PATCHES
CLS = 32
PTCL = 16
NK = 8
NEAR = 17
ROWS = BASE * NK
NB = 64
MESH = pl.DeviceIdType.MESH
F32 = jnp.float32
BF16 = jnp.bfloat16
VMEM = pltpu.VMEM

ANGLES = (np.float32(2.0 * math.pi) * np.arange(BASE, dtype=np.float32) / np.float32(ROT)).astype(np.float32)
COSINES = [float(x) for x in np.cos(ANGLES).astype(np.float32)]
SINES = [float(x) for x in np.sin(ANGLES).astype(np.float32)]


def bands():
    out, offset = [], 0
    for r in range(BASE):
        for patch in range(PATCHES):
            down = np.arange(PATCH)[:, None] + PATCH * (patch // 3) - SIDE // 2
            across = np.arange(PATCH)[None, :] + PATCH * (patch % 3) - SIDE // 2
            source = COSINES[r] * down - SINES[r] * across
            low = max(int(np.floor(source.min() - 1e-3)) + SIDE // 2, 0)
            high = min(int(np.floor(source.max() + 1e-3)) + 1 + SIDE // 2, SIDE - 1)
            count = high // 4 - low // 4 + 1
            out.append((r, patch, low // 4, count, offset))
            offset += count
    return out, offset


BANDS, BLOCKS = bands()
TOUCH = [[(r, patch) for r, patch, g, n, _ in BANDS if g <= group < g + n] for group in range(8)]
STARTS = [sum(len(t) for t in TOUCH[:group]) for group in range(9)]


def iota(shape, axis):
    return lax.broadcasted_iota(jnp.int32, shape, axis)


def grid_rows(grid):
    column = iota((1, LANES), 1)
    patch = (column // 128).astype(F32)
    inner = (column % 128).astype(F32)
    patch_down = jnp.floor((patch + 0.5) * (1.0 / 3.0))
    inner_down = jnp.floor((inner + 0.5) * (1.0 / PATCH))
    down = PATCH * patch_down + inner_down - SIDE // 2
    across = PATCH * (patch - 3.0 * patch_down) + inner - PATCH * inner_down - SIDE // 2
    grid[0:1, :] = across
    grid[1:2, :] = down
    grid[2:3, :] = (across * across + down * down) * (1.0 / (SIDE // 2) ** 2)
    a, d = across, down
    for s in range(4):
        inside = (a >= -16.0) & (a <= 15.0) & (d >= -16.0) & (d <= 15.0) & (inner < PATCH * PATCH - 0.5)
        grid[4 + s : 5 + s, :] = jnp.where(inside, (d + 16.0) * SIDE + a + 16.0, -1.0)
        a, d = -d, a


def split_matrix():
    source, place = iota((128, 128), 0), iota((128, 128), 1)
    return jnp.where(source == 2 * (place % 64) + place // 64, 1.0, 0.0).astype(BF16)


def join_matrix():
    source, place = iota((256, 256), 0), iota((256, 256), 1)
    inner = place % 128
    return jnp.where(source == 128 * (inner % 2) + 64 * (place // 128) + inner // 2, 1.0, 0.0).astype(BF16)


def pair_halves(first, second):
    low = iota(first.shape, 1) < 64
    real = jnp.where(low, first, pltpu.roll(second, 64, 1))
    imag = jnp.where(low, pltpu.roll(first, 64, 1), second)
    return real, imag


def column_of(row, size):
    return jnp.sum(jnp.where(iota((size, size), 0) == iota((size, size), 1), row, 0.0), axis=1, keepdims=True)


def make_tables(grid, tables):
    place = iota((SIDE, 128), 0).astype(F32) - float(SIDE // 2)
    for r, patch, group, count, offset in BANDS:
        qa = grid[0:1, 128 * patch : 128 * (patch + 1)]
        qd = grid[1:2, 128 * patch : 128 * (patch + 1)]
        hat_a = jnp.maximum(0.0, 1.0 - jnp.abs(COSINES[r] * qa + SINES[r] * qd - place))
        line = iota((8 * ((count + 1) // 2), 128), 0).astype(F32) + float(4 * group - SIDE // 2)
        hat_d = jnp.maximum(0.0, 1.0 - jnp.abs(COSINES[r] * qd - SINES[r] * qa - line))
        for p in range(4 * count):
            row = 128 * offset + SIDE * p
            tables[row : row + SIDE, :] = (hat_a * hat_d[p : p + 1, :]).astype(BF16)


def turn_tables(tables, tables_t):
    for r, patch, group, count, offset in BANDS:
        for i in range(count):
            place = STARTS[group + i] + TOUCH[group + i].index((r, patch))
            tables_t[128 * place : 128 * (place + 1), :] = tables[128 * (offset + i) : 128 * (offset + i + 1), :].T


def make_picks(grid, picks):
    def step(i, _):
        target = grid[pl.ds(4 + i // 4, 1), :]
        place = (iota((256, LANES), 0) + 256 * (i % 4)).astype(F32)
        picks[pl.ds(pl.multiple_of(i * 256, 256), 256), :] = jnp.where(place == target, 1.0, 0.0).astype(BF16)
        return 0

    lax.fori_loop(0, 16, step, 0)


def em_kernel(
    img_in, ref_in, prior_in, focus_in, group_in,
    new_ref, share_ref,
    grid, tables, tables_t, picks, contrast, mrow, message, imgs, refs, flat, wide, refmat, turned, vals, square_lo, stack,
    stat, stats, spread, rows, parts, heap, outbox, inbox,
    img_ref, ref_ref, prior_ref, focus_ref, group_ref, fetched,
    img_send, img_recv, ref_send, ref_recv, stat_send, stat_recv, sum_send, sum_recv, out_send, out_recv,
):
    c = lax.axis_index("cls")
    j = lax.axis_index("ptcl")
    home = j // 4
    mine = c // 4
    lane = lax.rem(j, 4)
    owner = lax.rem(c, 4) == home
    first = 4 * lax.rem(c, 4)

    def loop(low, high, body):
        def step(i, _):
            body(i)
            return 0

        lax.fori_loop(low, high, step, 0)

    def farthest(count, body):
        loop(0, count - 1, lambda i: body(count // 2 + ((i + 1) // 2) * (2 * (i % 2) - 1)))

    def owners(body):
        @functools.partial(loop, 0, NK)
        def _(i):
            g = lax.rem(mine + NK // 2 + ((i + 1) // 2) * (2 * (i % 2) - 1) + NK, NK)

            @pl.when(4 * g + home != c)
            def _():
                body(g)

    def row_peer(d):
        return {"ptcl": lax.rem(j + d, PTCL)}

    def column_peer(d):
        return {"cls": lax.rem(c + d, CLS)}

    def remote(src, dst, send, recv, device):
        return pltpu.make_async_remote_copy(
            src_ref=src, dst_ref=dst, send_sem=send, recv_sem=recv, device_id=device, device_id_type=MESH
        )

    fetches = [
        pltpu.make_async_copy(source, place, fetched.at[i])
        for i, (source, place) in enumerate(
            [(ref_in, ref_ref), (prior_in, prior_ref), (img_in, img_ref), (focus_in, focus_ref), (group_in, group_ref)]
        )
    ]
    for fetch in fetches:
        fetch.start()

    barrier = pltpu.get_barrier_semaphore()
    z, x = c // 2, lax.rem(c, 2)

    @functools.partial(owners)
    def _(g):
        @pl.when(lax.rem(2 * g + home // 2 - z + 20, 16) <= 8)
        def _():
            pl.semaphore_signal(barrier, inc=1, device_id={"cls": 4 * g + home}, device_id_type=MESH)

    farthest(PTCL, lambda d: pl.semaphore_signal(barrier, inc=1, device_id=row_peer(d), device_id_type=MESH))
    for fetch in fetches:
        fetch.wait()

    split = split_matrix()
    chosen = jnp.sum(
        jnp.where(iota((4, 2 * PIX), 0) == lane, ref_ref[...].astype(F32), 0.0), axis=0, keepdims=True
    )
    for m in range(16):
        mrow[m : m + 1, :] = chosen[:, 128 * m : 128 * (m + 1)]
    own_prior = jnp.sum(jnp.where(iota((1, 4), 1) == lane, prior_ref[...].astype(F32), 0.0), axis=1, keepdims=True)
    mrow[16:32, :] = jnp.broadcast_to(own_prior, (16, 128))
    message[...] = mrow[...].astype(BF16)
    grid_rows(grid)
    @pl.when(owner)
    def _():
        pl.semaphore_wait(barrier, PTCL - 1 + NEAR)

    @pl.when(jnp.logical_not(owner))
    def _():
        pl.semaphore_wait(barrier, PTCL - 1)

    def near(dz, flip):
        return {"cls": 2 * lax.rem(z + dz + 16, 16) + lax.rem(x + flip, 2)}

    def ref_copy(i):
        target = near((4 - i // 4) * (1 - 2 * ((i // 2) % 2)), lax.rem(i + 1, 2))
        return remote(message, refs.at[mine], ref_send.at[i], ref_recv.at[mine], target)

    behind, ahead = lax.rem(mine + NK - 2, NK), lax.rem(mine + 2, NK)

    def pass_on(i):
        source = jnp.where(i < 8, behind, ahead)
        target = near(jnp.where(i < 8, 4 - i // 2, i // 2 - 7), lax.rem(i, 2))
        return remote(refs.at[source], refs.at[source], ref_send.at[NEAR + i], ref_recv.at[source], target)

    def ref_arrives(g):
        remote(message, refs.at[g], ref_send.at[0], ref_recv.at[g], column_peer(1)).wait_recv()

    def image_copy(d, slot):
        return remote(img_ref, imgs.at[slot], img_send.at[d], img_recv.at[d], row_peer(d))

    @pl.when(owner)
    def _():
        loop(0, NEAR, lambda i: ref_copy(i).start())
        refs[mine] = message[...]

    farthest(PTCL, lambda d: image_copy(d, j).start())
    imgs[j] = img_ref[...]

    make_tables(grid, tables)
    group = column_of(group_ref[...].astype(F32), NB)
    groups_count = focus_ref.shape[1]
    focus = jnp.sum(
        jnp.where(group == iota((NB, groups_count), 1).astype(F32), focus_ref[...], 0.0), axis=1, keepdims=True
    )
    phase = math.pi * focus * grid[2:3, :]
    contrast[...] = -(0.99499 * jnp.sin(phase) + 0.1 * jnp.cos(phase))
    make_picks(grid, picks)

    @pl.when(owner)
    def _():
        ref_arrives(behind)
        loop(0, 8, lambda i: pass_on(i).start())
        ref_arrives(ahead)
        loop(8, 14, lambda i: pass_on(i).start())

    loop(1, PTCL, lambda d: image_copy(d, lax.rem(j + PTCL - d, PTCL)).wait_recv())

    for u in range(8):
        two = jnp.dot(imgs[2 * u : 2 * u + 2].reshape(128, 128), split, preferred_element_type=F32)
        real, imag = pair_halves(two[:NB], two[NB:])
        wide[:, 128 * u : 128 * (u + 1)] = jnp.concatenate([real, imag], axis=0).astype(BF16)

    @functools.partial(loop, 0, 4)
    def _(s):
        value = jnp.dot(
            wide[...], picks[pl.ds(pl.multiple_of(s * PIX, PIX), PIX), :], preferred_element_type=F32
        )
        here = contrast[...]
        row = pl.multiple_of(s * NB, NB)
        vals[0, pl.ds(row, NB), :] = (value[:NB] * here).astype(BF16)
        vals[1, pl.ds(row, NB), :] = (value[NB:] * here).astype(BF16)
        square = jnp.where(grid[pl.ds(4 + s, 1), :] >= 0.0, here * here, 0.0)
        high = square.astype(BF16)
        vals[2, pl.ds(row, NB), :] = high
        square_lo[pl.ds(row, NB), :] = (square - high.astype(F32)).astype(BF16)

    for i, block in enumerate([vals[0], vals[1], vals[2], square_lo[...], vals[2]]):
        stack[LANES * i : LANES * (i + 1), :] = block.T

    @functools.partial(owners)
    def _(g):
        @pl.when(jnp.logical_not(owner) | ((g != behind) & (g != ahead)))
        def _():
            ref_arrives(g)


    flat[...] = jnp.dot(refs[...].reshape(NK * 32, 128), split, preferred_element_type=F32)
    for u in range(8):
        real, imag = pair_halves(
            flat[pl.ds(2 * u, NK, stride=32), :], flat[pl.ds(2 * u + 1, NK, stride=32), :]
        )
        refmat[:, 128 * u : 128 * (u + 1)] = jnp.concatenate([real, imag], axis=0).astype(BF16)
    prior = flat[pl.ds(16, NK, stride=32), :]

    for r, patch, group, count, offset in BANDS:
        both = jnp.dot(
            refmat[:, 128 * group : 128 * (group + count)],
            tables[128 * offset : 128 * (offset + count), :],
            preferred_element_type=F32,
        )
        both = both.astype(BF16).astype(F32)
        turned[0, NK * r : NK * (r + 1), 128 * patch : 128 * (patch + 1)] = both[:NK]
        turned[1, NK * r : NK * (r + 1), 128 * patch : 128 * (patch + 1)] = both[NK:]

    real, imag = turned[0], turned[1]
    power = -0.5 * (real * real + imag * imag)
    power_hi = power.astype(BF16)
    power_lo = (power - power_hi.astype(F32)).astype(BF16)
    left = jnp.concatenate([real.astype(BF16), imag.astype(BF16), power_hi, power_hi, power_lo], axis=1)
    scores = jnp.dot(left, stack[...], preferred_element_type=F32)
    prior = jnp.concatenate([prior, prior], axis=1)
    logits = scores + jnp.concatenate([prior] * BASE, axis=0)
    peak = jnp.max(logits, axis=0, keepdims=True)
    peak = jnp.maximum(peak[:, :128], peak[:, 128:])
    peak = jnp.maximum(peak, pltpu.roll(peak, 64, 1))
    total = jnp.sum(jnp.exp(logits - jnp.concatenate([peak, peak], axis=1)), axis=0, keepdims=True)
    total = total[:, :128] + total[:, 128:]
    total = total + pltpu.roll(total, 64, 1)
    stat[...] = jnp.where(iota((2, 128), 0) == 0, peak, total)

    def stat_copy(d, slot):
        return remote(stat, stats.at[slot], stat_send.at[d], stat_recv.at[d], row_peer(d))

    farthest(PTCL, lambda d: stat_copy(d, j).start())
    stats[j] = stat[...]
    turn_tables(tables, tables_t)
    loop(1, PTCL, lambda d: image_copy(d, j).wait_send())

    @pl.when(owner)
    def _():
        loop(0, NEAR, lambda i: ref_copy(i).wait_send())
        loop(0, 14, lambda i: pass_on(i).wait_send())

    loop(1, PTCL, lambda d: stat_copy(d, lax.rem(j + PTCL - d, PTCL)).wait_recv())
    peaks = stats[:, 0:1, :]
    peak = jnp.max(peaks, axis=0)
    total = jnp.sum(stats[:, 1:2, :] * jnp.exp(peaks - peak[None]), axis=0)
    weights = (
        jnp.exp(logits - jnp.concatenate([peak, peak], axis=1)) / jnp.concatenate([total, total], axis=1)
    ).astype(BF16)
    counts = jnp.sum(weights.astype(F32), axis=1, keepdims=True)
    share = counts[0:NK]
    for r in range(1, BASE):
        share = share + counts[r * NK : (r + 1) * NK]

    for part in range(3):
        spread[part] = jnp.dot(weights, vals[part], preferred_element_type=F32)
    split_sums = []
    for r in range(BASE):
        value = jnp.concatenate([spread[part, NK * r : NK * (r + 1), :] for part in range(3)], axis=0)
        high = value.astype(BF16).astype(F32)
        split_sums.append(jnp.concatenate([high, value - high], axis=0).astype(BF16))
    for group in range(8):
        points = jnp.concatenate(
            [split_sums[r][:, 128 * patch : 128 * (patch + 1)] for r, patch in TOUCH[group]], axis=1
        )
        back = jnp.dot(
            points, tables_t[128 * STARTS[group] : 128 * STARTS[group + 1], :], preferred_element_type=F32
        )
        back = back[0:24] + back[24:48]
        for part in range(3):
            rows[pl.ds(8 * part + group, NK, stride=32), :] = back[NK * part : NK * (part + 1), :]
    for i in range(24, 32):
        rows[pl.ds(i, NK, stride=32), :] = jnp.broadcast_to(share, (NK, 128))
    for k in range(NK):
        parts[k] = rows[32 * k : 32 * (k + 1), :].astype(BF16)

    def sum_copy(g):
        return remote(parts.at[g], heap.at[c], sum_send.at[g], sum_recv.at[c], {"cls": 4 * g + home})

    def out_copy(d):
        target = lax.rem(j + d, PTCL)
        return remote(outbox.at[target], inbox.at[lane], out_send.at[d], out_recv.at[lane], row_peer(d))

    owners(lambda g: sum_copy(g).start())
    loop(1, PTCL, lambda d: stat_copy(d, j).wait_send())

    @pl.when(owner)
    def _():
        def arrive(i, total):
            source = lax.rem(c + CLS + ((i + 2) // 2) * (1 - 2 * lax.rem(i, 2)), CLS)
            remote(parts.at[0], heap.at[source], sum_send.at[0], sum_recv.at[source], {"cls": source}).wait_recv()
            return total + heap[source].astype(F32)

        sums = lax.fori_loop(0, CLS - 1, arrive, parts[mine].astype(F32))
        below = sums[16:24] + 1.0
        planes = jnp.concatenate([sums[0:8] / below, sums[8:16] / below], axis=1)
        high = planes.astype(BF16).astype(F32)
        both = jnp.concatenate([high, planes - high], axis=0).astype(BF16)
        joined = jnp.dot(both, join_matrix(), preferred_element_type=F32)
        joined = joined[0:8] + joined[8:16]
        for b in range(PTCL):
            u, h = b // 2, b % 2
            outbox[b] = jnp.where(
                iota((2, 128), 0) == 0, joined[u : u + 1, 128 * h : 128 * (h + 1)], sums[24:25, :]
            )
        farthest(PTCL, lambda d: out_copy(d).start())
        inbox[lane] = outbox[j]

    owners(lambda g: sum_copy(g).wait_send())

    @functools.partial(loop, 0, 4)
    def _(i):
        @pl.when(first + i != j)
        def _():
            remote(outbox.at[0], inbox.at[i], out_send.at[0], out_recv.at[i], row_peer(1)).wait_recv()

    new_ref[...] = jnp.concatenate([inbox[i, 0:1, :] for i in range(4)], axis=0)
    share_row = inbox[0, 1:2, :]
    for i in range(1, 4):
        share_row = jnp.where(iota((1, 128), 1) == i, inbox[i, 1:2, :], share_row)
    share_ref[...] = share_row * (128.0 / 2048.0)


    @pl.when(owner)
    def _():
        loop(1, PTCL, lambda d: out_copy(d).wait_send())


def on_device(images, references, log_prior, defocus, groups):
    vmem = pl.BlockSpec(memory_space=VMEM)
    dma = pltpu.SemaphoreType.DMA
    new, share = pl.pallas_call(
        em_kernel,
        out_shape=(VMEM((4, 128), F32), VMEM((1, 128), F32)),
        in_specs=[pl.BlockSpec(memory_space=pl.ANY)] * 5,
        out_specs=(vmem, vmem),
        scratch_shapes=[
            VMEM((8, LANES), F32),
            VMEM((BLOCKS * 128, 128), BF16),
            VMEM((BLOCKS * 128, 128), BF16),
            VMEM((4 * PIX, LANES), BF16),
            VMEM((NB, LANES), F32),
            VMEM((32, 128), F32),
            VMEM((32, 128), BF16),
            VMEM((PTCL, NB, 128), BF16),
            VMEM((NK, 32, 128), BF16),
            VMEM((NK * 32, 128), F32),
            VMEM((2 * NB, PIX), BF16),
            VMEM((2 * NK, PIX), BF16),
            VMEM((2, ROWS, LANES), F32),
            VMEM((3, 4 * NB, LANES), BF16),
            VMEM((4 * NB, LANES), BF16),
            VMEM((5 * LANES, 4 * NB), BF16),
            VMEM((2, 128), F32),
            VMEM((PTCL, 2, 128), F32),
            VMEM((3, ROWS, LANES), F32),
            VMEM((NK * 32, 128), F32),
            VMEM((NK, 32, 128), BF16),
            VMEM((CLS, 32, 128), BF16),
            VMEM((PTCL, 2, 128), F32),
            VMEM((4, 2, 128), F32),
            VMEM((NB, 128), BF16),
            VMEM((4, 2 * PIX), BF16),
            VMEM((1, 4), BF16),
            VMEM((1, defocus.shape[0]), F32),
            VMEM((1, NB), jnp.int32),
            dma((5,)),
            dma((PTCL,)),
            dma((PTCL,)),
            dma((CLS,)),
            dma((NK,)),
            dma((PTCL,)),
            dma((PTCL,)),
            dma((NK,)),
            dma((CLS,)),
            dma((PTCL,)),
            dma((4,)),
        ],
        compiler_params=pltpu.CompilerParams(
            collective_id=0, has_side_effects=True, vmem_limit_bytes=60 << 20
        ),
        name="em",
    )(images, references, log_prior[None, :], defocus[None, :], groups[None, :])
    return new, share[0, :4]


def solution(mesh):
    return jax.shard_map(
        on_device,
        mesh=mesh,
        in_specs=(P("cls", "ptcl"), P("cls", None), P("cls"), P(), P("cls")),
        out_specs=(P("cls", "ptcl"), P("cls")),
        check_vma=False,
    )
```

```python
import functools
import math

import jax
import jax.numpy as jnp
import numpy as np
from jax import lax
from jax.experimental import pallas as pl
from jax.experimental.pallas import tpu as pltpu
from jax.sharding import PartitionSpec as P

SIDE = 32
PIX = SIDE * SIDE
ROT = 36
BASE = ROT // 4
EXT = SIDE + 1
PATCH = 11
PATCHES = 9
LANES = 128 * PATCHES
CLS = 32
PTCL = 16
NK = 8
ROWS = BASE * NK
NB = 64
MESH = pl.DeviceIdType.MESH
F32 = jnp.float32
BF16 = jnp.bfloat16
VMEM = pltpu.VMEM

ANGLES = (np.float32(2.0 * math.pi) * np.arange(BASE, dtype=np.float32) / np.float32(ROT)).astype(np.float32)
COSINES = [float(x) for x in np.cos(ANGLES).astype(np.float32)]
SINES = [float(x) for x in np.sin(ANGLES).astype(np.float32)]


def bands():
    out, offset = [], 0
    for r in range(BASE):
        for patch in range(PATCHES):
            down = np.arange(PATCH)[:, None] + PATCH * (patch // 3) - SIDE // 2
            across = np.arange(PATCH)[None, :] + PATCH * (patch % 3) - SIDE // 2
            source = COSINES[r] * down - SINES[r] * across
            low = max(int(np.floor(source.min() - 1e-3)) + SIDE // 2, 0)
            high = min(int(np.floor(source.max() + 1e-3)) + 1 + SIDE // 2, SIDE - 1)
            count = high // 4 - low // 4 + 1
            out.append((r, patch, low // 4, count, offset))
            offset += count
    return out, offset


BANDS, BLOCKS = bands()
TOUCH = [[(r, patch) for r, patch, g, n, _ in BANDS if g <= group < g + n] for group in range(8)]
STARTS = [sum(len(t) for t in TOUCH[:group]) for group in range(9)]


def iota(shape, axis):
    return lax.broadcasted_iota(jnp.int32, shape, axis)


def grid_rows(grid):
    column = iota((1, LANES), 1)
    patch = (column // 128).astype(F32)
    inner = (column % 128).astype(F32)
    patch_down = jnp.floor((patch + 0.5) * (1.0 / 3.0))
    inner_down = jnp.floor((inner + 0.5) * (1.0 / PATCH))
    down = PATCH * patch_down + inner_down - SIDE // 2
    across = PATCH * (patch - 3.0 * patch_down) + inner - PATCH * inner_down - SIDE // 2
    grid[0:1, :] = across
    grid[1:2, :] = down
    grid[2:3, :] = (across * across + down * down) * (1.0 / (SIDE // 2) ** 2)
    a, d = across, down
    for s in range(4):
        inside = (a >= -16.0) & (a <= 15.0) & (d >= -16.0) & (d <= 15.0) & (inner < PATCH * PATCH - 0.5)
        grid[4 + s : 5 + s, :] = jnp.where(inside, (d + 16.0) * SIDE + a + 16.0, -1.0)
        a, d = -d, a


def split_matrix():
    source, place = iota((128, 128), 0), iota((128, 128), 1)
    return jnp.where(source == 2 * (place % 64) + place // 64, 1.0, 0.0).astype(BF16)


def join_matrix():
    source, place = iota((256, 256), 0), iota((256, 256), 1)
    inner = place % 128
    return jnp.where(source == 128 * (inner % 2) + 64 * (place // 128) + inner // 2, 1.0, 0.0).astype(BF16)


def pair_halves(first, second):
    low = iota(first.shape, 1) < 64
    real = jnp.where(low, first, pltpu.roll(second, 64, 1))
    imag = jnp.where(low, pltpu.roll(first, 64, 1), second)
    return real, imag


def column_of(row, size):
    return jnp.sum(jnp.where(iota((size, size), 0) == iota((size, size), 1), row, 0.0), axis=1, keepdims=True)


def make_tables(grid, tables):
    place = iota((SIDE, 128), 0).astype(F32) - float(SIDE // 2)
    for r, patch, group, count, offset in BANDS:
        qa = grid[0:1, 128 * patch : 128 * (patch + 1)]
        qd = grid[1:2, 128 * patch : 128 * (patch + 1)]
        hat_a = jnp.maximum(0.0, 1.0 - jnp.abs(COSINES[r] * qa + SINES[r] * qd - place))
        line = iota((8 * ((count + 1) // 2), 128), 0).astype(F32) + float(4 * group - SIDE // 2)
        hat_d = jnp.maximum(0.0, 1.0 - jnp.abs(COSINES[r] * qd - SINES[r] * qa - line))
        for p in range(4 * count):
            row = 128 * offset + SIDE * p
            tables[row : row + SIDE, :] = (hat_a * hat_d[p : p + 1, :]).astype(BF16)


def turn_tables(tables, tables_t):
    for r, patch, group, count, offset in BANDS:
        for i in range(count):
            place = STARTS[group + i] + TOUCH[group + i].index((r, patch))
            tables_t[128 * place : 128 * (place + 1), :] = tables[128 * (offset + i) : 128 * (offset + i + 1), :].T


def make_picks(grid, picks):
    def step(i, _):
        target = grid[pl.ds(4 + i // 4, 1), :]
        place = (iota((256, LANES), 0) + 256 * (i % 4)).astype(F32)
        picks[pl.ds(pl.multiple_of(i * 256, 256), 256), :] = jnp.where(place == target, 1.0, 0.0).astype(BF16)
        return 0

    lax.fori_loop(0, 16, step, 0)


def em_kernel(
    img_in, ref_in, prior_in, focus_in, group_in,
    new_ref, share_ref,
    grid, tables, tables_t, picks, contrast, mrow, message, imgs, refs, flat, wide, refmat, turned, vals, square_lo, stack,
    stat, stats, spread, rows, parts, heap, outbox, inbox,
    img_ref, ref_ref, prior_ref, focus_ref, group_ref, fetched,
    img_send, img_recv, ref_send, ref_recv, stat_send, stat_recv, sum_send, sum_recv, out_send, out_recv,
):
    c = lax.axis_index("cls")
    j = lax.axis_index("ptcl")
    home = j // 4
    mine = c // 4
    lane = lax.rem(j, 4)
    owner = lax.rem(c, 4) == home
    first = 4 * lax.rem(c, 4)

    def loop(low, high, body):
        def step(i, _):
            body(i)
            return 0

        lax.fori_loop(low, high, step, 0)

    def farthest(count, body):
        loop(0, count - 1, lambda i: body(count // 2 + ((i + 1) // 2) * (2 * (i % 2) - 1)))

    def owners(body):
        @functools.partial(loop, 0, NK)
        def _(i):
            g = lax.rem(mine + NK // 2 + ((i + 1) // 2) * (2 * (i % 2) - 1) + NK, NK)

            @pl.when(4 * g + home != c)
            def _():
                body(g)

    def row_peer(d):
        return {"ptcl": lax.rem(j + d, PTCL)}

    def column_peer(d):
        return {"cls": lax.rem(c + d, CLS)}

    def remote(src, dst, send, recv, device):
        return pltpu.make_async_remote_copy(
            src_ref=src, dst_ref=dst, send_sem=send, recv_sem=recv, device_id=device, device_id_type=MESH
        )

    fetches = [
        pltpu.make_async_copy(source, place, fetched.at[i])
        for i, (source, place) in enumerate(
            [(ref_in, ref_ref), (prior_in, prior_ref), (img_in, img_ref), (focus_in, focus_ref), (group_in, group_ref)]
        )
    ]
    for fetch in fetches:
        fetch.start()

    barrier = pltpu.get_barrier_semaphore()
    owners(lambda g: pl.semaphore_signal(
        barrier, inc=1, device_id={"cls": 4 * g + home}, device_id_type=MESH))
    farthest(PTCL, lambda d: pl.semaphore_signal(barrier, inc=1, device_id=row_peer(d), device_id_type=MESH))
    for fetch in fetches:
        fetch.wait()

    split = split_matrix()
    chosen = jnp.sum(
        jnp.where(iota((4, 2 * PIX), 0) == lane, ref_ref[...].astype(F32), 0.0), axis=0, keepdims=True
    )
    for m in range(16):
        mrow[m : m + 1, :] = chosen[:, 128 * m : 128 * (m + 1)]
    own_prior = jnp.sum(jnp.where(iota((1, 4), 1) == lane, prior_ref[...].astype(F32), 0.0), axis=1, keepdims=True)
    mrow[16:32, :] = jnp.broadcast_to(own_prior, (16, 128))
    message[...] = mrow[...].astype(BF16)
    grid_rows(grid)
    @pl.when(owner)
    def _():
        pl.semaphore_wait(barrier, PTCL - 1 + CLS - 1)

    @pl.when(jnp.logical_not(owner))
    def _():
        pl.semaphore_wait(barrier, PTCL - 1)

    def ref_copy(d):
        return remote(message, refs.at[mine], ref_send.at[d], ref_recv.at[mine], column_peer(d))

    def ref_arrives(g):
        remote(message, refs.at[g], ref_send.at[0], ref_recv.at[g], column_peer(1)).wait_recv()

    def image_copy(d, slot):
        return remote(img_ref, imgs.at[slot], img_send.at[d], img_recv.at[d], row_peer(d))

    @pl.when(owner)
    def _():
        farthest(CLS, lambda d: ref_copy(d).start())
        refs[mine] = message[...]

    farthest(PTCL, lambda d: image_copy(d, j).start())
    imgs[j] = img_ref[...]

    make_tables(grid, tables)
    group = column_of(group_ref[...].astype(F32), NB)
    groups_count = focus_ref.shape[1]
    focus = jnp.sum(
        jnp.where(group == iota((NB, groups_count), 1).astype(F32), focus_ref[...], 0.0), axis=1, keepdims=True
    )
    phase = math.pi * focus * grid[2:3, :]
    contrast[...] = -(0.99499 * jnp.sin(phase) + 0.1 * jnp.cos(phase))
    make_picks(grid, picks)

    loop(1, PTCL, lambda d: image_copy(d, lax.rem(j + PTCL - d, PTCL)).wait_recv())

    for u in range(8):
        two = jnp.dot(imgs[2 * u : 2 * u + 2].reshape(128, 128), split, preferred_element_type=F32)
        real, imag = pair_halves(two[:NB], two[NB:])
        wide[:, 128 * u : 128 * (u + 1)] = jnp.concatenate([real, imag], axis=0).astype(BF16)

    @functools.partial(loop, 0, 4)
    def _(s):
        value = jnp.dot(
            wide[...], picks[pl.ds(pl.multiple_of(s * PIX, PIX), PIX), :], preferred_element_type=F32
        )
        here = contrast[...]
        row = pl.multiple_of(s * NB, NB)
        vals[0, pl.ds(row, NB), :] = (value[:NB] * here).astype(BF16)
        vals[1, pl.ds(row, NB), :] = (value[NB:] * here).astype(BF16)
        square = jnp.where(grid[pl.ds(4 + s, 1), :] >= 0.0, here * here, 0.0)
        high = square.astype(BF16)
        vals[2, pl.ds(row, NB), :] = high
        square_lo[pl.ds(row, NB), :] = (square - high.astype(F32)).astype(BF16)

    for i, block in enumerate([vals[0], vals[1], vals[2], square_lo[...], vals[2]]):
        stack[LANES * i : LANES * (i + 1), :] = block.T

    owners(ref_arrives)

    flat[...] = jnp.dot(refs[...].reshape(NK * 32, 128), split, preferred_element_type=F32)
    for u in range(8):
        real, imag = pair_halves(
            flat[pl.ds(2 * u, NK, stride=32), :], flat[pl.ds(2 * u + 1, NK, stride=32), :]
        )
        refmat[:, 128 * u : 128 * (u + 1)] = jnp.concatenate([real, imag], axis=0).astype(BF16)
    prior = flat[pl.ds(16, NK, stride=32), :]

    for r, patch, group, count, offset in BANDS:
        both = jnp.dot(
            refmat[:, 128 * group : 128 * (group + count)],
            tables[128 * offset : 128 * (offset + count), :],
            preferred_element_type=F32,
        )
        both = both.astype(BF16).astype(F32)
        turned[0, NK * r : NK * (r + 1), 128 * patch : 128 * (patch + 1)] = both[:NK]
        turned[1, NK * r : NK * (r + 1), 128 * patch : 128 * (patch + 1)] = both[NK:]

    real, imag = turned[0], turned[1]
    power = -0.5 * (real * real + imag * imag)
    power_hi = power.astype(BF16)
    power_lo = (power - power_hi.astype(F32)).astype(BF16)
    left = jnp.concatenate([real.astype(BF16), imag.astype(BF16), power_hi, power_hi, power_lo], axis=1)
    scores = jnp.dot(left, stack[...], preferred_element_type=F32)
    prior = jnp.concatenate([prior, prior], axis=1)
    logits = scores + jnp.concatenate([prior] * BASE, axis=0)
    peak = jnp.max(logits, axis=0, keepdims=True)
    peak = jnp.maximum(peak[:, :128], peak[:, 128:])
    peak = jnp.maximum(peak, pltpu.roll(peak, 64, 1))
    total = jnp.sum(jnp.exp(logits - jnp.concatenate([peak, peak], axis=1)), axis=0, keepdims=True)
    total = total[:, :128] + total[:, 128:]
    total = total + pltpu.roll(total, 64, 1)
    stat[...] = jnp.where(iota((2, 128), 0) == 0, peak, total)

    def stat_copy(d, slot):
        return remote(stat, stats.at[slot], stat_send.at[d], stat_recv.at[d], row_peer(d))

    farthest(PTCL, lambda d: stat_copy(d, j).start())
    stats[j] = stat[...]
    turn_tables(tables, tables_t)
    loop(1, PTCL, lambda d: image_copy(d, j).wait_send())

    @pl.when(owner)
    def _():
        loop(1, CLS, lambda d: ref_copy(d).wait_send())

    loop(1, PTCL, lambda d: stat_copy(d, lax.rem(j + PTCL - d, PTCL)).wait_recv())
    peaks = stats[:, 0:1, :]
    peak = jnp.max(peaks, axis=0)
    total = jnp.sum(stats[:, 1:2, :] * jnp.exp(peaks - peak[None]), axis=0)
    weights = (
        jnp.exp(logits - jnp.concatenate([peak, peak], axis=1)) / jnp.concatenate([total, total], axis=1)
    ).astype(BF16)
    counts = jnp.sum(weights.astype(F32), axis=1, keepdims=True)
    share = counts[0:NK]
    for r in range(1, BASE):
        share = share + counts[r * NK : (r + 1) * NK]

    for part in range(3):
        spread[part] = jnp.dot(weights, vals[part], preferred_element_type=F32)
    split_sums = []
    for r in range(BASE):
        value = jnp.concatenate([spread[part, NK * r : NK * (r + 1), :] for part in range(3)], axis=0)
        high = value.astype(BF16).astype(F32)
        split_sums.append(jnp.concatenate([high, value - high], axis=0).astype(BF16))
    for group in range(8):
        points = jnp.concatenate(
            [split_sums[r][:, 128 * patch : 128 * (patch + 1)] for r, patch in TOUCH[group]], axis=1
        )
        back = jnp.dot(
            points, tables_t[128 * STARTS[group] : 128 * STARTS[group + 1], :], preferred_element_type=F32
        )
        back = back[0:24] + back[24:48]
        for part in range(3):
            rows[pl.ds(8 * part + group, NK, stride=32), :] = back[NK * part : NK * (part + 1), :]
    for i in range(24, 32):
        rows[pl.ds(i, NK, stride=32), :] = jnp.broadcast_to(share, (NK, 128))
    for k in range(NK):
        parts[k] = rows[32 * k : 32 * (k + 1), :].astype(BF16)

    def sum_copy(g):
        return remote(parts.at[g], heap.at[c], sum_send.at[g], sum_recv.at[c], {"cls": 4 * g + home})

    def out_copy(d):
        target = lax.rem(j + d, PTCL)
        return remote(outbox.at[target], inbox.at[lane], out_send.at[d], out_recv.at[lane], row_peer(d))

    owners(lambda g: sum_copy(g).start())
    loop(1, PTCL, lambda d: stat_copy(d, j).wait_send())

    @pl.when(owner)
    def _():
        def arrive(i, total):
            source = lax.rem(c + CLS + ((i + 2) // 2) * (1 - 2 * lax.rem(i, 2)), CLS)
            remote(parts.at[0], heap.at[source], sum_send.at[0], sum_recv.at[source], {"cls": source}).wait_recv()
            return total + heap[source].astype(F32)

        sums = lax.fori_loop(0, CLS - 1, arrive, parts[mine].astype(F32))
        below = sums[16:24] + 1.0
        planes = jnp.concatenate([sums[0:8] / below, sums[8:16] / below], axis=1)
        high = planes.astype(BF16).astype(F32)
        both = jnp.concatenate([high, planes - high], axis=0).astype(BF16)
        joined = jnp.dot(both, join_matrix(), preferred_element_type=F32)
        joined = joined[0:8] + joined[8:16]
        for b in range(PTCL):
            u, h = b // 2, b % 2
            outbox[b] = jnp.where(
                iota((2, 128), 0) == 0, joined[u : u + 1, 128 * h : 128 * (h + 1)], sums[24:25, :]
            )
        farthest(PTCL, lambda d: out_copy(d).start())
        inbox[lane] = outbox[j]

    owners(lambda g: sum_copy(g).wait_send())

    @functools.partial(loop, 0, 4)
    def _(i):
        @pl.when(first + i != j)
        def _():
            remote(outbox.at[0], inbox.at[i], out_send.at[0], out_recv.at[i], row_peer(1)).wait_recv()

    new_ref[...] = jnp.concatenate([inbox[i, 0:1, :] for i in range(4)], axis=0)
    share_row = inbox[0, 1:2, :]
    for i in range(1, 4):
        share_row = jnp.where(iota((1, 128), 1) == i, inbox[i, 1:2, :], share_row)
    share_ref[...] = share_row * (128.0 / 2048.0)


    @pl.when(owner)
    def _():
        loop(1, PTCL, lambda d: out_copy(d).wait_send())


def on_device(images, references, log_prior, defocus, groups):
    vmem = pl.BlockSpec(memory_space=VMEM)
    dma = pltpu.SemaphoreType.DMA
    new, share = pl.pallas_call(
        em_kernel,
        out_shape=(VMEM((4, 128), F32), VMEM((1, 128), F32)),
        in_specs=[pl.BlockSpec(memory_space=pl.ANY)] * 5,
        out_specs=(vmem, vmem),
        scratch_shapes=[
            VMEM((8, LANES), F32),
            VMEM((BLOCKS * 128, 128), BF16),
            VMEM((BLOCKS * 128, 128), BF16),
            VMEM((4 * PIX, LANES), BF16),
            VMEM((NB, LANES), F32),
            VMEM((32, 128), F32),
            VMEM((32, 128), BF16),
            VMEM((PTCL, NB, 128), BF16),
            VMEM((NK, 32, 128), BF16),
            VMEM((NK * 32, 128), F32),
            VMEM((2 * NB, PIX), BF16),
            VMEM((2 * NK, PIX), BF16),
            VMEM((2, ROWS, LANES), F32),
            VMEM((3, 4 * NB, LANES), BF16),
            VMEM((4 * NB, LANES), BF16),
            VMEM((5 * LANES, 4 * NB), BF16),
            VMEM((2, 128), F32),
            VMEM((PTCL, 2, 128), F32),
            VMEM((3, ROWS, LANES), F32),
            VMEM((NK * 32, 128), F32),
            VMEM((NK, 32, 128), BF16),
            VMEM((CLS, 32, 128), BF16),
            VMEM((PTCL, 2, 128), F32),
            VMEM((4, 2, 128), F32),
            VMEM((NB, 128), BF16),
            VMEM((4, 2 * PIX), BF16),
            VMEM((1, 4), BF16),
            VMEM((1, defocus.shape[0]), F32),
            VMEM((1, NB), jnp.int32),
            dma((5,)),
            dma((PTCL,)),
            dma((PTCL,)),
            dma((CLS,)),
            dma((NK,)),
            dma((PTCL,)),
            dma((PTCL,)),
            dma((NK,)),
            dma((CLS,)),
            dma((PTCL,)),
            dma((4,)),
        ],
        compiler_params=pltpu.CompilerParams(
            collective_id=0, has_side_effects=True, vmem_limit_bytes=60 << 20
        ),
        name="em",
    )(images, references, log_prior[None, :], defocus[None, :], groups[None, :])
    return new, share[0, :4]


def solution(mesh):
    return jax.shard_map(
        on_device,
        mesh=mesh,
        in_specs=(P("cls", "ptcl"), P("cls", None), P("cls"), P(), P("cls")),
        out_specs=(P("cls", "ptcl"), P("cls")),
        check_vma=False,
    )
```

```python
import functools
import math

import jax
import jax.numpy as jnp
import numpy as np
from jax import lax
from jax.experimental import pallas as pl
from jax.experimental.pallas import tpu as pltpu
from jax.sharding import PartitionSpec as P

SIDE = 32
PIX = SIDE * SIDE
ROT = 36
BASE = ROT // 4
EXT = SIDE + 1
PATCH = 11
PATCHES = 9
LANES = 128 * PATCHES
CLS = 32
PTCL = 16
NK = 8
NEAR = 17
ROWS = BASE * NK
NB = 64
MESH = pl.DeviceIdType.MESH
F32 = jnp.float32
BF16 = jnp.bfloat16
VMEM = pltpu.VMEM

ANGLES = (np.float32(2.0 * math.pi) * np.arange(BASE, dtype=np.float32) / np.float32(ROT)).astype(np.float32)
COSINES = [float(x) for x in np.cos(ANGLES).astype(np.float32)]
SINES = [float(x) for x in np.sin(ANGLES).astype(np.float32)]


def bands():
    out, offset = [], 0
    for r in range(BASE):
        for patch in range(PATCHES):
            down = np.arange(PATCH)[:, None] + PATCH * (patch // 3) - SIDE // 2
            across = np.arange(PATCH)[None, :] + PATCH * (patch % 3) - SIDE // 2
            source = COSINES[r] * down - SINES[r] * across
            low = max(int(np.floor(source.min() - 1e-3)) + SIDE // 2, 0)
            high = min(int(np.floor(source.max() + 1e-3)) + 1 + SIDE // 2, SIDE - 1)
            count = high // 4 - low // 4 + 1
            out.append((r, patch, low // 4, count, offset))
            offset += count
    return out, offset


BANDS, BLOCKS = bands()
TOUCH = [[(r, patch) for r, patch, g, n, _ in BANDS if g <= group < g + n] for group in range(8)]
STARTS = [sum(len(t) for t in TOUCH[:group]) for group in range(9)]


def iota(shape, axis):
    return lax.broadcasted_iota(jnp.int32, shape, axis)


def grid_rows(grid):
    column = iota((1, LANES), 1)
    patch = (column // 128).astype(F32)
    inner = (column % 128).astype(F32)
    patch_down = jnp.floor((patch + 0.5) * (1.0 / 3.0))
    inner_down = jnp.floor((inner + 0.5) * (1.0 / PATCH))
    down = PATCH * patch_down + inner_down - SIDE // 2
    across = PATCH * (patch - 3.0 * patch_down) + inner - PATCH * inner_down - SIDE // 2
    grid[0:1, :] = across
    grid[1:2, :] = down
    grid[2:3, :] = (across * across + down * down) * (1.0 / (SIDE // 2) ** 2)
    a, d = across, down
    for s in range(4):
        inside = (a >= -16.0) & (a <= 15.0) & (d >= -16.0) & (d <= 15.0) & (inner < PATCH * PATCH - 0.5)
        grid[4 + s : 5 + s, :] = jnp.where(inside, (d + 16.0) * SIDE + a + 16.0, -1.0)
        a, d = -d, a


def split_matrix():
    source, place = iota((128, 128), 0), iota((128, 128), 1)
    return jnp.where(source == 2 * (place % 64) + place // 64, 1.0, 0.0).astype(BF16)


def join_matrix():
    source, place = iota((256, 256), 0), iota((256, 256), 1)
    inner = place % 128
    return jnp.where(source == 128 * (inner % 2) + 64 * (place // 128) + inner // 2, 1.0, 0.0).astype(BF16)


def pair_halves(first, second):
    low = iota(first.shape, 1) < 64
    real = jnp.where(low, first, pltpu.roll(second, 64, 1))
    imag = jnp.where(low, pltpu.roll(first, 64, 1), second)
    return real, imag


def column_of(row, size):
    return jnp.sum(jnp.where(iota((size, size), 0) == iota((size, size), 1), row, 0.0), axis=1, keepdims=True)


def make_tables(grid, tables):
    place = iota((SIDE, 128), 0).astype(F32) - float(SIDE // 2)
    for r, patch, group, count, offset in BANDS:
        qa = grid[0:1, 128 * patch : 128 * (patch + 1)]
        qd = grid[1:2, 128 * patch : 128 * (patch + 1)]
        hat_a = jnp.maximum(0.0, 1.0 - jnp.abs(COSINES[r] * qa + SINES[r] * qd - place))
        line = iota((8 * ((count + 1) // 2), 128), 0).astype(F32) + float(4 * group - SIDE // 2)
        hat_d = jnp.maximum(0.0, 1.0 - jnp.abs(COSINES[r] * qd - SINES[r] * qa - line))
        for p in range(4 * count):
            row = 128 * offset + SIDE * p
            tables[row : row + SIDE, :] = (hat_a * hat_d[p : p + 1, :]).astype(BF16)


def turn_tables(tables, tables_t):
    for r, patch, group, count, offset in BANDS:
        for i in range(count):
            place = STARTS[group + i] + TOUCH[group + i].index((r, patch))
            tables_t[128 * place : 128 * (place + 1), :] = tables[128 * (offset + i) : 128 * (offset + i + 1), :].T


def make_picks(grid, picks):
    def step(i, _):
        target = grid[pl.ds(4 + i // 4, 1), :]
        place = (iota((256, LANES), 0) + 256 * (i % 4)).astype(F32)
        picks[pl.ds(pl.multiple_of(i * 256, 256), 256), :] = jnp.where(place == target, 1.0, 0.0).astype(BF16)
        return 0

    lax.fori_loop(0, 16, step, 0)


def em_kernel(
    img_in, ref_in, prior_in, focus_in, group_in,
    new_ref, share_ref,
    grid, tables, tables_t, picks, contrast, mrow, message, imgs, refs, flat, wide, refmat, turned, vals, square_lo, stack,
    stat, stats, spread, rows, parts, heap, outbox, inbox,
    img_ref, ref_ref, prior_ref, focus_ref, group_ref, fetched,
    img_send, img_recv, ref_send, ref_recv, stat_send, stat_recv, sum_send, sum_recv, out_send, out_recv,
):
    c = lax.axis_index("cls")
    j = lax.axis_index("ptcl")
    home = j // 4
    mine = c // 4
    lane = lax.rem(j, 4)
    owner = lax.rem(c, 4) == home
    first = 4 * lax.rem(c, 4)

    def loop(low, high, body):
        def step(i, _):
            body(i)
            return 0

        lax.fori_loop(low, high, step, 0)

    def farthest(count, body):
        loop(0, count - 1, lambda i: body(count // 2 + ((i + 1) // 2) * (2 * (i % 2) - 1)))

    def owners(body):
        @functools.partial(loop, 0, NK)
        def _(i):
            g = lax.rem(mine + NK // 2 + ((i + 1) // 2) * (2 * (i % 2) - 1) + NK, NK)

            @pl.when(4 * g + home != c)
            def _():
                body(g)

    def row_peer(d):
        return {"ptcl": lax.rem(j + d, PTCL)}

    def column_peer(d):
        return {"cls": lax.rem(c + d, CLS)}

    def remote(src, dst, send, recv, device):
        return pltpu.make_async_remote_copy(
            src_ref=src, dst_ref=dst, send_sem=send, recv_sem=recv, device_id=device, device_id_type=MESH
        )

    fetches = [
        pltpu.make_async_copy(source, place, fetched.at[i])
        for i, (source, place) in enumerate(
            [(ref_in, ref_ref), (prior_in, prior_ref), (img_in, img_ref), (focus_in, focus_ref), (group_in, group_ref)]
        )
    ]
    for fetch in fetches:
        fetch.start()

    barrier = pltpu.get_barrier_semaphore()
    z, x = c // 2, lax.rem(c, 2)

    @functools.partial(owners)
    def _(g):
        @pl.when(lax.rem(2 * g + home // 2 - z + 20, 16) <= 8)
        def _():
            pl.semaphore_signal(barrier, inc=1, device_id={"cls": 4 * g + home}, device_id_type=MESH)

    farthest(PTCL, lambda d: pl.semaphore_signal(barrier, inc=1, device_id=row_peer(d), device_id_type=MESH))
    for fetch in fetches:
        fetch.wait()

    split = split_matrix()
    chosen = jnp.sum(
        jnp.where(iota((4, 2 * PIX), 0) == lane, ref_ref[...].astype(F32), 0.0), axis=0, keepdims=True
    )
    for m in range(16):
        mrow[m : m + 1, :] = chosen[:, 128 * m : 128 * (m + 1)]
    own_prior = jnp.sum(jnp.where(iota((1, 4), 1) == lane, prior_ref[...].astype(F32), 0.0), axis=1, keepdims=True)
    mrow[16:32, :] = jnp.broadcast_to(own_prior, (16, 128))
    for m in range(9):
        message[m] = mrow[2 * m : 2 * m + 2, :].astype(BF16)
    flat[...] = jnp.zeros_like(flat)
    grid_rows(grid)
    @pl.when(owner)
    def _():
        pl.semaphore_wait(barrier, PTCL - 1 + NEAR)

    @pl.when(jnp.logical_not(owner))
    def _():
        pl.semaphore_wait(barrier, PTCL - 1)

    def near(dz, flip):
        return {"cls": 2 * lax.rem(z + dz + 16, 16) + lax.rem(x + flip, 2)}

    def ref_copy(i):
        target = near((4 - i // 4) * (1 - 2 * ((i // 2) % 2)), lax.rem(i + 1, 2))
        return remote(message, refs.at[mine], ref_send.at[i], ref_recv.at[mine], target)

    behind, ahead = lax.rem(mine + NK - 2, NK), lax.rem(mine + 2, NK)

    def pass_on(i):
        source = jnp.where(i < 8, behind, ahead)
        target = near(jnp.where(i < 8, 4 - i // 2, i // 2 - 7), lax.rem(i, 2))
        return remote(refs.at[source], refs.at[source], ref_send.at[NEAR + i], ref_recv.at[source], target)

    def ref_arrives(g):
        remote(message, refs.at[g], ref_send.at[0], ref_recv.at[g], column_peer(1)).wait_recv()

    def image_copy(d, slot):
        return remote(img_ref, imgs.at[slot], img_send.at[d], img_recv.at[d], row_peer(d))

    @pl.when(owner)
    def _():
        loop(0, NEAR, lambda i: ref_copy(i).start())
        refs[mine] = message[...]

    farthest(PTCL, lambda d: image_copy(d, j).start())
    imgs[j] = img_ref[...]

    make_tables(grid, tables)
    group = column_of(group_ref[...].astype(F32), NB)
    groups_count = focus_ref.shape[1]
    focus = jnp.sum(
        jnp.where(group == iota((NB, groups_count), 1).astype(F32), focus_ref[...], 0.0), axis=1, keepdims=True
    )
    phase = math.pi * focus * grid[2:3, :]
    contrast[...] = -(0.99499 * jnp.sin(phase) + 0.1 * jnp.cos(phase))
    make_picks(grid, picks)

    @pl.when(owner)
    def _():
        ref_arrives(behind)
        loop(0, 8, lambda i: pass_on(i).start())
        ref_arrives(ahead)
        loop(8, 14, lambda i: pass_on(i).start())

    loop(1, PTCL, lambda d: image_copy(d, lax.rem(j + PTCL - d, PTCL)).wait_recv())

    for u in range(8):
        two = jnp.dot(imgs[2 * u : 2 * u + 2].reshape(128, 128), split, preferred_element_type=F32)
        real, imag = pair_halves(two[:NB], two[NB:])
        wide[:, 128 * u : 128 * (u + 1)] = jnp.concatenate([real, imag], axis=0).astype(BF16)

    @functools.partial(loop, 0, 4)
    def _(s):
        value = jnp.dot(
            wide[...], picks[pl.ds(pl.multiple_of(s * PIX, PIX), PIX), :], preferred_element_type=F32
        )
        here = contrast[...]
        row = pl.multiple_of(s * NB, NB)
        vals[0, pl.ds(row, NB), :] = (value[:NB] * here).astype(BF16)
        vals[1, pl.ds(row, NB), :] = (value[NB:] * here).astype(BF16)
        square = jnp.where(grid[pl.ds(4 + s, 1), :] >= 0.0, here * here, 0.0)
        high = square.astype(BF16)
        vals[2, pl.ds(row, NB), :] = high
        square_lo[pl.ds(row, NB), :] = (square - high.astype(F32)).astype(BF16)

    for i, block in enumerate([vals[0], vals[1], vals[2], square_lo[...], vals[2]]):
        stack[LANES * i : LANES * (i + 1), :] = block.T

    @functools.partial(owners)
    def _(g):
        @pl.when(jnp.logical_not(owner) | ((g != behind) & (g != ahead)))
        def _():
            ref_arrives(g)


    for k in range(NK):
        for m in range(9):
            flat[32 * k + 2 * m : 32 * k + 2 * m + 2, :] = refs[k, m].astype(F32)
    flat[...] = jnp.dot(flat[...].astype(BF16), split, preferred_element_type=F32)
    for u in range(8):
        real, imag = pair_halves(
            flat[pl.ds(2 * u, NK, stride=32), :], flat[pl.ds(2 * u + 1, NK, stride=32), :]
        )
        refmat[:, 128 * u : 128 * (u + 1)] = jnp.concatenate([real, imag], axis=0).astype(BF16)
    prior = flat[pl.ds(16, NK, stride=32), :]

    for r, patch, group, count, offset in BANDS:
        both = jnp.dot(
            refmat[:, 128 * group : 128 * (group + count)],
            tables[128 * offset : 128 * (offset + count), :],
            preferred_element_type=F32,
        )
        both = both.astype(BF16).astype(F32)
        turned[0, NK * r : NK * (r + 1), 128 * patch : 128 * (patch + 1)] = both[:NK]
        turned[1, NK * r : NK * (r + 1), 128 * patch : 128 * (patch + 1)] = both[NK:]

    real, imag = turned[0], turned[1]
    power = -0.5 * (real * real + imag * imag)
    power_hi = power.astype(BF16)
    power_lo = (power - power_hi.astype(F32)).astype(BF16)
    left = jnp.concatenate([real.astype(BF16), imag.astype(BF16), power_hi, power_hi, power_lo], axis=1)
    scores = jnp.dot(left, stack[...], preferred_element_type=F32)
    prior = jnp.concatenate([prior, prior], axis=1)
    logits = scores + jnp.concatenate([prior] * BASE, axis=0)
    peak = jnp.max(logits, axis=0, keepdims=True)
    peak = jnp.maximum(peak[:, :128], peak[:, 128:])
    peak = jnp.maximum(peak, pltpu.roll(peak, 64, 1))
    total = jnp.sum(jnp.exp(logits - jnp.concatenate([peak, peak], axis=1)), axis=0, keepdims=True)
    total = total[:, :128] + total[:, 128:]
    total = total + pltpu.roll(total, 64, 1)
    stat[...] = jnp.where(iota((2, 128), 0) == 0, peak, total)

    def stat_copy(d, slot):
        return remote(stat, stats.at[slot], stat_send.at[d], stat_recv.at[d], row_peer(d))

    farthest(PTCL, lambda d: stat_copy(d, j).start())
    stats[j] = stat[...]
    turn_tables(tables, tables_t)
    loop(1, PTCL, lambda d: image_copy(d, j).wait_send())

    @pl.when(owner)
    def _():
        loop(0, NEAR, lambda i: ref_copy(i).wait_send())
        loop(0, 14, lambda i: pass_on(i).wait_send())

    loop(1, PTCL, lambda d: stat_copy(d, lax.rem(j + PTCL - d, PTCL)).wait_recv())
    peaks = stats[:, 0:1, :]
    peak = jnp.max(peaks, axis=0)
    total = jnp.sum(stats[:, 1:2, :] * jnp.exp(peaks - peak[None]), axis=0)
    weights = (
        jnp.exp(logits - jnp.concatenate([peak, peak], axis=1)) / jnp.concatenate([total, total], axis=1)
    ).astype(BF16)
    counts = jnp.sum(weights.astype(F32), axis=1, keepdims=True)
    share = counts[0:NK]
    for r in range(1, BASE):
        share = share + counts[r * NK : (r + 1) * NK]

    for part in range(3):
        spread[part] = jnp.dot(weights, vals[part], preferred_element_type=F32)
    split_sums = []
    for r in range(BASE):
        value = jnp.concatenate([spread[part, NK * r : NK * (r + 1), :] for part in range(3)], axis=0)
        high = value.astype(BF16).astype(F32)
        split_sums.append(jnp.concatenate([high, value - high], axis=0).astype(BF16))
    for group in range(8):
        points = jnp.concatenate(
            [split_sums[r][:, 128 * patch : 128 * (patch + 1)] for r, patch in TOUCH[group]], axis=1
        )
        back = jnp.dot(
            points, tables_t[128 * STARTS[group] : 128 * STARTS[group + 1], :], preferred_element_type=F32
        )
        back = back[0:24] + back[24:48]
        for part in range(3):
            rows[pl.ds(8 * part + group, NK, stride=32), :] = back[NK * part : NK * (part + 1), :]
    for i in range(24, 32):
        rows[pl.ds(i, NK, stride=32), :] = jnp.broadcast_to(share, (NK, 128))
    for k in range(NK):
        parts[k] = rows[32 * k : 32 * (k + 1), :].astype(BF16)

    def sum_copy(g):
        return remote(parts.at[g], heap.at[c], sum_send.at[g], sum_recv.at[c], {"cls": 4 * g + home})

    def out_copy(d):
        target = lax.rem(j + d, PTCL)
        return remote(outbox.at[target], inbox.at[lane], out_send.at[d], out_recv.at[lane], row_peer(d))

    owners(lambda g: sum_copy(g).start())
    loop(1, PTCL, lambda d: stat_copy(d, j).wait_send())

    @pl.when(owner)
    def _():
        def arrive(i, total):
            source = lax.rem(c + CLS + ((i + 2) // 2) * (1 - 2 * lax.rem(i, 2)), CLS)
            remote(parts.at[0], heap.at[source], sum_send.at[0], sum_recv.at[source], {"cls": source}).wait_recv()
            return total + heap[source].astype(F32)

        sums = lax.fori_loop(0, CLS - 1, arrive, parts[mine].astype(F32))
        below = sums[16:24] + 1.0
        planes = jnp.concatenate([sums[0:8] / below, sums[8:16] / below], axis=1)
        high = planes.astype(BF16).astype(F32)
        both = jnp.concatenate([high, planes - high], axis=0).astype(BF16)
        joined = jnp.dot(both, join_matrix(), preferred_element_type=F32)
        joined = joined[0:8] + joined[8:16]
        for b in range(PTCL):
            u, h = b // 2, b % 2
            outbox[b] = jnp.where(
                iota((2, 128), 0) == 0, joined[u : u + 1, 128 * h : 128 * (h + 1)], sums[24:25, :]
            )
        farthest(PTCL, lambda d: out_copy(d).start())
        inbox[lane] = outbox[j]

    owners(lambda g: sum_copy(g).wait_send())

    @functools.partial(loop, 0, 4)
    def _(i):
        @pl.when(first + i != j)
        def _():
            remote(outbox.at[0], inbox.at[i], out_send.at[0], out_recv.at[i], row_peer(1)).wait_recv()

    new_ref[...] = jnp.concatenate([inbox[i, 0:1, :] for i in range(4)], axis=0)
    share_row = inbox[0, 1:2, :]
    for i in range(1, 4):
        share_row = jnp.where(iota((1, 128), 1) == i, inbox[i, 1:2, :], share_row)
    share_ref[...] = share_row * (128.0 / 2048.0)


    @pl.when(owner)
    def _():
        loop(1, PTCL, lambda d: out_copy(d).wait_send())


def on_device(images, references, log_prior, defocus, groups):
    vmem = pl.BlockSpec(memory_space=VMEM)
    dma = pltpu.SemaphoreType.DMA
    new, share = pl.pallas_call(
        em_kernel,
        out_shape=(VMEM((4, 128), F32), VMEM((1, 128), F32)),
        in_specs=[pl.BlockSpec(memory_space=pl.ANY)] * 5,
        out_specs=(vmem, vmem),
        scratch_shapes=[
            VMEM((8, LANES), F32),
            VMEM((BLOCKS * 128, 128), BF16),
            VMEM((BLOCKS * 128, 128), BF16),
            VMEM((4 * PIX, LANES), BF16),
            VMEM((NB, LANES), F32),
            VMEM((32, 128), F32),
            VMEM((9, 2, 128), BF16),
            VMEM((PTCL, NB, 128), BF16),
            VMEM((NK, 9, 2, 128), BF16),
            VMEM((NK * 32, 128), F32),
            VMEM((2 * NB, PIX), BF16),
            VMEM((2 * NK, PIX), BF16),
            VMEM((2, ROWS, LANES), F32),
            VMEM((3, 4 * NB, LANES), BF16),
            VMEM((4 * NB, LANES), BF16),
            VMEM((5 * LANES, 4 * NB), BF16),
            VMEM((2, 128), F32),
            VMEM((PTCL, 2, 128), F32),
            VMEM((3, ROWS, LANES), F32),
            VMEM((NK * 32, 128), F32),
            VMEM((NK, 32, 128), BF16),
            VMEM((CLS, 32, 128), BF16),
            VMEM((PTCL, 2, 128), F32),
            VMEM((4, 2, 128), F32),
            VMEM((NB, 128), BF16),
            VMEM((4, 2 * PIX), BF16),
            VMEM((1, 4), BF16),
            VMEM((1, defocus.shape[0]), F32),
            VMEM((1, NB), jnp.int32),
            dma((5,)),
            dma((PTCL,)),
            dma((PTCL,)),
            dma((CLS,)),
            dma((NK,)),
            dma((PTCL,)),
            dma((PTCL,)),
            dma((NK,)),
            dma((CLS,)),
            dma((PTCL,)),
            dma((4,)),
        ],
        compiler_params=pltpu.CompilerParams(
            collective_id=0, has_side_effects=True, vmem_limit_bytes=60 << 20
        ),
        name="em",
    )(images, references, log_prior[None, :], defocus[None, :], groups[None, :])
    return new, share[0, :4]


def solution(mesh):
    return jax.shard_map(
        on_device,
        mesh=mesh,
        in_specs=(P("cls", "ptcl"), P("cls", None), P("cls"), P(), P("cls")),
        out_specs=(P("cls", "ptcl"), P("cls")),
        check_vma=False,
    )
```

```python
import functools
import math

import jax
import jax.numpy as jnp
import numpy as np
from jax import lax
from jax.experimental import pallas as pl
from jax.experimental.pallas import tpu as pltpu
from jax.sharding import PartitionSpec as P

SIDE = 32
PIX = SIDE * SIDE
ROT = 36
BASE = ROT // 4
EXT = SIDE + 1
PATCH = 11
PATCHES = 9
LANES = 128 * PATCHES
CLS = 32
PTCL = 16
NK = 8
NEAR = 17
ROWS = BASE * NK
NB = 64
MESH = pl.DeviceIdType.MESH
F32 = jnp.float32
BF16 = jnp.bfloat16
VMEM = pltpu.VMEM

ANGLES = (np.float32(2.0 * math.pi) * np.arange(BASE, dtype=np.float32) / np.float32(ROT)).astype(np.float32)
COSINES = [float(x) for x in np.cos(ANGLES).astype(np.float32)]
SINES = [float(x) for x in np.sin(ANGLES).astype(np.float32)]


def bands():
    out, offset = [], 0
    for r in range(BASE):
        for patch in range(PATCHES):
            down = np.arange(PATCH)[:, None] + PATCH * (patch // 3) - SIDE // 2
            across = np.arange(PATCH)[None, :] + PATCH * (patch % 3) - SIDE // 2
            source = COSINES[r] * down - SINES[r] * across
            low = max(int(np.floor(source.min() - 1e-3)) + SIDE // 2, 0)
            high = min(int(np.floor(source.max() + 1e-3)) + 1 + SIDE // 2, SIDE - 1)
            count = high // 4 - low // 4 + 1
            out.append((r, patch, low // 4, count, offset))
            offset += count
    return out, offset


BANDS, BLOCKS = bands()
TOUCH = [[(r, patch) for r, patch, g, n, _ in BANDS if g <= group < g + n] for group in range(8)]
STARTS = [sum(len(t) for t in TOUCH[:group]) for group in range(9)]


def iota(shape, axis):
    return lax.broadcasted_iota(jnp.int32, shape, axis)


def grid_rows(grid):
    column = iota((1, LANES), 1)
    patch = (column // 128).astype(F32)
    inner = (column % 128).astype(F32)
    patch_down = jnp.floor((patch + 0.5) * (1.0 / 3.0))
    inner_down = jnp.floor((inner + 0.5) * (1.0 / PATCH))
    down = PATCH * patch_down + inner_down - SIDE // 2
    across = PATCH * (patch - 3.0 * patch_down) + inner - PATCH * inner_down - SIDE // 2
    grid[0:1, :] = across
    grid[1:2, :] = down
    grid[2:3, :] = (across * across + down * down) * (1.0 / (SIDE // 2) ** 2)
    a, d = across, down
    for s in range(4):
        inside = (a >= -16.0) & (a <= 15.0) & (d >= -16.0) & (d <= 15.0) & (inner < PATCH * PATCH - 0.5)
        grid[4 + s : 5 + s, :] = jnp.where(inside, (d + 16.0) * SIDE + a + 16.0, -1.0)
        a, d = -d, a


def split_matrix():
    source, place = iota((128, 128), 0), iota((128, 128), 1)
    return jnp.where(source == 2 * (place % 64) + place // 64, 1.0, 0.0).astype(BF16)


def join_matrix():
    source, place = iota((256, 256), 0), iota((256, 256), 1)
    inner = place % 128
    return jnp.where(source == 128 * (inner % 2) + 64 * (place // 128) + inner // 2, 1.0, 0.0).astype(BF16)


def pair_halves(first, second):
    low = iota(first.shape, 1) < 64
    real = jnp.where(low, first, pltpu.roll(second, 64, 1))
    imag = jnp.where(low, pltpu.roll(first, 64, 1), second)
    return real, imag


def column_of(row, size):
    return jnp.sum(jnp.where(iota((size, size), 0) == iota((size, size), 1), row, 0.0), axis=1, keepdims=True)


def make_tables(grid, tables):
    place = iota((SIDE, 128), 0).astype(F32) - float(SIDE // 2)
    for r, patch, group, count, offset in BANDS:
        qa = grid[0:1, 128 * patch : 128 * (patch + 1)]
        qd = grid[1:2, 128 * patch : 128 * (patch + 1)]
        hat_a = jnp.maximum(0.0, 1.0 - jnp.abs(COSINES[r] * qa + SINES[r] * qd - place))
        line = iota((8 * ((count + 1) // 2), 128), 0).astype(F32) + float(4 * group - SIDE // 2)
        hat_d = jnp.maximum(0.0, 1.0 - jnp.abs(COSINES[r] * qd - SINES[r] * qa - line))
        for p in range(4 * count):
            row = 128 * offset + SIDE * p
            tables[row : row + SIDE, :] = (hat_a * hat_d[p : p + 1, :]).astype(BF16)


def turn_tables(tables, tables_t):
    for r, patch, group, count, offset in BANDS:
        for i in range(count):
            place = STARTS[group + i] + TOUCH[group + i].index((r, patch))
            tables_t[128 * place : 128 * (place + 1), :] = tables[128 * (offset + i) : 128 * (offset + i + 1), :].T


def make_picks(grid, picks):
    def step(i, _):
        target = grid[pl.ds(4 + i // 4, 1), :]
        place = (iota((256, LANES), 0) + 256 * (i % 4)).astype(F32)
        picks[pl.ds(pl.multiple_of(i * 256, 256), 256), :] = jnp.where(place == target, 1.0, 0.0).astype(BF16)
        return 0

    lax.fori_loop(0, 16, step, 0)


def em_kernel(
    img_in, ref_in, prior_in, focus_in, group_in,
    new_ref, share_ref,
    grid, tables, tables_t, picks, contrast, mrow, message, imgs, refs, flat, wide, refmat, turned, vals, square_lo, stack,
    stat, stats, spread, rows, parts, heap, outbox, inbox,
    img_ref, ref_ref, prior_ref, focus_ref, group_ref, fetched,
    img_send, img_recv, ref_send, ref_recv, stat_send, stat_recv, sum_send, sum_recv, out_send, out_recv,
):
    c = lax.axis_index("cls")
    j = lax.axis_index("ptcl")
    home = j // 4
    mine = c // 4
    lane = lax.rem(j, 4)
    owner = lax.rem(c, 4) == home
    first = 4 * lax.rem(c, 4)

    def loop(low, high, body):
        def step(i, _):
            body(i)
            return 0

        lax.fori_loop(low, high, step, 0)

    def farthest(count, body):
        loop(0, count - 1, lambda i: body(count // 2 + ((i + 1) // 2) * (2 * (i % 2) - 1)))

    def owners(body):
        @functools.partial(loop, 0, NK)
        def _(i):
            g = lax.rem(mine + NK // 2 + ((i + 1) // 2) * (2 * (i % 2) - 1) + NK, NK)

            @pl.when(4 * g + home != c)
            def _():
                body(g)

    def row_peer(d):
        return {"ptcl": lax.rem(j + d, PTCL)}

    def column_peer(d):
        return {"cls": lax.rem(c + d, CLS)}

    def remote(src, dst, send, recv, device):
        return pltpu.make_async_remote_copy(
            src_ref=src, dst_ref=dst, send_sem=send, recv_sem=recv, device_id=device, device_id_type=MESH
        )

    fetches = [
        pltpu.make_async_copy(source, place, fetched.at[i])
        for i, (source, place) in enumerate(
            [(ref_in, ref_ref), (prior_in, prior_ref), (img_in, img_ref), (focus_in, focus_ref), (group_in, group_ref)]
        )
    ]
    for fetch in fetches:
        fetch.start()

    barrier = pltpu.get_barrier_semaphore()
    z, x = c // 2, lax.rem(c, 2)

    @functools.partial(owners)
    def _(g):
        @pl.when(lax.rem(2 * g + home // 2 - z + 20, 16) <= 8)
        def _():
            pl.semaphore_signal(barrier, inc=1, device_id={"cls": 4 * g + home}, device_id_type=MESH)

    farthest(PTCL, lambda d: pl.semaphore_signal(barrier, inc=1, device_id=row_peer(d), device_id_type=MESH))
    for fetch in fetches:
        fetch.wait()

    split = split_matrix()
    chosen = jnp.sum(
        jnp.where(iota((4, 2 * PIX), 0) == lane, ref_ref[...].astype(F32), 0.0), axis=0, keepdims=True
    )
    for m in range(16):
        mrow[m : m + 1, :] = chosen[:, 128 * m : 128 * (m + 1)]
    own_prior = jnp.sum(jnp.where(iota((1, 4), 1) == lane, prior_ref[...].astype(F32), 0.0), axis=1, keepdims=True)
    mrow[16:32, :] = jnp.broadcast_to(own_prior, (16, 128))
    message[...] = mrow[...].astype(BF16)
    grid_rows(grid)
    @pl.when(owner)
    def _():
        pl.semaphore_wait(barrier, PTCL - 1 + NEAR)

    @pl.when(jnp.logical_not(owner))
    def _():
        pl.semaphore_wait(barrier, PTCL - 1)

    def near(dz, flip):
        return {"cls": 2 * lax.rem(z + dz + 16, 16) + lax.rem(x + flip, 2)}

    def ref_copy(i):
        target = near((4 - i // 4) * (1 - 2 * ((i // 2) % 2)), lax.rem(i + 1, 2))
        return remote(message, refs.at[mine], ref_send.at[i], ref_recv.at[mine], target)

    behind, ahead = lax.rem(mine + NK - 2, NK), lax.rem(mine + 2, NK)

    def pass_on(i):
        source = jnp.where(i < 8, behind, ahead)
        target = near(jnp.where(i < 8, 4 - i // 2, i // 2 - 7), lax.rem(i, 2))
        return remote(refs.at[source], refs.at[source], ref_send.at[NEAR + i], ref_recv.at[source], target)

    def ref_arrives(g):
        remote(message, refs.at[g], ref_send.at[0], ref_recv.at[g], column_peer(1)).wait_recv()

    def image_copy(d, slot):
        return remote(img_ref, imgs.at[slot], img_send.at[d], img_recv.at[d], row_peer(d))

    @pl.when(owner)
    def _():
        loop(0, NEAR, lambda i: ref_copy(i).start())
        refs[mine] = message[...]

    farthest(PTCL, lambda d: image_copy(d, j).start())
    imgs[j] = img_ref[...]

    make_tables(grid, tables)
    group = column_of(group_ref[...].astype(F32), NB)
    groups_count = focus_ref.shape[1]
    focus = jnp.sum(
        jnp.where(group == iota((NB, groups_count), 1).astype(F32), focus_ref[...], 0.0), axis=1, keepdims=True
    )
    phase = math.pi * focus * grid[2:3, :]
    contrast[...] = -(0.99499 * jnp.sin(phase) + 0.1 * jnp.cos(phase))
    make_picks(grid, picks)

    @pl.when(owner)
    def _():
        def pass_behind():
            ref_arrives(behind)
            loop(0, 8, lambda i: pass_on(i).start())

        def pass_ahead():
            ref_arrives(ahead)
            loop(8, 14, lambda i: pass_on(i).start())

        other_first = lax.rem(z + 4, 16) < 8

        @pl.when(other_first)
        def _():
            pass_ahead()

        pass_behind()

        @pl.when(jnp.logical_not(other_first))
        def _():
            pass_ahead()

    loop(1, PTCL, lambda d: image_copy(d, lax.rem(j + PTCL - d, PTCL)).wait_recv())

    for u in range(8):
        two = jnp.dot(imgs[2 * u : 2 * u + 2].reshape(128, 128), split, preferred_element_type=F32)
        real, imag = pair_halves(two[:NB], two[NB:])
        wide[:, 128 * u : 128 * (u + 1)] = jnp.concatenate([real, imag], axis=0).astype(BF16)

    @functools.partial(loop, 0, 4)
    def _(s):
        value = jnp.dot(
            wide[...], picks[pl.ds(pl.multiple_of(s * PIX, PIX), PIX), :], preferred_element_type=F32
        )
        here = contrast[...]
        row = pl.multiple_of(s * NB, NB)
        vals[0, pl.ds(row, NB), :] = (value[:NB] * here).astype(BF16)
        vals[1, pl.ds(row, NB), :] = (value[NB:] * here).astype(BF16)
        square = jnp.where(grid[pl.ds(4 + s, 1), :] >= 0.0, here * here, 0.0)
        high = square.astype(BF16)
        vals[2, pl.ds(row, NB), :] = high
        square_lo[pl.ds(row, NB), :] = (square - high.astype(F32)).astype(BF16)

    for i, block in enumerate([vals[0], vals[1], vals[2], square_lo[...], vals[2]]):
        stack[LANES * i : LANES * (i + 1), :] = block.T

    @functools.partial(owners)
    def _(g):
        @pl.when(jnp.logical_not(owner) | ((g != behind) & (g != ahead)))
        def _():
            ref_arrives(g)


    flat[...] = jnp.dot(refs[...].reshape(NK * 32, 128), split, preferred_element_type=F32)
    for u in range(8):
        real, imag = pair_halves(
            flat[pl.ds(2 * u, NK, stride=32), :], flat[pl.ds(2 * u + 1, NK, stride=32), :]
        )
        refmat[:, 128 * u : 128 * (u + 1)] = jnp.concatenate([real, imag], axis=0).astype(BF16)
    prior = flat[pl.ds(16, NK, stride=32), :]

    for r, patch, group, count, offset in BANDS:
        both = jnp.dot(
            refmat[:, 128 * group : 128 * (group + count)],
            tables[128 * offset : 128 * (offset + count), :],
            preferred_element_type=F32,
        )
        both = both.astype(BF16).astype(F32)
        turned[0, NK * r : NK * (r + 1), 128 * patch : 128 * (patch + 1)] = both[:NK]
        turned[1, NK * r : NK * (r + 1), 128 * patch : 128 * (patch + 1)] = both[NK:]

    real, imag = turned[0], turned[1]
    power = -0.5 * (real * real + imag * imag)
    power_hi = power.astype(BF16)
    power_lo = (power - power_hi.astype(F32)).astype(BF16)
    left = jnp.concatenate([real.astype(BF16), imag.astype(BF16), power_hi, power_hi, power_lo], axis=1)
    scores = jnp.dot(left, stack[...], preferred_element_type=F32)
    prior = jnp.concatenate([prior, prior], axis=1)
    logits = scores + jnp.concatenate([prior] * BASE, axis=0)
    peak = jnp.max(logits, axis=0, keepdims=True)
    peak = jnp.maximum(peak[:, :128], peak[:, 128:])
    peak = jnp.maximum(peak, pltpu.roll(peak, 64, 1))
    total = jnp.sum(jnp.exp(logits - jnp.concatenate([peak, peak], axis=1)), axis=0, keepdims=True)
    total = total[:, :128] + total[:, 128:]
    total = total + pltpu.roll(total, 64, 1)
    stat[...] = jnp.where(iota((2, 128), 0) == 0, peak, total)

    def stat_copy(d, slot):
        return remote(stat, stats.at[slot], stat_send.at[d], stat_recv.at[d], row_peer(d))

    farthest(PTCL, lambda d: stat_copy(d, j).start())
    stats[j] = stat[...]
    turn_tables(tables, tables_t)
    loop(1, PTCL, lambda d: image_copy(d, j).wait_send())

    @pl.when(owner)
    def _():
        loop(0, NEAR, lambda i: ref_copy(i).wait_send())
        loop(0, 14, lambda i: pass_on(i).wait_send())

    loop(1, PTCL, lambda d: stat_copy(d, lax.rem(j + PTCL - d, PTCL)).wait_recv())
    peaks = stats[:, 0:1, :]
    peak = jnp.max(peaks, axis=0)
    total = jnp.sum(stats[:, 1:2, :] * jnp.exp(peaks - peak[None]), axis=0)
    weights = (
        jnp.exp(logits - jnp.concatenate([peak, peak], axis=1)) / jnp.concatenate([total, total], axis=1)
    ).astype(BF16)
    counts = jnp.sum(weights.astype(F32), axis=1, keepdims=True)
    share = counts[0:NK]
    for r in range(1, BASE):
        share = share + counts[r * NK : (r + 1) * NK]

    for part in range(3):
        spread[part] = jnp.dot(weights, vals[part], preferred_element_type=F32)
    split_sums = []
    for r in range(BASE):
        value = jnp.concatenate([spread[part, NK * r : NK * (r + 1), :] for part in range(3)], axis=0)
        high = value.astype(BF16).astype(F32)
        split_sums.append(jnp.concatenate([high, value - high], axis=0).astype(BF16))
    for group in range(8):
        points = jnp.concatenate(
            [split_sums[r][:, 128 * patch : 128 * (patch + 1)] for r, patch in TOUCH[group]], axis=1
        )
        back = jnp.dot(
            points, tables_t[128 * STARTS[group] : 128 * STARTS[group + 1], :], preferred_element_type=F32
        )
        back = back[0:24] + back[24:48]
        for part in range(3):
            rows[pl.ds(8 * part + group, NK, stride=32), :] = back[NK * part : NK * (part + 1), :]
    for i in range(24, 32):
        rows[pl.ds(i, NK, stride=32), :] = jnp.broadcast_to(share, (NK, 128))
    for k in range(NK):
        parts[k] = rows[32 * k : 32 * (k + 1), :].astype(BF16)

    def sum_copy(g):
        return remote(parts.at[g], heap.at[c], sum_send.at[g], sum_recv.at[c], {"cls": 4 * g + home})

    def out_copy(d):
        target = lax.rem(j + d, PTCL)
        return remote(outbox.at[target], inbox.at[lane], out_send.at[d], out_recv.at[lane], row_peer(d))

    owners(lambda g: sum_copy(g).start())
    loop(1, PTCL, lambda d: stat_copy(d, j).wait_send())

    @pl.when(owner)
    def _():
        def arrive(i, total):
            source = lax.rem(c + CLS + ((i + 2) // 2) * (1 - 2 * lax.rem(i, 2)), CLS)
            remote(parts.at[0], heap.at[source], sum_send.at[0], sum_recv.at[source], {"cls": source}).wait_recv()
            return total + heap[source].astype(F32)

        sums = lax.fori_loop(0, CLS - 1, arrive, parts[mine].astype(F32))
        below = sums[16:24] + 1.0
        planes = jnp.concatenate([sums[0:8] / below, sums[8:16] / below], axis=1)
        high = planes.astype(BF16).astype(F32)
        both = jnp.concatenate([high, planes - high], axis=0).astype(BF16)
        joined = jnp.dot(both, join_matrix(), preferred_element_type=F32)
        joined = joined[0:8] + joined[8:16]
        for b in range(PTCL):
            u, h = b // 2, b % 2
            outbox[b] = jnp.where(
                iota((2, 128), 0) == 0, joined[u : u + 1, 128 * h : 128 * (h + 1)], sums[24:25, :]
            )
        farthest(PTCL, lambda d: out_copy(d).start())
        inbox[lane] = outbox[j]

    owners(lambda g: sum_copy(g).wait_send())

    @functools.partial(loop, 0, 4)
    def _(i):
        @pl.when(first + i != j)
        def _():
            remote(outbox.at[0], inbox.at[i], out_send.at[0], out_recv.at[i], row_peer(1)).wait_recv()

    new_ref[...] = jnp.concatenate([inbox[i, 0:1, :] for i in range(4)], axis=0)
    share_row = inbox[0, 1:2, :]
    for i in range(1, 4):
        share_row = jnp.where(iota((1, 128), 1) == i, inbox[i, 1:2, :], share_row)
    share_ref[...] = share_row * (128.0 / 2048.0)


    @pl.when(owner)
    def _():
        loop(1, PTCL, lambda d: out_copy(d).wait_send())


def on_device(images, references, log_prior, defocus, groups):
    vmem = pl.BlockSpec(memory_space=VMEM)
    dma = pltpu.SemaphoreType.DMA
    new, share = pl.pallas_call(
        em_kernel,
        out_shape=(VMEM((4, 128), F32), VMEM((1, 128), F32)),
        in_specs=[pl.BlockSpec(memory_space=pl.ANY)] * 5,
        out_specs=(vmem, vmem),
        scratch_shapes=[
            VMEM((8, LANES), F32),
            VMEM((BLOCKS * 128, 128), BF16),
            VMEM((BLOCKS * 128, 128), BF16),
            VMEM((4 * PIX, LANES), BF16),
            VMEM((NB, LANES), F32),
            VMEM((32, 128), F32),
            VMEM((32, 128), BF16),
            VMEM((PTCL, NB, 128), BF16),
            VMEM((NK, 32, 128), BF16),
            VMEM((NK * 32, 128), F32),
            VMEM((2 * NB, PIX), BF16),
            VMEM((2 * NK, PIX), BF16),
            VMEM((2, ROWS, LANES), F32),
            VMEM((3, 4 * NB, LANES), BF16),
            VMEM((4 * NB, LANES), BF16),
            VMEM((5 * LANES, 4 * NB), BF16),
            VMEM((2, 128), F32),
            VMEM((PTCL, 2, 128), F32),
            VMEM((3, ROWS, LANES), F32),
            VMEM((NK * 32, 128), F32),
            VMEM((NK, 32, 128), BF16),
            VMEM((CLS, 32, 128), BF16),
            VMEM((PTCL, 2, 128), F32),
            VMEM((4, 2, 128), F32),
            VMEM((NB, 128), BF16),
            VMEM((4, 2 * PIX), BF16),
            VMEM((1, 4), BF16),
            VMEM((1, defocus.shape[0]), F32),
            VMEM((1, NB), jnp.int32),
            dma((5,)),
            dma((PTCL,)),
            dma((PTCL,)),
            dma((CLS,)),
            dma((NK,)),
            dma((PTCL,)),
            dma((PTCL,)),
            dma((NK,)),
            dma((CLS,)),
            dma((PTCL,)),
            dma((4,)),
        ],
        compiler_params=pltpu.CompilerParams(
            collective_id=0, has_side_effects=True, vmem_limit_bytes=60 << 20
        ),
        name="em",
    )(images, references, log_prior[None, :], defocus[None, :], groups[None, :])
    return new, share[0, :4]


def solution(mesh):
    return jax.shard_map(
        on_device,
        mesh=mesh,
        in_specs=(P("cls", "ptcl"), P("cls", None), P("cls"), P(), P("cls")),
        out_specs=(P("cls", "ptcl"), P("cls")),
        check_vma=False,
    )
```
